512 devices in a mesh: row: 32 (over x, y), col: 16 (over z, core).
Axes of the slice: x: 4, y: 8, z: 8, core: 2. Of those that a mesh axis runs over, the one named last changes fastest.
Arguments:
- right_sides: float32 [15, 512, 4096], P(None, 'row', 'col'), may hold values from -6 to 6
- diag_inverse: bfloat16 [15, 4096, 4096], P(None, 'row', 'col'), may hold values from -2 to 2, as said below
- panels: bfloat16 [14, 3, 4096, 4096], P(None, None, 'col', 'row'), may hold values from -0.046875 to 0.046875
- block_map: int32 [14, 16, 3], replicated, may hold values from 8 to 15, as said below
Outputs:
- solution: float32 [15, 512, 4096], P(None, 'col', 'row')
The draws below stay inside these ranges and needn't reach their ends.
Inputs may be any that keep to these rules, and one draw needn't show every extreme that they name: `block_map`: entry [s, q, c] is an ancestor of supernode s, or 15, which marks an empty slot; the ancestors named in one [s, q] are distinct. Each diag_inverse[n] is lower triangular: entries whose column index exceeds the row index are zero.
All inputs are finite; a program needn't handle non-finite values.
Results may differ from the reference program's by a relative error of at most 0.028.
Values may be sent and summed in bfloat16 or wider, within the bound.
No kernel may reach another device: no remote copies, remote signals or barrier semaphores. Data moves between devices by JAX's collectives and lax.ppermute only.
A program may use at most 64 MiB of HBM per device.

```python
import math
import jax
import jax.numpy as jnp
import numpy as np
from jax import lax

W = 4096
R = 512
LEV = 4
S = 15
SP = 14
CAP = 3
NBLK = 16
BLK = 256
SPAN = 128
N_ROW = 32
N_COL = 16


def draw_diag_inverse(key, part):
    first_key = jax.random.fold_in(key, 11)
    second_key = jax.random.fold_in(key, 12)
    spread = jnp.clip(jax.random.normal(first_key, (S, W, W), jnp.float32), -5.0, 5.0)
    pivots = jax.random.uniform(second_key, (S, W), jnp.float32, 0.6, 1.4)
    rows_iota = lax.broadcasted_iota(jnp.int32, (S, W, W), 1)
    cols_iota = lax.broadcasted_iota(jnp.int32, (S, W, W), 2)
    below_part = jnp.where(cols_iota < rows_iota, spread * (0.6 / math.sqrt(W)), 0.0)
    diagonal = jnp.where(cols_iota == rows_iota, pivots[:, :, None], 0.0)
    return (below_part + diagonal).astype(jnp.bfloat16)


def ancestor_table():
    ancestors = np.full((S - 1, LEV - 1), S, np.int32)
    for supernode in range(S - 1):
        level_index = LEV - 1
        while supernode >= 2 ** LEV - 2 ** level_index:
            level_index -= 1
        local_index = supernode - (2 ** LEV - 2 ** (level_index + 1))
        for distance in range(1, level_index + 1):
            ancestors[supernode, distance - 1] = 2 ** LEV - 2 ** (level_index - distance + 1) + (local_index >> distance)
    return ancestors


def draw_block_map(key, part):
    ancestors = jnp.asarray(ancestor_table())
    level_key = jax.random.fold_in(key, 21)
    live_key = jax.random.fold_in(key, 22)
    turn_key = jax.random.fold_in(key, 23)
    thresholds = jax.random.randint(level_key, (1, NBLK, 1), 1, 5)
    rolls = jax.random.randint(live_key, (S - 1, NBLK, LEV - 1), 0, 4)
    entries = jnp.where(rolls < thresholds, ancestors[:, None, :], S)
    turns = jax.random.randint(turn_key, (S - 1, NBLK, 1), 0, LEV - 1)
    order = (lax.broadcasted_iota(jnp.int32, (S - 1, NBLK, LEV - 1), 2) + turns) % (LEV - 1)
    return jnp.take_along_axis(entries, order, axis=2).astype(jnp.int32)


def block_scale(stream_key, shape, cuts, least, high):
    loudness = 1.0
    for dim, blocks in cuts:
        draws = jax.random.uniform(jax.random.fold_in(jax.random.fold_in(stream_key, 6), dim), (blocks,), jnp.float32, least / len(cuts), high / len(cuts))
        loudness = loudness * jnp.repeat(jnp.exp(draws), shape[dim] // blocks).reshape((-1,) + (1,) * (len(shape) - 1 - dim))
    return loudness


def normal_values(rng, extent, scale, reach, cuts=(), kind=jnp.bfloat16):
    gain = block_scale(rng, extent, cuts, -0.22, 0.18) if cuts else 1.0
    values = jax.random.normal(rng, extent, jnp.float32) * scale * gain
    return jnp.minimum(jnp.maximum(values, -reach), reach).astype(kind)


def setup_inputs(seed: int = 0) -> dict:
    seeds = jax.random.split(jax.random.key(seed), 5)
    return {
        "right_sides": normal_values(seeds[0], (S, R, W), 1.0, 6.0, ((1, 32), (2, 16)), jnp.float32),
        "diag_inverse": draw_diag_inverse(jax.random.fold_in(seeds[4], 71), 0),
        "panels": normal_values(seeds[2], (SP, CAP, W, W), (4 * W) ** -0.5, 0.046875, ((2, 16), (3, 32))),
        "block_map": draw_block_map(jax.random.fold_in(seeds[4], 71), 0),
    }


def node_tier(supernode):
    level_index = LEV - 1
    while supernode >= 2 ** LEV - 2 ** level_index:
        level_index -= 1
    return level_index


def ancestor_of(supernode, distance):
    level_index = node_tier(supernode)
    local_index = supernode - (2 ** LEV - 2 ** (level_index + 1))
    return 2 ** LEV - 2 ** (level_index - distance + 1) + (local_index >> distance)


def descendants_of(target):
    found = []
    for source in range(S - 1):
        for distance in range(1, node_tier(source) + 1):
            if ancestor_of(source, distance) == target:
                found.append(source)
    return found


def reference(right_sides, diag_inverse, panels, block_map):
    outputs = []
    rounded = []
    for level_index in range(LEV - 1, -1, -1):
        for supernode in range(2 ** LEV - 2 ** (level_index + 1), 2 ** LEV - 2 ** level_index):
            residual = right_sides[supernode]
            if level_index < LEV - 1:
                partial_value = jnp.zeros((N_ROW, R, W), jnp.float32)
                for source in descendants_of(supernode):
                    chosen = jnp.repeat((block_map[source] == supernode).T, BLK, axis=1)
                    selected = jnp.sum(jnp.where(chosen[:, :, None], panels[source].astype(jnp.float32), 0.0), axis=0)
                    partial_value = partial_value + jnp.einsum(
                        "cpk,ipk->pci",
                        rounded[source].astype(jnp.float32).reshape(R, N_ROW, SPAN),
                        selected.reshape(W, N_ROW, SPAN),
                        precision=lax.Precision.HIGHEST)
                partial_value = lax.optimization_barrier(partial_value.astype(jnp.bfloat16))
                residual = residual - jnp.sum(partial_value.astype(jnp.float32), axis=0)
            leveled = lax.optimization_barrier(residual.astype(jnp.bfloat16)).astype(jnp.float32)
            pieces = jnp.einsum(
                "cqk,iqk->qci",
                leveled.reshape(R, N_COL, BLK),
                diag_inverse[supernode].astype(jnp.float32).reshape(W, N_COL, BLK),
                precision=lax.Precision.HIGHEST)
            pieces = lax.optimization_barrier(pieces.astype(jnp.bfloat16))
            solution = jnp.sum(pieces.astype(jnp.float32), axis=0)
            outputs.append(solution)
            rounded.append(solution.astype(jnp.bfloat16))
    return jnp.stack(outputs)
```

```python
import jax
import jax.numpy as jnp
from jax import lax
from jax.experimental import pallas as pl
from jax.experimental.pallas import tpu as pltpu
from jax.sharding import Mesh
from jax.sharding import PartitionSpec as P

ROW = ("x", "y")
COL = ("z", "core")
ALL = ("x", "y", "z", "core")
NR = 32
NC = 16
VMEM_LIMIT = 56 * 1024 * 1024
F32 = jnp.float32
BF16 = jnp.bfloat16


def params(n=1):
    return pltpu.CompilerParams(
        vmem_limit_bytes=VMEM_LIMIT, dimension_semantics=("arbitrary",) * n
    )


def dot_t(a, b):
    return lax.dot_general(a, b, (((1,), (1,)), ((), ())), preferred_element_type=F32)


def slot_of(meta, source, target):
    base = 4 + (source * NC + meta[0]) * 3
    second = jnp.where(meta[base + 1] == target, 1, 0)
    slot = jnp.where(meta[base + 2] == target, 2, second)
    return slot, meta[base + slot] == target


def upper_pair(b):
    is_low = b < 8
    source = jnp.where(is_low, 8 + b // 2, 4 + b)
    target = jnp.where(is_low & (b % 2 == 0), 12 + b // 4, 14)
    return source, target


def select_upper(meta, panels):
    def kernel(meta_ref, p_ref, o_ref):
        _, found = slot_of(meta_ref, *upper_pair(pl.program_id(0)))
        o_ref[...] = jnp.where(found, p_ref[0], jnp.zeros_like(p_ref[0]))

    def index(b, meta_ref):
        source, target = upper_pair(b)
        slot, _ = slot_of(meta_ref, source, target)
        return source, slot, 0, 0

    return pl.pallas_call(
        kernel,
        grid_spec=pltpu.PrefetchScalarGridSpec(
            num_scalar_prefetch=1,
            grid=(10,),
            in_specs=[pl.BlockSpec((1, 1, 256, 128), index)],
            out_specs=pl.BlockSpec((1, 256, 128), lambda b, m: (b, 0, 0)),
        ),
        out_shape=jax.ShapeDtypeStruct((10, 256, 128), BF16),
        compiler_params=params(),
        name="select_upper",
    )(meta, panels)


def solve_leaves(spread, inverse):
    def kernel(b_ref, d_ref, x_ref, h_ref):
        acc = jnp.zeros((32, 128), F32)
        for c in range(NC):
            left = b_ref[2 * c : 2 * c + 2, 0].reshape(32, 256)
            acc = acc + dot_t(left, d_ref[c, 0])
        x_ref[0] = acc
        h_ref[0] = acc.astype(BF16)

    return pl.pallas_call(
        kernel,
        grid=(8,),
        in_specs=[
            pl.BlockSpec((32, 1, 16, 256), lambda n: (0, n, 0, 0)),
            pl.BlockSpec((16, 1, 128, 256), lambda n: (0, n, 0, 0)),
        ],
        out_specs=[
            pl.BlockSpec((1, 32, 128), lambda n: (n, 0, 0)),
            pl.BlockSpec((1, 32, 128), lambda n: (n, 0, 0)),
        ],
        out_shape=[
            jax.ShapeDtypeStruct((8, 32, 128), F32),
            jax.ShapeDtypeStruct((8, 32, 128), BF16),
        ],
        compiler_params=params(),
        name="solve_leaves",
    )(spread, inverse)


def update_from_leaves(meta, own, other, panels):
    def kernel(meta_ref, a_ref, b_ref, p_ref, o_ref):
        core = meta_ref[1]
        for t in range(7):
            target = 8 + t
            if t < 4:
                sources = range(2 * t, 2 * t + 2)
            elif t < 6:
                sources = range(4 * (t - 4), 4 * (t - 4) + 4)
            else:
                sources = range(8)
            blocks = []
            for s in sources:
                slot, found = slot_of(meta_ref, s, target)
                block = p_ref[s, slot]
                blocks.append(jnp.where(found, block, jnp.zeros_like(block)))
            for parity, x_ref in ((core, a_ref), (1 - core, b_ref)):
                acc = jnp.zeros((256, 256), F32)
                for s, block in zip(sources, blocks, strict=True):
                    acc = acc + dot_t(x_ref[:, s].reshape(256, 128), block)
                o_ref[:, pl.ds(parity, 1), :, t] = acc.astype(BF16).reshape(8, 1, 2, 16, 256)

    return pl.pallas_call(
        kernel,
        grid_spec=pltpu.PrefetchScalarGridSpec(
            num_scalar_prefetch=1,
            grid=(1,),
            in_specs=[
                pl.BlockSpec((8, 8, 32, 128), lambda i, m: (0, 0, 0, 0)),
                pl.BlockSpec((8, 8, 32, 128), lambda i, m: (0, 0, 0, 0)),
                pl.BlockSpec((8, 3, 256, 128), lambda i, m: (0, 0, 0, 0)),
            ],
            out_specs=pl.BlockSpec((8, 2, 2, 7, 16, 256), lambda i, m: (0, 0, 0, 0, 0, 0)),
        ),
        out_shape=jax.ShapeDtypeStruct((8, 2, 2, 7, 16, 256), BF16),
        compiler_params=params(),
        name="update_from_leaves",
    )(meta, own, other, panels)


def store_pieces(o_ref, residual, d_ref):
    for c in range(NC):
        for half in range(2):
            piece = dot_t(residual, d_ref[2 * c + half, 0])
            o_ref[c, 0, :, 128 * half : 128 * half + 128] = piece.astype(BF16)


def solve_first(parts, right, inverse):
    def kernel(p_ref, b_ref, d_ref, o_ref, rest_ref, scratch):
        n = pl.program_id(0)

        @pl.when(n == 0)
        def _():
            residual = b_ref[...] - jnp.sum(p_ref[...].astype(F32), axis=0)
            scratch[...] = residual[:4].astype(BF16)
            rest_ref[...] = residual[4:]

        store_pieces(o_ref, scratch[n], d_ref)

    return pl.pallas_call(
        kernel,
        grid=(4,),
        in_specs=[
            pl.BlockSpec((32, 7, 16, 256), lambda n: (0, 0, 0, 0)),
            pl.BlockSpec((7, 16, 256), lambda n: (0, 0, 0)),
            pl.BlockSpec((32, 1, 128, 256), lambda n: (0, n, 0, 0)),
        ],
        out_specs=[
            pl.BlockSpec((16, 1, 16, 256), lambda n: (0, n, 0, 0)),
            pl.BlockSpec((3, 16, 256), lambda n: (0, 0, 0)),
        ],
        out_shape=[
            jax.ShapeDtypeStruct((16, 4, 16, 256), BF16),
            jax.ShapeDtypeStruct((3, 16, 256), F32),
        ],
        scratch_shapes=[pltpu.VMEM((4, 16, 256), BF16)],
        compiler_params=params(),
        name="solve_first",
    )(parts, right, inverse)


def solve_next(known, blocks, rest, inverse, nodes, per_source, first_node):
    count, waiting = blocks.shape[1], rest.shape[0]
    after = waiting - nodes
    sources = known.shape[1]

    def kernel(x_ref, l_ref, rest_ref, d_ref, o_ref, *others):
        later_ref = others[0] if after else None
        acc, half = others[-2], others[-1]
        i = pl.program_id(0)

        @pl.when(i == 0)
        def _():
            acc[...] = rest_ref[...]

        @pl.when(i < count)
        def _():
            source = i // per_source
            if per_source == 2:
                target = jnp.where(i % 2 == 0, source // 2, waiting - 1)
            else:
                target = 0
            total = jnp.zeros((16, 256), F32)
            for r in range(NR):
                left = x_ref[r // 2, source, :, 128 * (r % 2) : 128 * (r % 2) + 128]
                total = total + dot_t(left, l_ref[r, 0])
            acc[target] = acc[target] - total

        @pl.when(i == count)
        def _():
            half[...] = acc[:nodes].astype(BF16)
            if after:
                later_ref[...] = acc[nodes:]

        @pl.when(i >= count)
        def _():
            store_pieces(o_ref, half[i - count], d_ref)

    out_specs = [
        pl.BlockSpec((16, 1, 16, 256), lambda i: (0, jnp.maximum(i - count, 0), 0, 0))
    ]
    out_shape = [jax.ShapeDtypeStruct((16, nodes, 16, 256), BF16)]
    if after:
        out_specs.append(pl.BlockSpec((after, 16, 256), lambda i: (0, 0, 0)))
        out_shape.append(jax.ShapeDtypeStruct((after, 16, 256), F32))
    return pl.pallas_call(
        kernel,
        grid=(count + nodes,),
        in_specs=[
            pl.BlockSpec((16, sources, 16, 256), lambda i: (0, 0, 0, 0)),
            pl.BlockSpec((32, 1, 256, 128), lambda i: (0, jnp.minimum(i, count - 1), 0, 0)),
            pl.BlockSpec((waiting, 16, 256), lambda i: (0, 0, 0)),
            pl.BlockSpec(
                (32, 1, 128, 256), lambda i: (0, first_node + jnp.maximum(i - count, 0), 0, 0)
            ),
        ],
        out_specs=out_specs,
        out_shape=out_shape,
        scratch_shapes=[pltpu.VMEM((waiting, 16, 256), F32), pltpu.VMEM((nodes, 16, 256), BF16)],
        compiler_params=params(),
        name="solve_next",
    )(known, blocks, rest, inverse)


def add_pieces(pieces):
    n = pieces.shape[1]

    def kernel(p_ref, x_ref, h_ref):
        total = jnp.sum(p_ref[...].astype(F32), axis=0)
        x_ref[...] = total
        h_ref[...] = total.astype(BF16)

    return pl.pallas_call(
        kernel,
        out_shape=[
            jax.ShapeDtypeStruct((n, 16, 256), F32),
            jax.ShapeDtypeStruct((n, 16, 256), BF16),
        ],
        compiler_params=params(0),
        name="add_pieces",
    )(pieces)


def exchange(values, axes):
    shape = values.shape
    flat = values.reshape(shape[0], -1, shape[-1])
    return lax.all_to_all(flat, axes, 0, 0, tiled=True).reshape(shape)


def spread_over(values, axes, size):
    return exchange(jnp.broadcast_to(values[None], (size,) + values.shape), axes)


def place(values, row):
    odd = row % 2 == 1
    low, high = values[..., :128], values[..., 128:]
    received = []
    for p in range(2):
        pairs = []
        for r in range(NR):
            for c in range(NC):
                pairs.append((r * NC + c, (2 * c + (r + p) % 2) * NC + r // 2))
        take_high = odd if p == 0 else ~odd
        received.append(lax.ppermute(jnp.where(take_high, high, low), ALL, pairs))
    first = jnp.where(odd, received[1], received[0])
    second = jnp.where(odd, received[0], received[1])
    return jnp.concatenate([first, second], axis=1)


def per_device(right_sides, diag_inverse, panels, block_map):
    row = lax.axis_index(ROW)
    col = lax.axis_index(COL)
    core = lax.axis_index("core")
    zero = jnp.zeros((), jnp.int32)
    meta = jnp.concatenate(
        [jnp.stack([col, core, zero, zero]).astype(jnp.int32), block_map.reshape(-1)]
    )

    leaf_inverse = lax.all_gather(diag_inverse[:8], COL, axis=0)
    upper = select_upper(meta, panels)
    inverse_two = lax.all_gather(diag_inverse[8:], ROW, axis=0)
    blocks_two = lax.all_gather(upper[:8], ROW, axis=0)
    blocks_one = lax.all_gather(upper[8:], ROW, axis=0)

    pairs = [
        (r * NC + c, (2 * c + r % 2) * NC + r // 2) for r in range(NR) for c in range(NC)
    ]
    moved = lax.ppermute(right_sides[:8].astype(BF16), ALL, pairs)
    spread = spread_over(moved, ROW, NR)
    leaves, leaves_half = solve_leaves(spread, leaf_inverse)
    own = spread_over(leaves_half, "z", 8)
    other = lax.ppermute(own, "core", [(0, 1), (1, 0)])
    parts = update_from_leaves(meta, own, other, panels)
    parts = exchange(parts.reshape(NR, 7, 16, 256), ROW)

    pieces, rest = solve_first(parts, right_sides[8:], inverse_two)
    two, two_half = add_pieces(exchange(pieces, COL))
    known = lax.all_gather(two_half, COL, axis=0)
    pieces, rest = solve_next(known, blocks_two, rest, inverse_two, 2, 2, 4)
    one, one_half = add_pieces(exchange(pieces, COL))
    known = spread_over(one_half, COL, NC)
    early = place(jnp.concatenate([two, one], axis=0), row)
    (pieces,) = solve_next(known, blocks_one, rest, inverse_two, 1, 1, 6)
    root, _ = add_pieces(exchange(pieces, COL))
    return jnp.concatenate([leaves, early, place(root, row)], axis=0)


def solution(mesh):
    split = Mesh(mesh.devices.reshape(4, 8, 8, 2), ALL)
    return jax.shard_map(
        per_device,
        mesh=split,
        in_specs=(P(None, ROW, COL), P(None, ROW, COL), P(None, None, COL, ROW), P()),
        out_specs=P(None, COL, ROW),
        check_vma=False,
    )
```

```python
import jax
import jax.numpy as jnp
from jax import lax
from jax.experimental import pallas as pl
from jax.experimental.pallas import tpu as pltpu
from jax.sharding import Mesh
from jax.sharding import PartitionSpec as P

ROW = ("x", "y")
COL = ("z", "core")
ALL = ("x", "y", "z", "core")
NR = 32
NC = 16
VMEM_LIMIT = 24 * 1024 * 1024
F32 = jnp.float32
BF16 = jnp.bfloat16


def params(n=1):
    return pltpu.CompilerParams(
        vmem_limit_bytes=VMEM_LIMIT, dimension_semantics=("arbitrary",) * n
    )


def dot_t(a, b):
    return lax.dot_general(a, b, (((1,), (1,)), ((), ())), preferred_element_type=F32)


def slot_of(meta, source, target):
    base = 4 + (source * NC + meta[0]) * 3
    second = jnp.where(meta[base + 1] == target, 1, 0)
    slot = jnp.where(meta[base + 2] == target, 2, second)
    return slot, meta[base + slot] == target


def upper_pair(b):
    is_low = b < 8
    source = jnp.where(is_low, 8 + b // 2, 4 + b)
    target = jnp.where(is_low & (b % 2 == 0), 12 + b // 4, 14)
    return source, target


def select_upper(meta, panels):
    def kernel(meta_ref, p_ref, o_ref):
        _, found = slot_of(meta_ref, *upper_pair(pl.program_id(0)))
        o_ref[...] = jnp.where(found, p_ref[0], jnp.zeros_like(p_ref[0]))

    def index(b, meta_ref):
        source, target = upper_pair(b)
        slot, _ = slot_of(meta_ref, source, target)
        return source, slot, 0, 0

    return pl.pallas_call(
        kernel,
        grid_spec=pltpu.PrefetchScalarGridSpec(
            num_scalar_prefetch=1,
            grid=(10,),
            in_specs=[pl.BlockSpec((1, 1, 256, 128), index)],
            out_specs=pl.BlockSpec((1, 256, 128), lambda b, m: (b, 0, 0)),
        ),
        out_shape=jax.ShapeDtypeStruct((10, 256, 128), BF16),
        compiler_params=params(),
        name="select_upper",
    )(meta, panels)


def solve_leaves(spread, inverse):
    def kernel(b_ref, d_ref, x_ref, h_ref):
        acc = jnp.zeros((32, 128), F32)
        for c in range(NC):
            left = b_ref[2 * c : 2 * c + 2, 0].reshape(32, 256)
            acc = acc + dot_t(left, d_ref[c, 0])
        x_ref[0] = acc
        h_ref[0] = acc.astype(BF16)

    return pl.pallas_call(
        kernel,
        grid=(8,),
        in_specs=[
            pl.BlockSpec((32, 1, 16, 256), lambda n: (0, n, 0, 0)),
            pl.BlockSpec((16, 1, 128, 256), lambda n: (0, n, 0, 0)),
        ],
        out_specs=[
            pl.BlockSpec((1, 32, 128), lambda n: (n, 0, 0)),
            pl.BlockSpec((1, 32, 128), lambda n: (n, 0, 0)),
        ],
        out_shape=[
            jax.ShapeDtypeStruct((8, 32, 128), F32),
            jax.ShapeDtypeStruct((8, 32, 128), BF16),
        ],
        compiler_params=params(),
        name="solve_leaves",
    )(spread, inverse)


def update_from_leaves(meta, own, other, panels):
    def kernel(meta_ref, a_ref, b_ref, p_ref, o_ref):
        core = meta_ref[1]
        for t in range(7):
            target = 8 + t
            if t < 4:
                sources = range(2 * t, 2 * t + 2)
            elif t < 6:
                sources = range(4 * (t - 4), 4 * (t - 4) + 4)
            else:
                sources = range(8)
            blocks = []
            for s in sources:
                slot, found = slot_of(meta_ref, s, target)
                block = p_ref[s, slot]
                blocks.append(jnp.where(found, block, jnp.zeros_like(block)))
            for parity, x_ref in ((core, a_ref), (1 - core, b_ref)):
                acc = jnp.zeros((256, 256), F32)
                for s, block in zip(sources, blocks, strict=True):
                    acc = acc + dot_t(x_ref[:, s].reshape(256, 128), block)
                o_ref[:, pl.ds(parity, 1), :, t] = acc.astype(BF16).reshape(8, 1, 2, 16, 256)

    return pl.pallas_call(
        kernel,
        grid_spec=pltpu.PrefetchScalarGridSpec(
            num_scalar_prefetch=1,
            grid=(1,),
            in_specs=[
                pl.BlockSpec((8, 8, 32, 128), lambda i, m: (0, 0, 0, 0)),
                pl.BlockSpec((8, 8, 32, 128), lambda i, m: (0, 0, 0, 0)),
                pl.BlockSpec((8, 3, 256, 128), lambda i, m: (0, 0, 0, 0)),
            ],
            out_specs=pl.BlockSpec((8, 2, 2, 7, 16, 256), lambda i, m: (0, 0, 0, 0, 0, 0)),
        ),
        out_shape=jax.ShapeDtypeStruct((8, 2, 2, 7, 16, 256), BF16),
        compiler_params=params(),
        name="update_from_leaves",
    )(meta, own, other, panels)


VMEM = pl.BlockSpec(memory_space=pltpu.VMEM)
SMEM = pl.BlockSpec(memory_space=pltpu.SMEM)


def first_residual(meta, parts, right):
    def kernel(meta_ref, p_ref, b_ref, even_ref, odd_ref):
        residual = b_ref[8:] - jnp.sum(p_ref[...].astype(F32), axis=0)
        low, high = residual[..., :128], residual[..., 128:]
        odd = meta_ref[2] == 1
        even_ref[...] = jnp.where(odd, high, low)
        odd_ref[...] = jnp.where(odd, low, high)

    return pl.pallas_call(
        kernel,
        in_specs=[SMEM, VMEM, VMEM],
        out_specs=[VMEM, VMEM],
        out_shape=[jax.ShapeDtypeStruct((7, 16, 128), F32)] * 2,
        compiler_params=params(0),
        name="first_residual",
    )(meta, parts, right)


def join_residual(meta, even, odd_sent):
    def kernel(meta_ref, a_ref, b_ref, o_ref, rest_ref):
        odd = meta_ref[2] == 1
        a, b = a_ref[...], b_ref[...]
        first = jnp.where(odd, b, a)
        second = jnp.where(odd, a, b)
        rest_ref[:, :16] = first[4:]
        rest_ref[:, 16:] = second[4:]
        both = jnp.concatenate([first[:4], second[:4]], axis=1).astype(BF16)
        for r in range(NR):
            o_ref[r] = both

    return pl.pallas_call(
        kernel,
        in_specs=[SMEM, VMEM, VMEM],
        out_specs=[VMEM, VMEM],
        out_shape=[
            jax.ShapeDtypeStruct((NR, 4, 32, 128), BF16),
            jax.ShapeDtypeStruct((3, 32, 128), F32),
        ],
        compiler_params=params(0),
        name="join_residual",
    )(meta, even, odd_sent)


def solve_node(x_ref, d_ref, n, place):
    acc = jnp.zeros((32, 128), F32)
    for c in range(NC):
        left = jnp.concatenate([x_ref[2 * c, n], x_ref[2 * c + 1, n]], axis=1)
        acc = acc + dot_t(left, d_ref[c, place])
    return acc


def solve_level(residual, inverse, place, blocks, block_place, targets):
    nodes = residual.shape[1]

    def kernel(x_ref, d_ref, l_ref, s_ref, o_ref):
        solved = []
        for n in range(nodes):
            x = solve_node(x_ref, d_ref, n, place + n)
            s_ref[n] = x
            solved.append(x.astype(BF16))
        for c in range(NC):
            for t, terms in enumerate(targets):
                acc = jnp.zeros((32, 256), F32)
                for s, b in terms:
                    acc = acc + dot_t(solved[s], l_ref[c, block_place + b])
                out = acc.astype(BF16)
                o_ref[2 * c, t] = out[:, :128]
                o_ref[2 * c + 1, t] = out[:, 128:]

    return pl.pallas_call(
        kernel,
        in_specs=[VMEM, VMEM, VMEM],
        out_specs=[VMEM, VMEM],
        out_shape=[
            jax.ShapeDtypeStruct((nodes, 32, 128), F32),
            jax.ShapeDtypeStruct((NR, len(targets), 32, 128), BF16),
        ],
        compiler_params=params(0),
        name="solve_level",
    )(residual, inverse, blocks)


def solve_root(residual, inverse):
    def kernel(x_ref, d_ref, s_ref):
        s_ref[0] = solve_node(x_ref, d_ref, 0, 6)

    return pl.pallas_call(
        kernel,
        in_specs=[VMEM, VMEM],
        out_specs=VMEM,
        out_shape=jax.ShapeDtypeStruct((1, 32, 128), F32),
        compiler_params=params(0),
        name="solve_root",
    )(residual, inverse)


def next_residual(parts, rest, nodes):
    count = rest.shape[0]
    after = count - nodes

    def kernel(p_ref, rest_ref, o_ref, *later):
        residual = rest_ref[...] - jnp.sum(p_ref[...].astype(F32), axis=0)
        half = residual[:nodes].astype(BF16)
        for r in range(NR):
            o_ref[r] = half
        if after:
            later[0][...] = residual[nodes:]

    out_shape = [jax.ShapeDtypeStruct((NR, nodes, 32, 128), BF16)]
    if after:
        out_shape.append(jax.ShapeDtypeStruct((after, 32, 128), F32))
    return pl.pallas_call(
        kernel,
        in_specs=[VMEM, VMEM],
        out_specs=[VMEM] * len(out_shape),
        out_shape=out_shape,
        compiler_params=params(0),
        name="next_residual",
    )(parts, rest)


def exchange(values, axes):
    shape = values.shape
    flat = values.reshape(shape[0], -1, shape[-1])
    return lax.all_to_all(flat, axes, 0, 0, tiled=True).reshape(shape)


def spread_over(values, axes, size):
    return exchange(jnp.broadcast_to(values[None], (size,) + values.shape), axes)


def to_owner(values, p):
    pairs = [
        (r * NC + c, (2 * c + (r + p) % 2) * NC + r // 2) for r in range(NR) for c in range(NC)
    ]
    return lax.ppermute(values, ALL, pairs)


def per_device(right_sides, diag_inverse, panels, block_map):
    row = lax.axis_index(ROW)
    col = lax.axis_index(COL)
    core = lax.axis_index("core")
    leaf_inverse = lax.all_gather(diag_inverse[:8], COL, axis=0)
    moved = to_owner(right_sides[:8].astype(BF16), 0)
    spread = spread_over(moved, ROW, NR)

    zero = jnp.zeros((), jnp.int32)
    meta = jnp.concatenate(
        [jnp.stack([col, core, row % 2, zero]).astype(jnp.int32), block_map.reshape(-1)]
    )
    meta, _ = lax.optimization_barrier((meta, moved))
    blocks = lax.all_gather(select_upper(meta, panels), COL, axis=0)
    inverse = lax.all_gather(diag_inverse[8:], COL, axis=0)

    leaves, leaves_half = solve_leaves(spread, leaf_inverse)
    own = spread_over(leaves_half, "z", 8)
    other = lax.ppermute(own, "core", [(0, 1), (1, 0)])
    parts = update_from_leaves(meta, own, other, panels)
    parts = exchange(parts.reshape(NR, 7, 16, 256), ROW)
    even, odd = first_residual(meta, parts, right_sides)
    residual, rest = join_residual(meta, to_owner(even, 0), to_owner(odd, 1))

    residual = exchange(residual, ROW)
    targets = [[(0, 0), (1, 2)], [(2, 4), (3, 6)], [(0, 1), (1, 3), (2, 5), (3, 7)]]
    two, parts = solve_level(residual, inverse, 0, blocks, 0, targets)
    residual, rest = next_residual(exchange(parts, ROW), rest, 2)
    residual = exchange(residual, ROW)
    one, parts = solve_level(residual, inverse, 4, blocks, 8, [[(0, 0), (1, 1)]])
    (residual,) = next_residual(exchange(parts, ROW), rest, 1)
    root = solve_root(exchange(residual, ROW), inverse)
    return jnp.concatenate([leaves, two, one, root], axis=0)


def solution(mesh):
    split = Mesh(mesh.devices.reshape(4, 8, 8, 2), ALL)
    return jax.shard_map(
        per_device,
        mesh=split,
        in_specs=(P(None, ROW, COL), P(None, ROW, COL), P(None, None, COL, ROW), P()),
        out_specs=P(None, COL, ROW),
        check_vma=False,
    )
```

```python
import jax
import jax.numpy as jnp
from jax import lax
from jax.experimental import pallas as pl
from jax.experimental.pallas import tpu as pltpu
from jax.sharding import Mesh
from jax.sharding import PartitionSpec as P

ROW = ("x", "y")
COL = ("z", "core")
ALL = ("x", "y", "z", "core")
NR = 32
NC = 16
VMEM_LIMIT = 24 * 1024 * 1024
F32 = jnp.float32
BF16 = jnp.bfloat16
VMEM = pl.BlockSpec(memory_space=pltpu.VMEM)
SMEM = pl.BlockSpec(memory_space=pltpu.SMEM)
HBM = pl.BlockSpec(memory_space=pltpu.HBM)


def params(n=1):
    return pltpu.CompilerParams(
        vmem_limit_bytes=VMEM_LIMIT, dimension_semantics=("arbitrary",) * n
    )


def dot_t(a, b):
    return lax.dot_general(a, b, (((1,), (1,)), ((), ())), preferred_element_type=F32)


def slot_of(meta, source, target):
    base = 4 + (source * NC + meta[0]) * 3
    second = jnp.where(meta[base + 1] == target, 1, 0)
    slot = jnp.where(meta[base + 2] == target, 2, second)
    return slot, meta[base + slot] == target


def gathered_block(b):
    is_low = b < 8
    source = jnp.where(is_low, 8 + b // 2, 4 + b)
    target = jnp.where(is_low & (b % 2 == 0), 12 + b // 4, 14)
    return source, target


def stack_upper(meta, inverse, panels, first_node, nodes, first_block, blocks):
    def kernel(meta_ref, d_ref, p_ref, o_ref):
        i = pl.program_id(0)

        @pl.when(i < nodes)
        def _():
            o_ref[...] = d_ref[...]

        @pl.when(i >= nodes)
        def _():
            _, found = slot_of(meta_ref, *gathered_block(first_block + i - nodes))
            block = p_ref[0, 0]
            block = jnp.where(found, block, jnp.zeros_like(block))
            o_ref[0, :, :128] = block[:128]
            o_ref[0, :, 128:] = block[128:]

    def index(i, meta_ref):
        source, target = gathered_block(first_block + jnp.maximum(i - nodes, 0))
        slot, _ = slot_of(meta_ref, source, target)
        return source, slot, 0, 0

    return pl.pallas_call(
        kernel,
        grid_spec=pltpu.PrefetchScalarGridSpec(
            num_scalar_prefetch=1,
            grid=(nodes + blocks,),
            in_specs=[
                pl.BlockSpec(
                    (1, 128, 256), lambda i, m: (first_node + jnp.minimum(i, nodes - 1), 0, 0)
                ),
                pl.BlockSpec((1, 1, 256, 128), index),
            ],
            out_specs=pl.BlockSpec((1, 128, 256), lambda i, m: (i, 0, 0)),
        ),
        out_shape=jax.ShapeDtypeStruct((nodes + blocks, 128, 256), BF16),
        compiler_params=params(),
        name="stack_upper",
    )(meta, inverse, panels)


def solve_leaves(spread, inverse):
    def kernel(b_ref, d_hbm, x_ref, h_ref, d_ref, sem):
        copies = [
            pltpu.make_async_copy(d_hbm.at[:, n], d_ref.at[:, n], sem.at[n]) for n in range(8)
        ]
        for copy in copies:
            copy.start()
        for n in range(8):
            copies[n].wait()
            acc = jnp.zeros((32, 128), F32)
            for c in range(NC):
                left = b_ref[2 * c : 2 * c + 2, n].reshape(32, 256)
                acc = acc + dot_t(left, d_ref[c, n])
            x_ref[n] = acc
            half = acc.astype(BF16)
            for z in range(8):
                h_ref[z, n] = half

    return pl.pallas_call(
        kernel,
        in_specs=[VMEM, HBM],
        out_specs=[VMEM, VMEM],
        out_shape=[
            jax.ShapeDtypeStruct((8, 32, 128), F32),
            jax.ShapeDtypeStruct((8, 8, 32, 128), BF16),
        ],
        scratch_shapes=[
            pltpu.VMEM((NC, 8, 128, 256), BF16),
            pltpu.SemaphoreType.DMA((8,)),
        ],
        compiler_params=params(0),
        name="solve_leaves",
    )(spread, inverse)


def update_from_leaves(meta, own, other, panels, right):
    def kernel(meta_ref, a_ref, b_ref, p_ref, r_ref, o_ref):
        core, row = meta_ref[1], meta_ref[2]
        for t in range(7):
            target = 8 + t
            if t < 4:
                sources = range(2 * t, 2 * t + 2)
            elif t < 6:
                sources = range(4 * (t - 4), 4 * (t - 4) + 4)
            else:
                sources = range(8)
            blocks = []
            for s in sources:
                slot, found = slot_of(meta_ref, s, target)
                block = p_ref[s, slot]
                blocks.append(jnp.where(found, block, jnp.zeros_like(block)))
            for parity, x_ref in ((core, a_ref), (1 - core, b_ref)):
                acc = jnp.zeros((256, 256), F32)
                for s, block in zip(sources, blocks, strict=True):
                    acc = acc + dot_t(x_ref[:, s].reshape(256, 128), block)
                for half in range(2):
                    value = acc[:, 128 * half : 128 * half + 128].astype(BF16)
                    o_ref[:, pl.ds(parity, 1), half, t] = value.reshape(8, 1, 32, 128)
        z, parity = row // 4, (row // 2) % 2
        start = pl.multiple_of(16 * (row % 2), 16)
        for half in range(2):
            for t in range(7):
                part = o_ref[z, parity, half, t, pl.ds(start, 16), :].astype(F32)
                part = part - r_ref[8 + t, :, 128 * half : 128 * half + 128]
                o_ref[z, parity, half, t, pl.ds(start, 16), :] = part.astype(BF16)

    return pl.pallas_call(
        kernel,
        grid=(1,),
        in_specs=[
            SMEM,
            VMEM,
            VMEM,
            pl.BlockSpec((8, 3, 256, 128), lambda i: (0, 0, 0, 0)),
            VMEM,
        ],
        out_specs=VMEM,
        out_shape=jax.ShapeDtypeStruct((8, 2, 2, 7, 32, 128), BF16),
        compiler_params=params(),
        name="update_from_leaves",
    )(meta, own, other, panels, right)


def first_residual(parts):
    def kernel(p_ref, o_ref):
        o_ref[...] = (-jnp.sum(p_ref[...].astype(F32), axis=0)).astype(BF16)

    return pl.pallas_call(
        kernel,
        in_specs=[VMEM],
        out_specs=VMEM,
        out_shape=jax.ShapeDtypeStruct((7, 32, 128), BF16),
        compiler_params=params(0),
        name="first_residual",
    )(parts)


def solve_node(x_ref, d_ref, n, place):
    acc = jnp.zeros((32, 128), F32)
    for c in range(NC):
        left = jnp.concatenate([x_ref[2 * c, n], x_ref[2 * c + 1, n]], axis=1)
        acc = acc + dot_t(left, d_ref[c, place])
    return acc


def update_above(solved, w_ref, c, nodes, targets, o_ref):
    for t, terms in enumerate(targets):
        for half in range(2):
            acc = jnp.zeros((32, 128), F32)
            for s, b in terms:
                block = w_ref[c, nodes + b, :, 128 * half : 128 * half + 128]
                acc = acc + dot_t(solved[s], block)
            o_ref[2 * c + half, t] = acc.astype(BF16)


def solve_level(residual, weights, nodes, targets, stream):
    groups = 4

    def body(x_ref, w_ref, s_ref, o_ref, wait):
        solved = []
        for n in range(nodes):
            wait(n)
            x = solve_node(x_ref, w_ref, n, n)
            s_ref[n] = x
            solved.append(x.astype(BF16))
        for g in range(groups):
            wait(nodes + g)
            for c in range(g * NC // groups, (g + 1) * NC // groups):
                update_above(solved, w_ref, c, nodes, targets, o_ref)

    def direct(x_ref, w_ref, s_ref, o_ref):
        body(x_ref, w_ref, s_ref, o_ref, lambda i: None)

    def streamed(x_ref, w_hbm, s_ref, o_ref, w_ref, sem):
        pieces = [(slice(None), n) for n in range(nodes)]
        for g in range(groups):
            pieces.append((pl.ds(g * NC // groups, NC // groups), slice(nodes, None)))
        copies = [
            pltpu.make_async_copy(w_hbm.at[piece], w_ref.at[piece], sem.at[i])
            for i, piece in enumerate(pieces)
        ]
        for copy in copies:
            copy.start()
        body(x_ref, w_ref, s_ref, o_ref, lambda i: copies[i].wait())

    scratch = [
        pltpu.VMEM(weights.shape, BF16),
        pltpu.SemaphoreType.DMA((nodes + groups,)),
    ]
    return pl.pallas_call(
        streamed if stream else direct,
        in_specs=[VMEM, HBM if stream else VMEM],
        out_specs=[VMEM, VMEM],
        out_shape=[
            jax.ShapeDtypeStruct((nodes, 32, 128), F32),
            jax.ShapeDtypeStruct((NR, len(targets), 32, 128), BF16),
        ],
        scratch_shapes=scratch if stream else [],
        compiler_params=params(0),
        name="solve_level",
    )(residual, weights)


def solve_root(residual, inverse):
    def kernel(x_ref, d_ref, s_ref):
        s_ref[0] = solve_node(x_ref, d_ref, 0, 2)

    return pl.pallas_call(
        kernel,
        in_specs=[VMEM, VMEM],
        out_specs=VMEM,
        out_shape=jax.ShapeDtypeStruct((1, 32, 128), F32),
        compiler_params=params(0),
        name="solve_root",
    )(residual, inverse)


def next_residual(parts, rest, nodes):
    count = rest.shape[0]
    after = count - nodes

    def kernel(p_ref, rest_ref, o_ref, *later):
        residual = rest_ref[...].astype(F32) - jnp.sum(p_ref[...].astype(F32), axis=0)
        half = residual[:nodes].astype(BF16)
        for r in range(NR):
            o_ref[r] = half
        if after:
            later[0][...] = residual[nodes:]

    out_shape = [jax.ShapeDtypeStruct((NR, nodes, 32, 128), BF16)]
    if after:
        out_shape.append(jax.ShapeDtypeStruct((after, 32, 128), F32))
    return pl.pallas_call(
        kernel,
        in_specs=[VMEM, VMEM],
        out_specs=[VMEM] * len(out_shape),
        out_shape=out_shape,
        compiler_params=params(0),
        name="next_residual",
    )(parts, rest)


def exchange(values, axes):
    shape = values.shape
    flat = values.reshape(shape[0], -1, shape[-1])
    return lax.all_to_all(flat, axes, 0, 0, tiled=True).reshape(shape)


def spread_over(values, axes, size):
    return exchange(jnp.broadcast_to(values[None], (size,) + values.shape), axes)


def to_owner(values):
    pairs = [
        (r * NC + c, (2 * c + r % 2) * NC + r // 2) for r in range(NR) for c in range(NC)
    ]
    return lax.ppermute(values, ALL, pairs)


def per_device(right_sides, diag_inverse, panels, block_map):
    row = lax.axis_index(ROW)
    col = lax.axis_index(COL)
    core = lax.axis_index("core")
    leaf_inverse = lax.all_gather(diag_inverse[:8], COL, axis=0)
    moved = to_owner(right_sides[:8].astype(BF16))
    spread = spread_over(moved, ROW, NR)

    zero = jnp.zeros((), jnp.int32)
    meta = jnp.concatenate(
        [jnp.stack([col, core, row, zero]).astype(jnp.int32), block_map.reshape(-1)]
    )
    meta, _ = lax.optimization_barrier((meta, moved))
    stack_two = stack_upper(meta, diag_inverse, panels, 8, 4, 0, 8)
    stack_one = stack_upper(meta, diag_inverse, panels, 12, 3, 8, 2)

    leaves, copies = solve_leaves(spread, leaf_inverse)
    own = exchange(copies, "z")
    other = lax.ppermute(own, "core", [(0, 1), (1, 0)])
    stack_two, stack_one, own = lax.optimization_barrier((stack_two, stack_one, own))
    weights_two = lax.all_gather(stack_two, COL, axis=0)
    weights_one = lax.all_gather(stack_one, COL, axis=0)
    parts = update_from_leaves(meta, own, other, panels, right_sides)
    parts = exchange(parts.reshape(NR, 7, 32, 128), ROW)
    residual = to_owner(first_residual(parts))

    targets = [[(0, 0), (1, 2)], [(2, 4), (3, 6)], [(0, 1), (1, 3), (2, 5), (3, 7)]]
    spread = spread_over(residual[:4], ROW, NR)
    two, parts = solve_level(spread, weights_two, 4, targets, True)
    spread, rest = next_residual(exchange(parts, ROW), residual[4:], 2)
    targets = [[(0, 1), (1, 2)]]
    one, parts = solve_level(exchange(spread, ROW), weights_one, 2, targets, False)
    (spread,) = next_residual(exchange(parts, ROW), rest, 1)
    root = solve_root(exchange(spread, ROW), weights_one)
    return jnp.concatenate([leaves, two, one, root], axis=0)


def solution(mesh):
    split = Mesh(mesh.devices.reshape(4, 8, 8, 2), ALL)
    return jax.shard_map(
        per_device,
        mesh=split,
        in_specs=(P(None, ROW, COL), P(None, ROW, COL), P(None, None, COL, ROW), P()),
        out_specs=P(None, COL, ROW),
        check_vma=False,
    )
```

```python
import jax
import jax.numpy as jnp
from jax import lax
from jax.experimental import pallas as pl
from jax.experimental.pallas import tpu as pltpu
from jax.sharding import Mesh
from jax.sharding import PartitionSpec as P

ROW = ("x", "y")
COL = ("z", "core")
ALL = ("x", "y", "z", "core")
NR = 32
NC = 16
VMEM_LIMIT = 24 * 1024 * 1024
STREAM_LIMIT = 56 * 1024 * 1024
F32 = jnp.float32
BF16 = jnp.bfloat16
VMEM = pl.BlockSpec(memory_space=pltpu.VMEM)
SMEM = pl.BlockSpec(memory_space=pltpu.SMEM)
HBM = pl.BlockSpec(memory_space=pltpu.HBM)


def params(n=1, limit=VMEM_LIMIT):
    return pltpu.CompilerParams(
        vmem_limit_bytes=limit, dimension_semantics=("arbitrary",) * n
    )


def dot_t(a, b):
    return lax.dot_general(a, b, (((1,), (1,)), ((), ())), preferred_element_type=F32)


def slot_of(meta, source, target):
    base = 4 + (source * NC + meta[0]) * 3
    second = jnp.where(meta[base + 1] == target, 1, 0)
    slot = jnp.where(meta[base + 2] == target, 2, second)
    return slot, meta[base + slot] == target


def gathered_block(b):
    is_low = b < 8
    source = jnp.where(is_low, 8 + b // 2, 4 + b)
    target = jnp.where(is_low & (b % 2 == 0), 12 + b // 4, 14)
    return source, target


def stack_upper(meta, inverse, panels, first_node, nodes, first_block, blocks):
    def kernel(meta_ref, d_ref, p_ref, o_ref):
        i = pl.program_id(0)

        @pl.when(i < nodes)
        def _():
            o_ref[...] = d_ref[...]

        @pl.when(i >= nodes)
        def _():
            _, found = slot_of(meta_ref, *gathered_block(first_block + i - nodes))
            block = p_ref[0, 0]
            block = jnp.where(found, block, jnp.zeros_like(block))
            o_ref[0, :, :128] = block[:128]
            o_ref[0, :, 128:] = block[128:]

    def index(i, meta_ref):
        source, target = gathered_block(first_block + jnp.maximum(i - nodes, 0))
        slot, _ = slot_of(meta_ref, source, target)
        return source, slot, 0, 0

    return pl.pallas_call(
        kernel,
        grid_spec=pltpu.PrefetchScalarGridSpec(
            num_scalar_prefetch=1,
            grid=(nodes + blocks,),
            in_specs=[
                pl.BlockSpec(
                    (1, 128, 256), lambda i, m: (first_node + jnp.minimum(i, nodes - 1), 0, 0)
                ),
                pl.BlockSpec((1, 1, 256, 128), index),
            ],
            out_specs=pl.BlockSpec((1, 128, 256), lambda i, m: (i, 0, 0)),
        ),
        out_shape=jax.ShapeDtypeStruct((nodes + blocks, 128, 256), BF16),
        compiler_params=params(),
        name="stack_upper",
    )(meta, inverse, panels)


def solve_leaves(spread, inverse):
    def kernel(b_ref, d_hbm, x_ref, h_ref, d_ref, sem):
        copies = [
            pltpu.make_async_copy(d_hbm.at[:, n], d_ref.at[:, n], sem.at[n]) for n in range(8)
        ]
        for copy in copies:
            copy.start()
        for n in range(8):
            copies[n].wait()
            acc = jnp.zeros((32, 128), F32)
            for c in range(NC):
                left = b_ref[2 * c : 2 * c + 2, n].reshape(32, 256)
                acc = acc + dot_t(left, d_ref[c, n])
            x_ref[n] = acc
            half = acc.astype(BF16)
            for z in range(8):
                h_ref[z, n] = half

    return pl.pallas_call(
        kernel,
        in_specs=[VMEM, HBM],
        out_specs=[VMEM, VMEM],
        out_shape=[
            jax.ShapeDtypeStruct((8, 32, 128), F32),
            jax.ShapeDtypeStruct((8, 8, 32, 128), BF16),
        ],
        scratch_shapes=[
            pltpu.VMEM((NC, 8, 128, 256), BF16),
            pltpu.SemaphoreType.DMA((8,)),
        ],
        compiler_params=params(0, STREAM_LIMIT),
        name="solve_leaves",
    )(spread, inverse)


def update_from_leaves(meta, own, other, panels, right):
    def kernel(meta_ref, a_ref, b_ref, p_ref, r_ref, o_ref):
        core, row = meta_ref[1], meta_ref[2]
        for t in range(7):
            target = 8 + t
            if t < 4:
                sources = range(2 * t, 2 * t + 2)
            elif t < 6:
                sources = range(4 * (t - 4), 4 * (t - 4) + 4)
            else:
                sources = range(8)
            blocks = []
            for s in sources:
                slot, found = slot_of(meta_ref, s, target)
                block = p_ref[s, slot]
                blocks.append(jnp.where(found, block, jnp.zeros_like(block)))
            for parity, x_ref in ((core, a_ref), (1 - core, b_ref)):
                acc = jnp.zeros((256, 256), F32)
                for s, block in zip(sources, blocks, strict=True):
                    acc = acc + dot_t(x_ref[:, s].reshape(256, 128), block)
                for half in range(2):
                    value = acc[:, 128 * half : 128 * half + 128].astype(BF16)
                    o_ref[:, pl.ds(parity, 1), half, t] = value.reshape(8, 1, 32, 128)
        z, parity = row // 4, (row // 2) % 2
        start = pl.multiple_of(16 * (row % 2), 16)
        for half in range(2):
            for t in range(7):
                part = o_ref[z, parity, half, t, pl.ds(start, 16), :].astype(F32)
                part = part - r_ref[8 + t, :, 128 * half : 128 * half + 128]
                o_ref[z, parity, half, t, pl.ds(start, 16), :] = part.astype(BF16)

    return pl.pallas_call(
        kernel,
        grid=(1,),
        in_specs=[
            SMEM,
            VMEM,
            VMEM,
            pl.BlockSpec((8, 3, 256, 128), lambda i: (0, 0, 0, 0)),
            VMEM,
        ],
        out_specs=VMEM,
        out_shape=jax.ShapeDtypeStruct((8, 2, 2, 7, 32, 128), BF16),
        compiler_params=params(),
        name="update_from_leaves",
    )(meta, own, other, panels, right)


def first_residual(parts):
    def kernel(p_ref, o_ref):
        o_ref[...] = (-jnp.sum(p_ref[...].astype(F32), axis=0)).astype(BF16)

    return pl.pallas_call(
        kernel,
        in_specs=[VMEM],
        out_specs=VMEM,
        out_shape=jax.ShapeDtypeStruct((7, 32, 128), BF16),
        compiler_params=params(0),
        name="first_residual",
    )(parts)


def solve_node(x_ref, d_ref, n, place):
    acc = jnp.zeros((32, 128), F32)
    for c in range(NC):
        left = jnp.concatenate([x_ref[2 * c, n], x_ref[2 * c + 1, n]], axis=1)
        acc = acc + dot_t(left, d_ref[c, place])
    return acc


def update_above(solved, w_ref, c, nodes, targets, o_ref):
    for t, terms in enumerate(targets):
        for half in range(2):
            acc = jnp.zeros((32, 128), F32)
            for s, b in terms:
                block = w_ref[c, nodes + b, :, 128 * half : 128 * half + 128]
                acc = acc + dot_t(solved[s], block)
            o_ref[2 * c + half, t] = acc.astype(BF16)


def solve_level(residual, weights, nodes, targets):
    groups = 4

    def kernel(x_ref, w_hbm, s_ref, o_ref, w_ref, sem):
        pieces = [(slice(None), n) for n in range(nodes)]
        for g in range(groups):
            pieces.append((pl.ds(g * NC // groups, NC // groups), slice(nodes, None)))
        copies = [
            pltpu.make_async_copy(w_hbm.at[piece], w_ref.at[piece], sem.at[i])
            for i, piece in enumerate(pieces)
        ]
        for copy in copies:
            copy.start()
        solved = []
        for n in range(nodes):
            copies[n].wait()
            x = solve_node(x_ref, w_ref, n, n)
            s_ref[n] = x
            solved.append(x.astype(BF16))
        for g in range(groups):
            copies[nodes + g].wait()
            for c in range(g * NC // groups, (g + 1) * NC // groups):
                update_above(solved, w_ref, c, nodes, targets, o_ref)

    return pl.pallas_call(
        kernel,
        in_specs=[VMEM, HBM],
        out_specs=[VMEM, VMEM],
        out_shape=[
            jax.ShapeDtypeStruct((nodes, 32, 128), F32),
            jax.ShapeDtypeStruct((NR, len(targets), 32, 128), BF16),
        ],
        scratch_shapes=[
            pltpu.VMEM(weights.shape, BF16),
            pltpu.SemaphoreType.DMA((nodes + groups,)),
        ],
        compiler_params=params(0, STREAM_LIMIT),
        name="solve_level",
    )(residual, weights)


def solve_root(residual, inverse):
    def kernel(x_ref, d_ref, s_ref):
        s_ref[0] = solve_node(x_ref, d_ref, 0, 2)

    return pl.pallas_call(
        kernel,
        in_specs=[VMEM, VMEM],
        out_specs=VMEM,
        out_shape=jax.ShapeDtypeStruct((1, 32, 128), F32),
        compiler_params=params(0),
        name="solve_root",
    )(residual, inverse)


def next_residual(parts, rest, nodes):
    count = rest.shape[0]
    after = count - nodes

    def kernel(p_ref, rest_ref, o_ref, *later):
        residual = rest_ref[...].astype(F32) - jnp.sum(p_ref[...].astype(F32), axis=0)
        half = residual[:nodes].astype(BF16)
        for r in range(NR):
            o_ref[r] = half
        if after:
            later[0][...] = residual[nodes:]

    out_shape = [jax.ShapeDtypeStruct((NR, nodes, 32, 128), BF16)]
    if after:
        out_shape.append(jax.ShapeDtypeStruct((after, 32, 128), F32))
    return pl.pallas_call(
        kernel,
        in_specs=[VMEM, VMEM],
        out_specs=[VMEM] * len(out_shape),
        out_shape=out_shape,
        compiler_params=params(0),
        name="next_residual",
    )(parts, rest)


def exchange(values, axes):
    shape = values.shape
    flat = values.reshape(shape[0], -1, shape[-1])
    return lax.all_to_all(flat, axes, 0, 0, tiled=True).reshape(shape)


def spread_over(values, axes, size):
    return exchange(jnp.broadcast_to(values[None], (size,) + values.shape), axes)


def to_owner(values):
    pairs = [
        (r * NC + c, (2 * c + r % 2) * NC + r // 2) for r in range(NR) for c in range(NC)
    ]
    return lax.ppermute(values, ALL, pairs)


def per_device(right_sides, diag_inverse, panels, block_map):
    row = lax.axis_index(ROW)
    col = lax.axis_index(COL)
    core = lax.axis_index("core")
    leaf_inverse = lax.all_gather(diag_inverse[:8], COL, axis=0)
    moved = to_owner(right_sides[:8].astype(BF16))

    zero = jnp.zeros((), jnp.int32)
    meta = jnp.concatenate(
        [jnp.stack([col, core, row, zero]).astype(jnp.int32), block_map.reshape(-1)]
    )
    stack_two = stack_upper(meta, diag_inverse, panels, 8, 4, 0, 8)
    stack_one = stack_upper(meta, diag_inverse, panels, 12, 3, 8, 2)
    moved, stack_two, stack_one = lax.optimization_barrier((moved, stack_two, stack_one))
    spread = spread_over(moved, ROW, NR)

    leaves, copies = solve_leaves(spread, leaf_inverse)
    own = exchange(copies, "z")
    other = lax.ppermute(own, "core", [(0, 1), (1, 0)])
    stack_two, stack_one, own = lax.optimization_barrier((stack_two, stack_one, own))
    weights_two = lax.all_gather(stack_two, COL, axis=0)
    weights_one = lax.all_gather(stack_one, COL, axis=0)
    parts = update_from_leaves(meta, own, other, panels, right_sides)
    parts = exchange(parts.reshape(NR, 7, 32, 128), ROW)
    residual = to_owner(first_residual(parts))

    targets = [[(0, 0), (1, 2)], [(2, 4), (3, 6)], [(0, 1), (1, 3), (2, 5), (3, 7)]]
    spread = spread_over(residual[:4], ROW, NR)
    two, parts = solve_level(spread, weights_two, 4, targets)
    spread, rest = next_residual(exchange(parts, ROW), residual[4:], 2)
    targets = [[(0, 1), (1, 2)]]
    one, parts = solve_level(exchange(spread, ROW), weights_one, 2, targets)
    (spread,) = next_residual(exchange(parts, ROW), rest, 1)
    root = solve_root(exchange(spread, ROW), weights_one)
    return jnp.concatenate([leaves, two, one, root], axis=0)


def solution(mesh):
    split = Mesh(mesh.devices.reshape(4, 8, 8, 2), ALL)
    return jax.shard_map(
        per_device,
        mesh=split,
        in_specs=(P(None, ROW, COL), P(None, ROW, COL), P(None, None, COL, ROW), P()),
        out_specs=P(None, COL, ROW),
        check_vma=False,
    )
```

```python
import jax
import jax.numpy as jnp
from jax import lax
from jax.experimental import pallas as pl
from jax.experimental.pallas import tpu as pltpu
from jax.sharding import Mesh
from jax.sharding import PartitionSpec as P

ROW = ("x", "y")
COL = ("z", "core")
ALL = ("x", "y", "z", "core")
NR = 32
NC = 16
VMEM_LIMIT = 24 * 1024 * 1024
STREAM_LIMIT = 56 * 1024 * 1024
DEPTH = 3
F32 = jnp.float32
BF16 = jnp.bfloat16
VMEM = pl.BlockSpec(memory_space=pltpu.VMEM)
SMEM = pl.BlockSpec(memory_space=pltpu.SMEM)
HBM = pl.BlockSpec(memory_space=pltpu.HBM)


def params(n=1, limit=VMEM_LIMIT):
    return pltpu.CompilerParams(
        vmem_limit_bytes=limit, dimension_semantics=("arbitrary",) * n
    )


def dot_t(a, b):
    return lax.dot_general(a, b, (((1,), (1,)), ((), ())), preferred_element_type=F32)


def slot_of(meta, source, target):
    base = 4 + (source * NC + meta[0]) * 3
    second = jnp.where(meta[base + 1] == target, 1, 0)
    slot = jnp.where(meta[base + 2] == target, 2, second)
    return slot, meta[base + slot] == target


def gathered_block(b):
    is_low = b < 8
    source = jnp.where(is_low, 8 + b // 2, 4 + b)
    target = jnp.where(is_low & (b % 2 == 0), 12 + b // 4, 14)
    return source, target


def stack_upper(meta, inverse, panels, first_node, nodes, first_block, blocks):
    def kernel(meta_ref, d_ref, p_ref, o_ref):
        i = pl.program_id(0)

        @pl.when(i < nodes)
        def _():
            o_ref[...] = d_ref[...]

        @pl.when(i >= nodes)
        def _():
            _, found = slot_of(meta_ref, *gathered_block(first_block + i - nodes))
            block = p_ref[0, 0]
            block = jnp.where(found, block, jnp.zeros_like(block))
            o_ref[0, :, :128] = block[:128]
            o_ref[0, :, 128:] = block[128:]

    def index(i, meta_ref):
        source, target = gathered_block(first_block + jnp.maximum(i - nodes, 0))
        slot, _ = slot_of(meta_ref, source, target)
        return source, slot, 0, 0

    return pl.pallas_call(
        kernel,
        grid_spec=pltpu.PrefetchScalarGridSpec(
            num_scalar_prefetch=1,
            grid=(nodes + blocks,),
            in_specs=[
                pl.BlockSpec(
                    (1, 128, 256), lambda i, m: (first_node + jnp.minimum(i, nodes - 1), 0, 0)
                ),
                pl.BlockSpec((1, 1, 256, 128), index),
            ],
            out_specs=pl.BlockSpec((1, 128, 256), lambda i, m: (i, 0, 0)),
        ),
        out_shape=jax.ShapeDtypeStruct((nodes + blocks, 128, 256), BF16),
        compiler_params=params(),
        name="stack_upper",
    )(meta, inverse, panels)


def solve_leaves(spread, inverse):
    def kernel(b_ref, d_hbm, x_ref, h_ref, d_ref, sem):
        copies = [
            pltpu.make_async_copy(d_hbm.at[:, n], d_ref.at[:, n], sem.at[n]) for n in range(8)
        ]
        for copy in copies[:DEPTH]:
            copy.start()
        for n in range(8):
            copies[n].wait()
            if n + DEPTH < 8:
                copies[n + DEPTH].start()
            acc = jnp.zeros((32, 128), F32)
            for c in range(NC):
                left = b_ref[2 * c : 2 * c + 2, n].reshape(32, 256)
                acc = acc + dot_t(left, d_ref[c, n])
            x_ref[n] = acc
            half = acc.astype(BF16)
            for z in range(8):
                h_ref[z, n] = half

    return pl.pallas_call(
        kernel,
        in_specs=[VMEM, HBM],
        out_specs=[VMEM, VMEM],
        out_shape=[
            jax.ShapeDtypeStruct((8, 32, 128), F32),
            jax.ShapeDtypeStruct((8, 8, 32, 128), BF16),
        ],
        scratch_shapes=[
            pltpu.VMEM((NC, 8, 128, 256), BF16),
            pltpu.SemaphoreType.DMA((8,)),
        ],
        compiler_params=params(0, STREAM_LIMIT),
        name="solve_leaves",
    )(spread, inverse)


def update_from_leaves(meta, own, other, panels, right):
    def kernel(meta_ref, a_ref, b_ref, p_ref, r_ref, o_ref):
        core, row = meta_ref[1], meta_ref[2]
        for t in range(7):
            target = 8 + t
            if t < 4:
                sources = range(2 * t, 2 * t + 2)
            elif t < 6:
                sources = range(4 * (t - 4), 4 * (t - 4) + 4)
            else:
                sources = range(8)
            blocks = []
            for s in sources:
                slot, found = slot_of(meta_ref, s, target)
                block = p_ref[s, slot]
                blocks.append(jnp.where(found, block, jnp.zeros_like(block)))
            for parity, x_ref in ((core, a_ref), (1 - core, b_ref)):
                acc = jnp.zeros((256, 256), F32)
                for s, block in zip(sources, blocks, strict=True):
                    acc = acc + dot_t(x_ref[:, s].reshape(256, 128), block)
                for half in range(2):
                    value = acc[:, 128 * half : 128 * half + 128].astype(BF16)
                    o_ref[:, pl.ds(parity, 1), half, t] = value.reshape(8, 1, 32, 128)
        z, parity = row // 4, (row // 2) % 2
        start = pl.multiple_of(16 * (row % 2), 16)
        for half in range(2):
            for t in range(7):
                part = o_ref[z, parity, half, t, pl.ds(start, 16), :].astype(F32)
                part = part - r_ref[8 + t, :, 128 * half : 128 * half + 128]
                o_ref[z, parity, half, t, pl.ds(start, 16), :] = part.astype(BF16)

    return pl.pallas_call(
        kernel,
        grid=(1,),
        in_specs=[
            SMEM,
            VMEM,
            VMEM,
            pl.BlockSpec((8, 3, 256, 128), lambda i: (0, 0, 0, 0)),
            VMEM,
        ],
        out_specs=VMEM,
        out_shape=jax.ShapeDtypeStruct((8, 2, 2, 7, 32, 128), BF16),
        compiler_params=params(),
        name="update_from_leaves",
    )(meta, own, other, panels, right)


def first_residual(parts):
    def kernel(p_ref, o_ref):
        o_ref[...] = (-jnp.sum(p_ref[...].astype(F32), axis=0)).astype(BF16)

    return pl.pallas_call(
        kernel,
        in_specs=[VMEM],
        out_specs=VMEM,
        out_shape=jax.ShapeDtypeStruct((7, 32, 128), BF16),
        compiler_params=params(0),
        name="first_residual",
    )(parts)


def solve_node(x_ref, d_ref, n, place):
    acc = jnp.zeros((32, 128), F32)
    for c in range(NC):
        left = jnp.concatenate([x_ref[2 * c, n], x_ref[2 * c + 1, n]], axis=1)
        acc = acc + dot_t(left, d_ref[c, place])
    return acc


def update_above(solved, w_ref, c, nodes, targets, o_ref):
    for t, terms in enumerate(targets):
        for half in range(2):
            acc = jnp.zeros((32, 128), F32)
            for s, b in terms:
                block = w_ref[c, nodes + b, :, 128 * half : 128 * half + 128]
                acc = acc + dot_t(solved[s], block)
            o_ref[2 * c + half, t] = acc.astype(BF16)


def solve_level(residual, weights, nodes, targets):
    groups = 4

    def kernel(x_ref, w_hbm, s_ref, o_ref, w_ref, sem):
        pieces = [(slice(None), n) for n in range(nodes)]
        for g in range(groups):
            pieces.append((pl.ds(g * NC // groups, NC // groups), slice(nodes, None)))
        copies = [
            pltpu.make_async_copy(w_hbm.at[piece], w_ref.at[piece], sem.at[i])
            for i, piece in enumerate(pieces)
        ]
        for copy in copies[:DEPTH]:
            copy.start()

        def arrived(i):
            copies[i].wait()
            if i + DEPTH < len(copies):
                copies[i + DEPTH].start()

        solved = []
        for n in range(nodes):
            arrived(n)
            x = solve_node(x_ref, w_ref, n, n)
            s_ref[n] = x
            solved.append(x.astype(BF16))
        for g in range(groups):
            arrived(nodes + g)
            for c in range(g * NC // groups, (g + 1) * NC // groups):
                update_above(solved, w_ref, c, nodes, targets, o_ref)

    return pl.pallas_call(
        kernel,
        in_specs=[VMEM, HBM],
        out_specs=[VMEM, VMEM],
        out_shape=[
            jax.ShapeDtypeStruct((nodes, 32, 128), F32),
            jax.ShapeDtypeStruct((NR, len(targets), 32, 128), BF16),
        ],
        scratch_shapes=[
            pltpu.VMEM(weights.shape, BF16),
            pltpu.SemaphoreType.DMA((nodes + groups,)),
        ],
        compiler_params=params(0, STREAM_LIMIT),
        name="solve_level",
    )(residual, weights)


def solve_root(residual, inverse):
    def kernel(x_ref, d_ref, s_ref):
        s_ref[0] = solve_node(x_ref, d_ref, 0, 2)

    return pl.pallas_call(
        kernel,
        in_specs=[VMEM, VMEM],
        out_specs=VMEM,
        out_shape=jax.ShapeDtypeStruct((1, 32, 128), F32),
        compiler_params=params(0),
        name="solve_root",
    )(residual, inverse)


def next_residual(parts, rest, nodes):
    count = rest.shape[0]
    after = count - nodes

    def kernel(p_ref, rest_ref, o_ref, *later):
        residual = rest_ref[...].astype(F32) - jnp.sum(p_ref[...].astype(F32), axis=0)
        half = residual[:nodes].astype(BF16)
        for r in range(NR):
            o_ref[r] = half
        if after:
            later[0][...] = residual[nodes:]

    out_shape = [jax.ShapeDtypeStruct((NR, nodes, 32, 128), BF16)]
    if after:
        out_shape.append(jax.ShapeDtypeStruct((after, 32, 128), F32))
    return pl.pallas_call(
        kernel,
        in_specs=[VMEM, VMEM],
        out_specs=[VMEM] * len(out_shape),
        out_shape=out_shape,
        compiler_params=params(0),
        name="next_residual",
    )(parts, rest)


def exchange(values, axes):
    shape = values.shape
    flat = values.reshape(shape[0], -1, shape[-1])
    return lax.all_to_all(flat, axes, 0, 0, tiled=True).reshape(shape)


def spread_over(values, axes, size):
    return exchange(jnp.broadcast_to(values[None], (size,) + values.shape), axes)


def to_owner(values):
    pairs = [
        (r * NC + c, (2 * c + r % 2) * NC + r // 2) for r in range(NR) for c in range(NC)
    ]
    return lax.ppermute(values, ALL, pairs)


def per_device(right_sides, diag_inverse, panels, block_map):
    row = lax.axis_index(ROW)
    col = lax.axis_index(COL)
    core = lax.axis_index("core")
    leaf_right, diag_inverse = lax.optimization_barrier(
        (right_sides[:8].astype(BF16), diag_inverse)
    )
    moved = to_owner(leaf_right)
    leaf_inverse = lax.all_gather(diag_inverse[:8], COL, axis=0)

    zero = jnp.zeros((), jnp.int32)
    meta = jnp.concatenate(
        [jnp.stack([col, core, row, zero]).astype(jnp.int32), block_map.reshape(-1)]
    )
    stack_two = stack_upper(meta, diag_inverse, panels, 8, 4, 0, 8)
    stack_one = stack_upper(meta, diag_inverse, panels, 12, 3, 8, 2)
    spread = spread_over(moved, ROW, NR)
    spread, stack_two, stack_one = lax.optimization_barrier((spread, stack_two, stack_one))

    leaves, copies = solve_leaves(spread, leaf_inverse)
    own = exchange(copies, "z")
    other = lax.ppermute(own, "core", [(0, 1), (1, 0)])
    stack_two, stack_one, own = lax.optimization_barrier((stack_two, stack_one, own))
    weights_two = lax.all_gather(stack_two, COL, axis=0)
    weights_one = lax.all_gather(stack_one, COL, axis=0)
    parts = update_from_leaves(meta, own, other, panels, right_sides)
    parts = exchange(parts.reshape(NR, 7, 32, 128), ROW)
    residual = to_owner(first_residual(parts))

    targets = [[(0, 0), (1, 2)], [(2, 4), (3, 6)], [(0, 1), (1, 3), (2, 5), (3, 7)]]
    spread = spread_over(residual[:4], ROW, NR)
    two, parts = solve_level(spread, weights_two, 4, targets)
    spread, rest = next_residual(exchange(parts, ROW), residual[4:], 2)
    targets = [[(0, 1), (1, 2)]]
    one, parts = solve_level(exchange(spread, ROW), weights_one, 2, targets)
    (spread,) = next_residual(exchange(parts, ROW), rest, 1)
    root = solve_root(exchange(spread, ROW), weights_one)
    return jnp.concatenate([leaves, two, one, root], axis=0)


def solution(mesh):
    split = Mesh(mesh.devices.reshape(4, 8, 8, 2), ALL)
    return jax.shard_map(
        per_device,
        mesh=split,
        in_specs=(P(None, ROW, COL), P(None, ROW, COL), P(None, None, COL, ROW), P()),
        out_specs=P(None, COL, ROW),
        check_vma=False,
    )
```

```python
import jax
import jax.numpy as jnp
from jax import lax
from jax.experimental import pallas as pl
from jax.experimental.pallas import tpu as pltpu
from jax.sharding import Mesh
from jax.sharding import PartitionSpec as P

ROW = ("x", "y")
COL = ("z", "core")
ALL = ("x", "y", "z", "core")
NR = 32
NC = 16
VMEM_LIMIT = 24 * 1024 * 1024
STREAM_LIMIT = 56 * 1024 * 1024
F32 = jnp.float32
BF16 = jnp.bfloat16
VMEM = pl.BlockSpec(memory_space=pltpu.VMEM)
SMEM = pl.BlockSpec(memory_space=pltpu.SMEM)
HBM = pl.BlockSpec(memory_space=pltpu.HBM)


def params(n=1, limit=VMEM_LIMIT):
    return pltpu.CompilerParams(
        vmem_limit_bytes=limit, dimension_semantics=("arbitrary",) * n
    )


def dot_t(a, b):
    return lax.dot_general(a, b, (((1,), (1,)), ((), ())), preferred_element_type=F32)


def slot_of(meta, source, target):
    base = 4 + (source * NC + meta[0]) * 3
    second = jnp.where(meta[base + 1] == target, 1, 0)
    slot = jnp.where(meta[base + 2] == target, 2, second)
    return slot, meta[base + slot] == target


def gathered_block(b):
    is_low = b < 8
    source = jnp.where(is_low, 8 + b // 2, 4 + b)
    target = jnp.where(is_low & (b % 2 == 0), 12 + b // 4, 14)
    return source, target


def stack_upper(meta, inverse, panels, first_node, nodes, first_block, blocks):
    def kernel(meta_ref, d_ref, p_ref, o_ref):
        i = pl.program_id(0)

        @pl.when(i < nodes)
        def _():
            o_ref[...] = d_ref[...]

        @pl.when(i >= nodes)
        def _():
            _, found = slot_of(meta_ref, *gathered_block(first_block + i - nodes))
            block = p_ref[0, 0]
            block = jnp.where(found, block, jnp.zeros_like(block))
            o_ref[0, :, :128] = block[:128]
            o_ref[0, :, 128:] = block[128:]

    def index(i, meta_ref):
        source, target = gathered_block(first_block + jnp.maximum(i - nodes, 0))
        slot, _ = slot_of(meta_ref, source, target)
        return source, slot, 0, 0

    return pl.pallas_call(
        kernel,
        grid_spec=pltpu.PrefetchScalarGridSpec(
            num_scalar_prefetch=1,
            grid=(nodes + blocks,),
            in_specs=[
                pl.BlockSpec(
                    (1, 128, 256), lambda i, m: (first_node + jnp.minimum(i, nodes - 1), 0, 0)
                ),
                pl.BlockSpec((1, 1, 256, 128), index),
            ],
            out_specs=pl.BlockSpec((1, 128, 256), lambda i, m: (i, 0, 0)),
        ),
        out_shape=jax.ShapeDtypeStruct((nodes + blocks, 128, 256), BF16),
        compiler_params=params(),
        name="stack_upper",
    )(meta, inverse, panels)


def solve_leaves(spread, inverse):
    def kernel(b_ref, d_hbm, x_ref, h_ref, d_ref, sem):
        copies = [pltpu.make_async_copy(d_hbm.at[c], d_ref.at[c], sem.at[c]) for c in range(NC)]
        for copy in copies:
            copy.start()
        for c in range(NC):
            copies[c].wait()
            for n in range(8):
                left = b_ref[2 * c : 2 * c + 2, n].reshape(32, 256)
                value = dot_t(left, d_ref[c, n])
                if c:
                    value = value + x_ref[n]
                x_ref[n] = value
        for n in range(8):
            half = x_ref[n].astype(BF16)
            for z in range(8):
                h_ref[z, n] = half

    return pl.pallas_call(
        kernel,
        in_specs=[VMEM, HBM],
        out_specs=[VMEM, VMEM],
        out_shape=[
            jax.ShapeDtypeStruct((8, 32, 128), F32),
            jax.ShapeDtypeStruct((8, 8, 32, 128), BF16),
        ],
        scratch_shapes=[
            pltpu.VMEM((NC, 8, 128, 256), BF16),
            pltpu.SemaphoreType.DMA((NC,)),
        ],
        compiler_params=params(0, STREAM_LIMIT),
        name="solve_leaves",
    )(spread, inverse)


def update_from_leaves(meta, own, other, panels, right):
    def kernel(meta_ref, a_ref, b_ref, p_ref, r_ref, o_ref):
        core, row = meta_ref[1], meta_ref[2]
        for t in range(7):
            target = 8 + t
            if t < 4:
                sources = range(2 * t, 2 * t + 2)
            elif t < 6:
                sources = range(4 * (t - 4), 4 * (t - 4) + 4)
            else:
                sources = range(8)
            blocks = []
            for s in sources:
                slot, found = slot_of(meta_ref, s, target)
                block = p_ref[s, slot]
                blocks.append(jnp.where(found, block, jnp.zeros_like(block)))
            for parity, x_ref in ((core, a_ref), (1 - core, b_ref)):
                acc = jnp.zeros((256, 256), F32)
                for s, block in zip(sources, blocks, strict=True):
                    acc = acc + dot_t(x_ref[:, s].reshape(256, 128), block)
                for half in range(2):
                    value = acc[:, 128 * half : 128 * half + 128].astype(BF16)
                    o_ref[:, pl.ds(parity, 1), half, t] = value.reshape(8, 1, 32, 128)
        z, parity = row // 4, (row // 2) % 2
        start = pl.multiple_of(16 * (row % 2), 16)
        for half in range(2):
            for t in range(7):
                part = o_ref[z, parity, half, t, pl.ds(start, 16), :].astype(F32)
                part = part - r_ref[8 + t, :, 128 * half : 128 * half + 128]
                o_ref[z, parity, half, t, pl.ds(start, 16), :] = part.astype(BF16)

    return pl.pallas_call(
        kernel,
        grid=(1,),
        in_specs=[
            SMEM,
            VMEM,
            VMEM,
            pl.BlockSpec((8, 3, 256, 128), lambda i: (0, 0, 0, 0)),
            VMEM,
        ],
        out_specs=VMEM,
        out_shape=jax.ShapeDtypeStruct((8, 2, 2, 7, 32, 128), BF16),
        compiler_params=params(),
        name="update_from_leaves",
    )(meta, own, other, panels, right)


def first_residual(parts):
    def kernel(p_ref, o_ref):
        o_ref[...] = (-jnp.sum(p_ref[...].astype(F32), axis=0)).astype(BF16)

    return pl.pallas_call(
        kernel,
        in_specs=[VMEM],
        out_specs=VMEM,
        out_shape=jax.ShapeDtypeStruct((7, 32, 128), BF16),
        compiler_params=params(0),
        name="first_residual",
    )(parts)


def solve_node(x_ref, d_ref, n, place):
    acc = jnp.zeros((32, 128), F32)
    for c in range(NC):
        left = jnp.concatenate([x_ref[2 * c, n], x_ref[2 * c + 1, n]], axis=1)
        acc = acc + dot_t(left, d_ref[c, place])
    return acc


def update_above(solved, w_ref, c, nodes, targets, o_ref):
    for t, terms in enumerate(targets):
        for half in range(2):
            acc = jnp.zeros((32, 128), F32)
            for s, b in terms:
                block = w_ref[c, nodes + b, :, 128 * half : 128 * half + 128]
                acc = acc + dot_t(solved[s], block)
            o_ref[2 * c + half, t] = acc.astype(BF16)


def solve_level(residual, weights, nodes, targets):
    used = nodes + min(b for terms in targets for _, b in terms)

    def kernel(x_ref, w_hbm, s_ref, o_ref, w_ref, sem):
        pieces = [(c, slice(0, nodes)) for c in range(NC)]
        pieces += [(c, slice(used, None)) for c in range(NC)]
        copies = [
            pltpu.make_async_copy(w_hbm.at[piece], w_ref.at[piece], sem.at[i])
            for i, piece in enumerate(pieces)
        ]
        for copy in copies:
            copy.start()
        for c in range(NC):
            copies[c].wait()
            for n in range(nodes):
                left = jnp.concatenate([x_ref[2 * c, n], x_ref[2 * c + 1, n]], axis=1)
                value = dot_t(left, w_ref[c, n])
                if c:
                    value = value + s_ref[n]
                s_ref[n] = value
        solved = [s_ref[n].astype(BF16) for n in range(nodes)]
        for c in range(NC):
            copies[NC + c].wait()
            update_above(solved, w_ref, c, nodes, targets, o_ref)

    return pl.pallas_call(
        kernel,
        in_specs=[VMEM, HBM],
        out_specs=[VMEM, VMEM],
        out_shape=[
            jax.ShapeDtypeStruct((nodes, 32, 128), F32),
            jax.ShapeDtypeStruct((NR, len(targets), 32, 128), BF16),
        ],
        scratch_shapes=[
            pltpu.VMEM(weights.shape, BF16),
            pltpu.SemaphoreType.DMA((2 * NC,)),
        ],
        compiler_params=params(0, STREAM_LIMIT),
        name="solve_level",
    )(residual, weights)


def solve_root(residual, inverse):
    def kernel(x_ref, d_ref, s_ref):
        s_ref[0] = solve_node(x_ref, d_ref, 0, 2)

    return pl.pallas_call(
        kernel,
        in_specs=[VMEM, VMEM],
        out_specs=VMEM,
        out_shape=jax.ShapeDtypeStruct((1, 32, 128), F32),
        compiler_params=params(0),
        name="solve_root",
    )(residual, inverse)


def next_residual(parts, rest, nodes):
    count = rest.shape[0]
    after = count - nodes

    def kernel(p_ref, rest_ref, o_ref, *later):
        residual = rest_ref[...].astype(F32) - jnp.sum(p_ref[...].astype(F32), axis=0)
        half = residual[:nodes].astype(BF16)
        for r in range(NR):
            o_ref[r] = half
        if after:
            later[0][...] = residual[nodes:]

    out_shape = [jax.ShapeDtypeStruct((NR, nodes, 32, 128), BF16)]
    if after:
        out_shape.append(jax.ShapeDtypeStruct((after, 32, 128), F32))
    return pl.pallas_call(
        kernel,
        in_specs=[VMEM, VMEM],
        out_specs=[VMEM] * len(out_shape),
        out_shape=out_shape,
        compiler_params=params(0),
        name="next_residual",
    )(parts, rest)


def exchange(values, axes):
    shape = values.shape
    flat = values.reshape(shape[0], -1, shape[-1])
    return lax.all_to_all(flat, axes, 0, 0, tiled=True).reshape(shape)


def spread_over(values, axes, size):
    return exchange(jnp.broadcast_to(values[None], (size,) + values.shape), axes)


def to_owner(values):
    pairs = [
        (r * NC + c, (2 * c + r % 2) * NC + r // 2) for r in range(NR) for c in range(NC)
    ]
    return lax.ppermute(values, ALL, pairs)


def per_device(right_sides, diag_inverse, panels, block_map):
    row = lax.axis_index(ROW)
    col = lax.axis_index(COL)
    core = lax.axis_index("core")
    leaf_right, diag_inverse = lax.optimization_barrier(
        (right_sides[:8].astype(BF16), diag_inverse)
    )
    moved = to_owner(leaf_right)
    leaf_inverse = lax.all_gather(diag_inverse[:8], COL, axis=0)

    zero = jnp.zeros((), jnp.int32)
    meta = jnp.concatenate(
        [jnp.stack([col, core, row, zero]).astype(jnp.int32), block_map.reshape(-1)]
    )
    stack_two = stack_upper(meta, diag_inverse, panels, 8, 4, 0, 8)
    stack_one = stack_upper(meta, diag_inverse, panels, 12, 3, 8, 2)
    spread = spread_over(moved, ROW, NR)
    spread, stack_two, stack_one = lax.optimization_barrier((spread, stack_two, stack_one))

    leaves, copies = solve_leaves(spread, leaf_inverse)
    own = exchange(copies, "z")
    other = lax.ppermute(own, "core", [(0, 1), (1, 0)])
    stack_two, stack_one, own = lax.optimization_barrier((stack_two, stack_one, own))
    weights_two = lax.all_gather(stack_two, COL, axis=0)
    weights_one = lax.all_gather(stack_one, COL, axis=0)
    parts = update_from_leaves(meta, own, other, panels, right_sides)
    parts = exchange(parts.reshape(NR, 7, 32, 128), ROW)
    residual = to_owner(first_residual(parts))

    targets = [[(0, 0), (1, 2)], [(2, 4), (3, 6)], [(0, 1), (1, 3), (2, 5), (3, 7)]]
    spread = spread_over(residual[:4], ROW, NR)
    two, parts = solve_level(spread, weights_two, 4, targets)
    spread, rest = next_residual(exchange(parts, ROW), residual[4:], 2)
    targets = [[(0, 1), (1, 2)]]
    one, parts = solve_level(exchange(spread, ROW), weights_one, 2, targets)
    (spread,) = next_residual(exchange(parts, ROW), rest, 1)
    root = solve_root(exchange(spread, ROW), weights_one)
    return jnp.concatenate([leaves, two, one, root], axis=0)


def solution(mesh):
    split = Mesh(mesh.devices.reshape(4, 8, 8, 2), ALL)
    return jax.shard_map(
        per_device,
        mesh=split,
        in_specs=(P(None, ROW, COL), P(None, ROW, COL), P(None, None, COL, ROW), P()),
        out_specs=P(None, COL, ROW),
        check_vma=False,
    )
```

```python
import jax
import jax.numpy as jnp
from jax import lax
from jax.experimental import pallas as pl
from jax.experimental.pallas import tpu as pltpu
from jax.sharding import Mesh
from jax.sharding import PartitionSpec as P

ROW = ("x", "y")
COL = ("z", "core")
ALL = ("x", "y", "z", "core")
NR = 32
NC = 16
VMEM_LIMIT = 24 * 1024 * 1024
STREAM_LIMIT = 56 * 1024 * 1024
F32 = jnp.float32
BF16 = jnp.bfloat16
VMEM = pl.BlockSpec(memory_space=pltpu.VMEM)
SMEM = pl.BlockSpec(memory_space=pltpu.SMEM)
HBM = pl.BlockSpec(memory_space=pltpu.HBM)


def params(n=1, limit=VMEM_LIMIT):
    return pltpu.CompilerParams(
        vmem_limit_bytes=limit, dimension_semantics=("arbitrary",) * n
    )


def dot_t(a, b):
    return lax.dot_general(a, b, (((1,), (1,)), ((), ())), preferred_element_type=F32)


def slot_of(meta, source, target):
    base = 4 + (source * NC + meta[0]) * 3
    second = jnp.where(meta[base + 1] == target, 1, 0)
    slot = jnp.where(meta[base + 2] == target, 2, second)
    return slot, meta[base + slot] == target


def selected(meta_ref, p_ref, source, target):
    slot, found = slot_of(meta_ref, source, target)
    block = p_ref[source, slot]
    return jnp.where(found, block, jnp.zeros_like(block))


MIRRORED_UPPER = [(9, 12), (9, 14), (11, 13), (11, 14), (13, 14)]
MIRRORED_LEAF = [(2, 9), (3, 9), (6, 11), (7, 11), (4, 13), (5, 13), (6, 13), (7, 13)]


def mirrored_weights(meta, inverse, panels):
    def kernel(meta_ref, d_ref, p_ref, upper_ref, leaf_ref):
        for i in range(3):
            upper_ref[i] = d_ref[9 + 2 * i]
        for i, (source, target) in enumerate(MIRRORED_UPPER):
            block = selected(meta_ref, p_ref, source, target)
            upper_ref[3 + i, :, :128] = block[:128]
            upper_ref[3 + i, :, 128:] = block[128:]
        for i, (source, target) in enumerate(MIRRORED_LEAF):
            leaf_ref[i] = selected(meta_ref, p_ref, source, target)

    return pl.pallas_call(
        kernel,
        in_specs=[SMEM, VMEM, VMEM],
        out_specs=[VMEM, VMEM],
        out_shape=[
            jax.ShapeDtypeStruct((8, 128, 256), BF16),
            jax.ShapeDtypeStruct((8, 256, 128), BF16),
        ],
        compiler_params=params(0),
        name="mirrored_weights",
    )(meta, inverse, panels)


def stack_weights(meta, inverse, panels, got):
    def kernel(meta_ref, d_ref, p_ref, g_ref, two_ref, one_ref):
        def join(out_ref, place, source, target, index):
            block = selected(meta_ref, p_ref, source, target)
            for half in range(2):
                rows = slice(128 * half, 128 * half + 128)
                out_ref[place + half, :, :128] = block[rows]
                out_ref[place + half, :, 128:] = g_ref[index, :, rows]

        two_ref[0] = d_ref[8]
        two_ref[1] = d_ref[10]
        two_ref[2] = g_ref[0]
        two_ref[3] = g_ref[1]
        join(two_ref, 4, 8, 12, 3)
        join(two_ref, 6, 10, 13, 5)
        join(two_ref, 8, 8, 14, 4)
        join(two_ref, 10, 10, 14, 6)
        one_ref[0] = d_ref[12]
        one_ref[1] = g_ref[2]
        one_ref[2] = d_ref[14]
        join(one_ref, 3, 12, 14, 7)

    return pl.pallas_call(
        kernel,
        in_specs=[SMEM, VMEM, VMEM, VMEM],
        out_specs=[VMEM, VMEM],
        out_shape=[
            jax.ShapeDtypeStruct((12, 128, 256), BF16),
            jax.ShapeDtypeStruct((5, 128, 256), BF16),
        ],
        compiler_params=params(0),
        name="stack_weights",
    )(meta, inverse, panels, got)


def solve_leaves(spread, inverse):
    def kernel(b_ref, d_hbm, x_ref, h_ref, d_ref, sem):
        copies = [pltpu.make_async_copy(d_hbm.at[c], d_ref.at[c], sem.at[c]) for c in range(NC)]
        for copy in copies:
            copy.start()
        for c in range(NC):
            copies[c].wait()
            for n in range(8):
                left = b_ref[2 * c : 2 * c + 2, n].reshape(32, 256)
                value = dot_t(left, d_ref[c, n])
                if c:
                    value = value + x_ref[n]
                x_ref[n] = value
        for n in range(8):
            half = x_ref[n].astype(BF16)
            for z in range(8):
                h_ref[z, n] = half

    return pl.pallas_call(
        kernel,
        in_specs=[VMEM, HBM],
        out_specs=[VMEM, VMEM],
        out_shape=[
            jax.ShapeDtypeStruct((8, 32, 128), F32),
            jax.ShapeDtypeStruct((8, 8, 32, 128), BF16),
        ],
        scratch_shapes=[
            pltpu.VMEM((NC, 8, 128, 256), BF16),
            pltpu.SemaphoreType.DMA((NC,)),
        ],
        compiler_params=params(0, STREAM_LIMIT),
        name="solve_leaves",
    )(spread, inverse)


def update_from_leaves(meta, own, other, panels, leaf_got, right, right_got):
    def kernel(meta_ref, a_ref, b_ref, p_ref, g_ref, r_ref, rg_ref, o_ref):
        core, row = meta_ref[1], meta_ref[2]
        for t in range(7):
            target = 8 + t
            if t < 4:
                sources = range(2 * t, 2 * t + 2)
            elif t < 6:
                sources = range(4 * (t - 4), 4 * (t - 4) + 4)
            else:
                sources = range(8)
            if t in (1, 3, 5):
                blocks = [g_ref[MIRRORED_LEAF.index((s, target))] for s in sources]
            else:
                blocks = [selected(meta_ref, p_ref, s, target) for s in sources]
            for parity, x_ref in ((core, a_ref), (1 - core, b_ref)):
                acc = jnp.zeros((256, 256), F32)
                for s, block in zip(sources, blocks, strict=True):
                    acc = acc + dot_t(x_ref[:, s].reshape(256, 128), block)
                for half in range(2):
                    side = 1 - half if t in (1, 3, 5) else half
                    value = acc[:, 128 * side : 128 * side + 128].astype(BF16)
                    o_ref[:, pl.ds(parity, 1), half, t] = value.reshape(8, 1, 32, 128)
        z, parity = row // 4, (row // 2) % 2
        start = pl.multiple_of(16 * (row % 2), 16)
        for half in range(2):
            for t in range(7):
                part = o_ref[z, parity, half, t, pl.ds(start, 16), :].astype(F32)
                if t in (1, 3, 5):
                    held = rg_ref[t // 2, :, 128 * (1 - half) : 128 * (1 - half) + 128]
                else:
                    held = r_ref[8 + t, :, 128 * half : 128 * half + 128]
                o_ref[z, parity, half, t, pl.ds(start, 16), :] = (part - held).astype(BF16)

    return pl.pallas_call(
        kernel,
        grid=(1,),
        in_specs=[
            SMEM,
            VMEM,
            VMEM,
            pl.BlockSpec((8, 3, 256, 128), lambda i: (0, 0, 0, 0)),
            VMEM,
            VMEM,
            VMEM,
        ],
        out_specs=VMEM,
        out_shape=jax.ShapeDtypeStruct((8, 2, 2, 7, 32, 128), BF16),
        compiler_params=params(),
        name="update_from_leaves",
    )(meta, own, other, panels, leaf_got, right, right_got)


def first_residual(parts):
    def kernel(p_ref, o_ref):
        o_ref[...] = (-jnp.sum(p_ref[...].astype(F32), axis=0)).astype(BF16)

    return pl.pallas_call(
        kernel,
        in_specs=[VMEM],
        out_specs=VMEM,
        out_shape=jax.ShapeDtypeStruct((7, 32, 128), BF16),
        compiler_params=params(0),
        name="first_residual",
    )(parts)


def first_payload(meta, residual):
    def kernel(meta_ref, x_ref, o_ref):
        row = meta_ref[2]
        for r in range(NR):
            for p in range(2):
                o_ref[r, p] = jnp.where(row <= r, x_ref[2 * p], x_ref[2 * p + 1])

    return pl.pallas_call(
        kernel,
        in_specs=[SMEM, VMEM],
        out_specs=VMEM,
        out_shape=jax.ShapeDtypeStruct((NR, 2, 32, 128), BF16),
        compiler_params=params(0),
        name="first_payload",
    )(meta, residual)


def solve_level(meta, spread, local, places, weights, targets):
    pairs = len(places)
    used = min(b for terms, _ in targets for _, b in terms)

    def kernel(meta_ref, x_ref, y_ref, w_hbm, natural_ref, mirrored_ref, o_ref, w_ref, sem):
        row = meta_ref[2]
        pieces = [(c, slice(0, 2 * pairs)) for c in range(NC)]
        pieces += [(c, slice(used, None)) for c in range(NC)]
        copies = [
            pltpu.make_async_copy(w_hbm.at[piece], w_ref.at[piece], sem.at[i])
            for i, piece in enumerate(pieces)
        ]
        for copy in copies:
            copy.start()

        def mirrored_block(b, p):
            return jnp.where(row == b, y_ref[places[p]], x_ref[b, p])

        for c in range(NC):
            copies[c].wait()
            for p in range(pairs):
                left = jnp.concatenate([x_ref[2 * c, p], x_ref[2 * c + 1, p]], axis=1)
                value = dot_t(left, w_ref[c, p])
                left = jnp.concatenate(
                    [mirrored_block(31 - 2 * c, p), mirrored_block(30 - 2 * c, p)], axis=1
                )
                other = dot_t(left, w_ref[c, pairs + p])
                if c:
                    value = value + natural_ref[p]
                    other = other + mirrored_ref[p]
                natural_ref[p] = value
                mirrored_ref[p] = other
        joined = [
            jnp.concatenate([natural_ref[p].astype(BF16), mirrored_ref[p].astype(BF16)], axis=1)
            for p in range(pairs)
        ]
        for c in range(NC):
            copies[NC + c].wait()
            for t, (terms, flipped) in enumerate(targets):
                for half in range(2):
                    total = jnp.zeros((32, 128), F32)
                    for p, b in terms:
                        total = total + dot_t(joined[p], w_ref[c, b + half])
                    r = 2 * c + half
                    o_ref[31 - r if flipped else r, t] = total.astype(BF16)

    return pl.pallas_call(
        kernel,
        in_specs=[SMEM, VMEM, VMEM, HBM],
        out_specs=[VMEM, VMEM, VMEM],
        out_shape=[
            jax.ShapeDtypeStruct((pairs, 32, 128), F32),
            jax.ShapeDtypeStruct((pairs, 32, 128), F32),
            jax.ShapeDtypeStruct((NR, len(targets), 32, 128), BF16),
        ],
        scratch_shapes=[
            pltpu.VMEM(weights.shape, BF16),
            pltpu.SemaphoreType.DMA((2 * NC,)),
        ],
        compiler_params=params(0, STREAM_LIMIT),
        name="solve_level",
    )(meta, spread, local, weights)


def solve_node(x_ref, d_ref, n, place):
    acc = jnp.zeros((32, 128), F32)
    for c in range(NC):
        left = jnp.concatenate([x_ref[2 * c, n], x_ref[2 * c + 1, n]], axis=1)
        acc = acc + dot_t(left, d_ref[c, place])
    return acc


def solve_root(residual, inverse):
    def kernel(x_ref, d_ref, s_ref):
        s_ref[0] = solve_node(x_ref, d_ref, 0, 2)

    return pl.pallas_call(
        kernel,
        in_specs=[VMEM, VMEM],
        out_specs=VMEM,
        out_shape=jax.ShapeDtypeStruct((1, 32, 128), F32),
        compiler_params=params(0),
        name="solve_root",
    )(residual, inverse)


def next_residual(meta, parts, residual):
    def kernel(meta_ref, p_ref, x_ref, o_ref, local_ref, rest_ref):
        row = meta_ref[2]
        total = x_ref[4:].astype(F32) - jnp.sum(p_ref[...].astype(F32), axis=0)
        natural, mirrored = total[0].astype(BF16), total[1].astype(BF16)
        for r in range(NR):
            o_ref[r, 0] = jnp.where(row <= r, natural, mirrored)
        local_ref[0] = mirrored
        rest_ref[0] = total[2]

    return pl.pallas_call(
        kernel,
        in_specs=[SMEM, VMEM, VMEM],
        out_specs=[VMEM, VMEM, VMEM],
        out_shape=[
            jax.ShapeDtypeStruct((NR, 1, 32, 128), BF16),
            jax.ShapeDtypeStruct((1, 32, 128), BF16),
            jax.ShapeDtypeStruct((1, 32, 128), F32),
        ],
        compiler_params=params(0),
        name="next_residual",
    )(meta, parts, residual)


def last_residual(parts, rest):
    def kernel(p_ref, rest_ref, o_ref):
        half = (rest_ref[...] - jnp.sum(p_ref[...].astype(F32), axis=0)).astype(BF16)
        for r in range(NR):
            o_ref[r] = half

    return pl.pallas_call(
        kernel,
        in_specs=[VMEM, VMEM],
        out_specs=VMEM,
        out_shape=jax.ShapeDtypeStruct((NR, 1, 32, 128), BF16),
        compiler_params=params(0),
        name="last_residual",
    )(parts, rest)


def exchange(values, axes):
    shape = values.shape
    flat = values.reshape(shape[0], -1, shape[-1])
    return lax.all_to_all(flat, axes, 0, 0, tiled=True).reshape(shape)


def spread_over(values, axes, size):
    return exchange(jnp.broadcast_to(values[None], (size,) + values.shape), axes)


def to_owner(values):
    pairs = [
        (r * NC + c, (2 * c + r % 2) * NC + r // 2) for r in range(NR) for c in range(NC)
    ]
    return lax.ppermute(values, ALL, pairs)


def to_mirrored_row(values):
    pairs = [(r * NC + c, (31 - r) * NC + c) for r in range(NR) for c in range(NC)]
    return lax.ppermute(values, ALL, pairs)


def to_mirrored_column(values):
    pairs = [(r * NC + c, r * NC + 15 - c) for r in range(NR) for c in range(NC)]
    return lax.ppermute(values, ALL, pairs)


def per_device(right_sides, diag_inverse, panels, block_map):
    row = lax.axis_index(ROW)
    col = lax.axis_index(COL)
    core = lax.axis_index("core")
    leaf_right, diag_inverse = lax.optimization_barrier(
        (right_sides[:8].astype(BF16), diag_inverse)
    )
    moved = to_owner(leaf_right)
    leaf_inverse = lax.all_gather(diag_inverse[:8], COL, axis=0)

    zero = jnp.zeros((), jnp.int32)
    meta = jnp.concatenate(
        [jnp.stack([col, core, row, zero]).astype(jnp.int32), block_map.reshape(-1)]
    )
    upper_sent, leaf_sent = mirrored_weights(meta, diag_inverse, panels)
    leaf_got = to_mirrored_column(leaf_sent)
    right_got = to_mirrored_column(right_sides[9:14:2])
    stack_two, stack_one = stack_weights(
        meta, diag_inverse, panels, to_mirrored_row(upper_sent)
    )
    spread = spread_over(moved, ROW, NR)
    spread, stack_two, stack_one, leaf_got, right_got = lax.optimization_barrier(
        (spread, stack_two, stack_one, leaf_got, right_got)
    )

    leaves, copies = solve_leaves(spread, leaf_inverse)
    own = exchange(copies, "z")
    other = lax.ppermute(own, "core", [(0, 1), (1, 0)])
    stack_two, stack_one, own = lax.optimization_barrier((stack_two, stack_one, own))
    weights_two = lax.all_gather(stack_two, COL, axis=0)
    weights_one = lax.all_gather(stack_one, COL, axis=0)
    parts = update_from_leaves(meta, own, other, panels, leaf_got, right_sides, right_got)
    parts = exchange(parts.reshape(NR, 7, 32, 128), ROW)
    residual = to_owner(first_residual(parts))

    spread = exchange(first_payload(meta, residual), ROW)
    targets = [([(0, 4)], False), ([(1, 6)], True), ([(0, 8), (1, 10)], False)]
    two, two_mirrored, parts = solve_level(meta, spread, residual, [1, 3], weights_two, targets)
    spread, local, rest = next_residual(meta, exchange(parts, ROW), residual)
    spread = exchange(spread, ROW)
    one, one_mirrored, parts = solve_level(
        meta, spread, local, [0], weights_one, [([(0, 3)], False)]
    )
    back = to_mirrored_row(jnp.concatenate([two_mirrored, one_mirrored], axis=0))
    spread = last_residual(exchange(parts, ROW), rest)
    root = solve_root(exchange(spread, ROW), weights_one)
    upper = [two[:1], back[:1], two[1:], back[1:2], one, back[2:], root]
    return jnp.concatenate([leaves, *upper], axis=0)


def solution(mesh):
    split = Mesh(mesh.devices.reshape(4, 8, 8, 2), ALL)
    return jax.shard_map(
        per_device,
        mesh=split,
        in_specs=(P(None, ROW, COL), P(None, ROW, COL), P(None, None, COL, ROW), P()),
        out_specs=P(None, COL, ROW),
        check_vma=False,
    )
```

```python
import jax
import jax.numpy as jnp
from jax import lax
from jax.experimental import pallas as pl
from jax.experimental.pallas import tpu as pltpu
from jax.sharding import Mesh
from jax.sharding import PartitionSpec as P

ROW = ("x", "y")
COL = ("z", "core")
ALL = ("x", "y", "z", "core")
NR = 32
NC = 16
VMEM_LIMIT = 24 * 1024 * 1024
STREAM_LIMIT = 56 * 1024 * 1024
F32 = jnp.float32
BF16 = jnp.bfloat16
VMEM = pl.BlockSpec(memory_space=pltpu.VMEM)
SMEM = pl.BlockSpec(memory_space=pltpu.SMEM)
HBM = pl.BlockSpec(memory_space=pltpu.HBM)


def params(n=1, limit=VMEM_LIMIT):
    return pltpu.CompilerParams(
        vmem_limit_bytes=limit, dimension_semantics=("arbitrary",) * n
    )


def dot_t(a, b):
    return lax.dot_general(a, b, (((1,), (1,)), ((), ())), preferred_element_type=F32)


def slot_of(meta, source, target):
    base = 4 + (source * NC + meta[0]) * 3
    second = jnp.where(meta[base + 1] == target, 1, 0)
    slot = jnp.where(meta[base + 2] == target, 2, second)
    return slot, meta[base + slot] == target


def selected(meta_ref, p_ref, source, target):
    slot, found = slot_of(meta_ref, source, target)
    block = p_ref[source, slot]
    return jnp.where(found, block, jnp.zeros_like(block))


MIRRORED_UPPER = [(9, 12), (9, 14), (11, 13), (11, 14), (13, 14)]


def mirrored_weights(meta, inverse, panels):
    def kernel(meta_ref, d_ref, p_ref, o_ref):
        for i in range(3):
            o_ref[i] = d_ref[9 + 2 * i]
        for i, (source, target) in enumerate(MIRRORED_UPPER):
            block = selected(meta_ref, p_ref, source, target)
            o_ref[3 + i, :, :128] = block[:128]
            o_ref[3 + i, :, 128:] = block[128:]

    return pl.pallas_call(
        kernel,
        in_specs=[SMEM, VMEM, VMEM],
        out_specs=VMEM,
        out_shape=jax.ShapeDtypeStruct((8, 128, 256), BF16),
        compiler_params=params(0),
        name="mirrored_weights",
    )(meta, inverse, panels)


def stack_weights(meta, inverse, panels, got):
    def kernel(meta_ref, d_ref, p_ref, g_ref, two_ref, one_ref):
        def join(out_ref, place, source, target, index):
            block = selected(meta_ref, p_ref, source, target)
            for half in range(2):
                rows = slice(128 * half, 128 * half + 128)
                out_ref[place + half, :, :128] = block[rows]
                out_ref[place + half, :, 128:] = g_ref[index, :, rows]

        two_ref[0] = d_ref[8]
        two_ref[1] = d_ref[10]
        two_ref[2] = g_ref[0]
        two_ref[3] = g_ref[1]
        join(two_ref, 4, 8, 12, 3)
        join(two_ref, 6, 10, 13, 5)
        join(two_ref, 8, 8, 14, 4)
        join(two_ref, 10, 10, 14, 6)
        one_ref[0] = d_ref[12]
        one_ref[1] = g_ref[2]
        one_ref[2] = d_ref[14]
        join(one_ref, 3, 12, 14, 7)

    return pl.pallas_call(
        kernel,
        in_specs=[SMEM, VMEM, VMEM, VMEM],
        out_specs=[VMEM, VMEM],
        out_shape=[
            jax.ShapeDtypeStruct((12, 128, 256), BF16),
            jax.ShapeDtypeStruct((5, 128, 256), BF16),
        ],
        compiler_params=params(0),
        name="stack_weights",
    )(meta, inverse, panels, got)


def solve_leaves(spread, inverse):
    def kernel(b_ref, d_hbm, x_ref, h_ref, d_ref, sem):
        copies = [pltpu.make_async_copy(d_hbm.at[c], d_ref.at[c], sem.at[c]) for c in range(NC)]
        for copy in copies:
            copy.start()
        for c in range(NC):
            copies[c].wait()
            for n in range(8):
                left = b_ref[2 * c : 2 * c + 2, n].reshape(32, 256)
                value = dot_t(left, d_ref[c, n])
                if c:
                    value = value + x_ref[n]
                x_ref[n] = value
        for n in range(8):
            half = x_ref[n].astype(BF16)
            for z in range(8):
                h_ref[z, n] = half

    return pl.pallas_call(
        kernel,
        in_specs=[VMEM, HBM],
        out_specs=[VMEM, VMEM],
        out_shape=[
            jax.ShapeDtypeStruct((8, 32, 128), F32),
            jax.ShapeDtypeStruct((8, 8, 32, 128), BF16),
        ],
        scratch_shapes=[
            pltpu.VMEM((NC, 8, 128, 256), BF16),
            pltpu.SemaphoreType.DMA((NC,)),
        ],
        compiler_params=params(0, STREAM_LIMIT),
        name="solve_leaves",
    )(spread, inverse)


def update_from_leaves(meta, own, other, panels, right):
    def kernel(meta_ref, a_ref, b_ref, p_ref, r_ref, o_ref):
        core, row = meta_ref[1], meta_ref[2]
        for t in range(7):
            target = 8 + t
            if t < 4:
                sources = range(2 * t, 2 * t + 2)
            elif t < 6:
                sources = range(4 * (t - 4), 4 * (t - 4) + 4)
            else:
                sources = range(8)
            blocks = []
            for s in sources:
                slot, found = slot_of(meta_ref, s, target)
                block = p_ref[s, slot]
                blocks.append(jnp.where(found, block, jnp.zeros_like(block)))
            for parity, x_ref in ((core, a_ref), (1 - core, b_ref)):
                acc = jnp.zeros((256, 256), F32)
                for s, block in zip(sources, blocks, strict=True):
                    acc = acc + dot_t(x_ref[:, s].reshape(256, 128), block)
                for half in range(2):
                    value = acc[:, 128 * half : 128 * half + 128].astype(BF16)
                    o_ref[:, pl.ds(parity, 1), half, t] = value.reshape(8, 1, 32, 128)
        z, parity = row // 4, (row // 2) % 2
        start = pl.multiple_of(16 * (row % 2), 16)
        for half in range(2):
            for t in range(7):
                part = o_ref[z, parity, half, t, pl.ds(start, 16), :].astype(F32)
                part = part - r_ref[8 + t, :, 128 * half : 128 * half + 128]
                o_ref[z, parity, half, t, pl.ds(start, 16), :] = part.astype(BF16)

    return pl.pallas_call(
        kernel,
        grid=(1,),
        in_specs=[
            SMEM,
            VMEM,
            VMEM,
            pl.BlockSpec((8, 3, 256, 128), lambda i: (0, 0, 0, 0)),
            VMEM,
        ],
        out_specs=VMEM,
        out_shape=jax.ShapeDtypeStruct((8, 2, 2, 7, 32, 128), BF16),
        compiler_params=params(),
        name="update_from_leaves",
    )(meta, own, other, panels, right)


def first_residual(parts):
    def kernel(p_ref, natural_ref, mirrored_ref):
        residual = (-jnp.sum(p_ref[...].astype(F32), axis=0)).astype(BF16)
        for i in range(4):
            natural_ref[i] = residual[2 * i]
        for i in range(3):
            mirrored_ref[i] = residual[2 * i + 1]

    return pl.pallas_call(
        kernel,
        in_specs=[VMEM],
        out_specs=[VMEM, VMEM],
        out_shape=[
            jax.ShapeDtypeStruct((4, 32, 128), BF16),
            jax.ShapeDtypeStruct((3, 32, 128), BF16),
        ],
        compiler_params=params(0),
        name="first_residual",
    )(parts)


def first_payload(meta, natural, mirrored):
    def kernel(meta_ref, n_ref, m_ref, o_ref):
        row = meta_ref[2]
        for r in range(NR):
            for p in range(2):
                o_ref[r, p] = jnp.where(row <= r, n_ref[p], m_ref[p])

    return pl.pallas_call(
        kernel,
        in_specs=[SMEM, VMEM, VMEM],
        out_specs=VMEM,
        out_shape=jax.ShapeDtypeStruct((NR, 2, 32, 128), BF16),
        compiler_params=params(0),
        name="first_payload",
    )(meta, natural, mirrored)


def solve_level(meta, spread, local, pairs, weights, targets):
    used = min(b for terms, _ in targets for _, b in terms)

    def kernel(meta_ref, x_ref, y_ref, w_hbm, natural_ref, mirrored_ref, o_ref, w_ref, sem):
        row = meta_ref[2]
        pieces = [(c, slice(0, 2 * pairs)) for c in range(NC)]
        pieces += [(c, slice(used, None)) for c in range(NC)]
        copies = [
            pltpu.make_async_copy(w_hbm.at[piece], w_ref.at[piece], sem.at[i])
            for i, piece in enumerate(pieces)
        ]
        for copy in copies:
            copy.start()

        def mirrored_block(b, p):
            return jnp.where(row == b, y_ref[p], x_ref[b, p])

        for c in range(NC):
            copies[c].wait()
            for p in range(pairs):
                left = jnp.concatenate([x_ref[2 * c, p], x_ref[2 * c + 1, p]], axis=1)
                value = dot_t(left, w_ref[c, p])
                left = jnp.concatenate(
                    [mirrored_block(31 - 2 * c, p), mirrored_block(30 - 2 * c, p)], axis=1
                )
                other = dot_t(left, w_ref[c, pairs + p])
                if c:
                    value = value + natural_ref[p]
                    other = other + mirrored_ref[p]
                natural_ref[p] = value
                mirrored_ref[p] = other
        joined = [
            jnp.concatenate([natural_ref[p].astype(BF16), mirrored_ref[p].astype(BF16)], axis=1)
            for p in range(pairs)
        ]
        for c in range(NC):
            copies[NC + c].wait()
            for t, (terms, flipped) in enumerate(targets):
                for half in range(2):
                    total = jnp.zeros((32, 128), F32)
                    for p, b in terms:
                        total = total + dot_t(joined[p], w_ref[c, b + half])
                    r = 2 * c + half
                    o_ref[31 - r if flipped else r, t] = total.astype(BF16)

    return pl.pallas_call(
        kernel,
        in_specs=[SMEM, VMEM, VMEM, HBM],
        out_specs=[VMEM, VMEM, VMEM],
        out_shape=[
            jax.ShapeDtypeStruct((pairs, 32, 128), F32),
            jax.ShapeDtypeStruct((pairs, 32, 128), F32),
            jax.ShapeDtypeStruct((NR, len(targets), 32, 128), BF16),
        ],
        scratch_shapes=[
            pltpu.VMEM(weights.shape, BF16),
            pltpu.SemaphoreType.DMA((2 * NC,)),
        ],
        compiler_params=params(0, STREAM_LIMIT),
        name="solve_level",
    )(meta, spread, local, weights)


def solve_node(x_ref, d_ref, n, place):
    acc = jnp.zeros((32, 128), F32)
    for c in range(NC):
        left = jnp.concatenate([x_ref[2 * c, n], x_ref[2 * c + 1, n]], axis=1)
        acc = acc + dot_t(left, d_ref[c, place])
    return acc


def solve_root(residual, weights):
    def kernel(x_ref, d_ref, s_ref):
        s_ref[0] = solve_node(x_ref, d_ref, 0, 0)

    return pl.pallas_call(
        kernel,
        grid=(1,),
        in_specs=[VMEM, pl.BlockSpec((NC, 1, 128, 256), lambda i: (0, 2, 0, 0))],
        out_specs=VMEM,
        out_shape=jax.ShapeDtypeStruct((1, 32, 128), F32),
        compiler_params=params(1, STREAM_LIMIT),
        name="solve_root",
    )(residual, weights)


def next_residual(meta, parts, natural, mirrored):
    def kernel(meta_ref, p_ref, n_ref, m_ref, o_ref, local_ref, rest_ref):
        row = meta_ref[2]
        total = jnp.sum(p_ref[...].astype(F32), axis=0)
        first = (n_ref[2].astype(F32) - total[0]).astype(BF16)
        second = (m_ref[2].astype(F32) - total[1]).astype(BF16)
        for r in range(NR):
            o_ref[r, 0] = jnp.where(row <= r, first, second)
        local_ref[0] = second
        rest_ref[0] = n_ref[3].astype(F32) - total[2]

    return pl.pallas_call(
        kernel,
        in_specs=[SMEM, VMEM, VMEM, VMEM],
        out_specs=[VMEM, VMEM, VMEM],
        out_shape=[
            jax.ShapeDtypeStruct((NR, 1, 32, 128), BF16),
            jax.ShapeDtypeStruct((1, 32, 128), BF16),
            jax.ShapeDtypeStruct((1, 32, 128), F32),
        ],
        compiler_params=params(0),
        name="next_residual",
    )(meta, parts, natural, mirrored)


def last_residual(parts, rest):
    def kernel(p_ref, rest_ref, o_ref):
        half = (rest_ref[...] - jnp.sum(p_ref[...].astype(F32), axis=0)).astype(BF16)
        for r in range(NR):
            o_ref[r] = half

    return pl.pallas_call(
        kernel,
        in_specs=[VMEM, VMEM],
        out_specs=VMEM,
        out_shape=jax.ShapeDtypeStruct((NR, 1, 32, 128), BF16),
        compiler_params=params(0),
        name="last_residual",
    )(parts, rest)


def exchange(values, axes):
    shape = values.shape
    flat = values.reshape(shape[0], -1, shape[-1])
    return lax.all_to_all(flat, axes, 0, 0, tiled=True).reshape(shape)


def spread_over(values, axes, size):
    return exchange(jnp.broadcast_to(values[None], (size,) + values.shape), axes)


def to_owner(values):
    pairs = [
        (r * NC + c, (2 * c + r % 2) * NC + r // 2) for r in range(NR) for c in range(NC)
    ]
    return lax.ppermute(values, ALL, pairs)


def to_mirrored_row(values):
    pairs = [(r * NC + c, (31 - r) * NC + c) for r in range(NR) for c in range(NC)]
    return lax.ppermute(values, ALL, pairs)


def to_mirrored_owner(values):
    pairs = [
        (r * NC + c, (31 - 2 * c - r % 2) * NC + r // 2) for r in range(NR) for c in range(NC)
    ]
    return lax.ppermute(values, ALL, pairs)


def per_device(right_sides, diag_inverse, panels, block_map):
    row = lax.axis_index(ROW)
    col = lax.axis_index(COL)
    core = lax.axis_index("core")
    leaf_right, diag_inverse = lax.optimization_barrier(
        (right_sides[:8].astype(BF16), diag_inverse)
    )
    moved = to_owner(leaf_right)
    leaf_inverse = lax.all_gather(diag_inverse[:8], COL, axis=0)

    zero = jnp.zeros((), jnp.int32)
    meta = jnp.concatenate(
        [jnp.stack([col, core, row, zero]).astype(jnp.int32), block_map.reshape(-1)]
    )
    sent = mirrored_weights(meta, diag_inverse, panels)
    spread = spread_over(moved, ROW, NR)
    spread, sent = lax.optimization_barrier((spread, sent))

    leaves, copies = solve_leaves(spread, leaf_inverse)
    copies, sent = lax.optimization_barrier((copies, sent))
    own = exchange(copies, "z")
    stack_two, stack_one = stack_weights(meta, diag_inverse, panels, to_mirrored_row(sent))
    stack_two, stack_one, own = lax.optimization_barrier((stack_two, stack_one, own))
    other = lax.ppermute(own, "core", [(0, 1), (1, 0)])
    weights_two = lax.all_gather(stack_two, COL, axis=0)
    weights_one = lax.all_gather(stack_one, COL, axis=0)
    parts = update_from_leaves(meta, own, other, panels, right_sides)
    natural, mirrored = first_residual(exchange(parts.reshape(NR, 7, 32, 128), ROW))
    natural, mirrored = to_owner(natural), to_mirrored_owner(mirrored)

    spread = exchange(first_payload(meta, natural, mirrored), ROW)
    targets = [([(0, 4)], False), ([(1, 6)], True), ([(0, 8), (1, 10)], False)]
    two, two_mirrored, parts = solve_level(meta, spread, mirrored, 2, weights_two, targets)
    spread, local, rest = next_residual(meta, exchange(parts, ROW), natural, mirrored)
    spread = exchange(spread, ROW)
    one, one_mirrored, parts = solve_level(
        meta, spread, local, 1, weights_one, [([(0, 3)], False)]
    )
    back = to_mirrored_row(jnp.concatenate([two_mirrored, one_mirrored], axis=0))
    spread = last_residual(exchange(parts, ROW), rest)
    root = solve_root(exchange(spread, ROW), weights_one)
    upper = [two[:1], back[:1], two[1:], back[1:2], one, back[2:], root]
    return jnp.concatenate([leaves, *upper], axis=0)


def solution(mesh):
    split = Mesh(mesh.devices.reshape(4, 8, 8, 2), ALL)
    return jax.shard_map(
        per_device,
        mesh=split,
        in_specs=(P(None, ROW, COL), P(None, ROW, COL), P(None, None, COL, ROW), P()),
        out_specs=P(None, COL, ROW),
        check_vma=False,
    )
```

```python
import jax
import jax.numpy as jnp
from jax import lax
from jax.experimental import pallas as pl
from jax.experimental.pallas import tpu as pltpu
from jax.sharding import Mesh
from jax.sharding import PartitionSpec as P

ROW = ("x", "y")
COL = ("z", "core")
ALL = ("x", "y", "z", "core")
NR = 32
NC = 16
VMEM_LIMIT = 24 * 1024 * 1024
STREAM_LIMIT = 56 * 1024 * 1024
F32 = jnp.float32
BF16 = jnp.bfloat16
VMEM = pl.BlockSpec(memory_space=pltpu.VMEM)
SMEM = pl.BlockSpec(memory_space=pltpu.SMEM)
HBM = pl.BlockSpec(memory_space=pltpu.HBM)


def params(n=1, limit=VMEM_LIMIT):
    return pltpu.CompilerParams(
        vmem_limit_bytes=limit, dimension_semantics=("arbitrary",) * n
    )


def dot_t(a, b):
    return lax.dot_general(a, b, (((1,), (1,)), ((), ())), preferred_element_type=F32)


def slot_of(meta, source, target):
    base = 4 + (source * NC + meta[0]) * 3
    second = jnp.where(meta[base + 1] == target, 1, 0)
    slot = jnp.where(meta[base + 2] == target, 2, second)
    return slot, meta[base + slot] == target


def selected(meta_ref, p_ref, source, target):
    slot, found = slot_of(meta_ref, source, target)
    block = p_ref[source, slot]
    return jnp.where(found, block, jnp.zeros_like(block))


def stack_weights(meta, inverse, panels):
    def kernel(meta_ref, d_ref, p_ref, two_ref, one_ref):
        def join(out_ref, place, source, target):
            for side in range(2):
                columns = slice(128 * side, 128 * side + 128)
                block = selected(meta_ref, p_ref, source + side, target)
                for half in range(2):
                    out_ref[place + half, :, columns] = block[128 * half : 128 * half + 128]

        two_ref[:4] = d_ref[8:12]
        one_ref[:3] = d_ref[12:]
        join(two_ref, 4, 8, 12)
        join(two_ref, 6, 10, 13)
        join(two_ref, 8, 8, 14)
        join(two_ref, 10, 10, 14)
        join(one_ref, 3, 12, 14)

    return pl.pallas_call(
        kernel,
        in_specs=[SMEM, VMEM, VMEM],
        out_specs=[VMEM, VMEM],
        out_shape=[
            jax.ShapeDtypeStruct((12, 128, 256), BF16),
            jax.ShapeDtypeStruct((5, 128, 256), BF16),
        ],
        compiler_params=params(0),
        name="stack_weights",
    )(meta, inverse, panels)


def solve_leaves(spread, inverse):
    def kernel(b_ref, d_hbm, x_ref, h_ref, d_ref, sem):
        copies = [pltpu.make_async_copy(d_hbm.at[c], d_ref.at[c], sem.at[c]) for c in range(NC)]
        for copy in copies:
            copy.start()
        for c in range(NC):
            copies[c].wait()
            for n in range(8):
                left = b_ref[2 * c : 2 * c + 2, n].reshape(32, 256)
                value = dot_t(left, d_ref[c, n])
                if c:
                    value = value + x_ref[n]
                x_ref[n] = value
        for n in range(8):
            half = x_ref[n].astype(BF16)
            for z in range(8):
                h_ref[z, n] = half

    return pl.pallas_call(
        kernel,
        in_specs=[VMEM, HBM],
        out_specs=[VMEM, VMEM],
        out_shape=[
            jax.ShapeDtypeStruct((8, 32, 128), F32),
            jax.ShapeDtypeStruct((8, 8, 32, 128), BF16),
        ],
        scratch_shapes=[
            pltpu.VMEM((NC, 8, 128, 256), BF16),
            pltpu.SemaphoreType.DMA((NC,)),
        ],
        compiler_params=params(0, STREAM_LIMIT),
        name="solve_leaves",
    )(spread, inverse)


def update_from_leaves(meta, own, other, panels, right):
    def kernel(meta_ref, a_ref, b_ref, p_ref, r_ref, o_ref):
        core, row = meta_ref[1], meta_ref[2]
        for t in range(7):
            target = 8 + t
            if t < 4:
                sources = range(2 * t, 2 * t + 2)
            elif t < 6:
                sources = range(4 * (t - 4), 4 * (t - 4) + 4)
            else:
                sources = range(8)
            blocks = [selected(meta_ref, p_ref, s, target) for s in sources]
            for parity, x_ref in ((core, a_ref), (1 - core, b_ref)):
                acc = jnp.zeros((256, 256), F32)
                for s, block in zip(sources, blocks, strict=True):
                    acc = acc + dot_t(x_ref[:, s].reshape(256, 128), block)
                for half in range(2):
                    value = acc[:, 128 * half : 128 * half + 128].astype(BF16)
                    o_ref[:, pl.ds(parity, 1), half, t] = value.reshape(8, 1, 32, 128)
        z, parity = row // 4, (row // 2) % 2
        start = pl.multiple_of(16 * (row % 2), 16)
        for half in range(2):
            for t in range(7):
                part = o_ref[z, parity, half, t, pl.ds(start, 16), :].astype(F32)
                part = part - r_ref[8 + t, :, 128 * half : 128 * half + 128]
                o_ref[z, parity, half, t, pl.ds(start, 16), :] = part.astype(BF16)

    return pl.pallas_call(
        kernel,
        grid=(1,),
        in_specs=[
            SMEM,
            VMEM,
            VMEM,
            pl.BlockSpec((8, 3, 256, 128), lambda i: (0, 0, 0, 0)),
            VMEM,
        ],
        out_specs=VMEM,
        out_shape=jax.ShapeDtypeStruct((8, 2, 2, 7, 32, 128), BF16),
        compiler_params=params(),
        name="update_from_leaves",
    )(meta, own, other, panels, right)


def first_residual(parts):
    def kernel(p_ref, o_ref):
        o_ref[...] = (-jnp.sum(p_ref[...].astype(F32), axis=0)).astype(BF16)

    return pl.pallas_call(
        kernel,
        in_specs=[VMEM],
        out_specs=VMEM,
        out_shape=jax.ShapeDtypeStruct((7, 32, 128), BF16),
        compiler_params=params(0),
        name="first_residual",
    )(parts)


def solve_node(x_ref, d_ref, n, place):
    acc = jnp.zeros((32, 128), F32)
    for c in range(NC):
        left = jnp.concatenate([x_ref[2 * c, n], x_ref[2 * c + 1, n]], axis=1)
        acc = acc + dot_t(left, d_ref[c, place])
    return acc


def solve_pairs(x_ref, w_hbm, s_ref, w_ref, sem, nodes, first, update):
    pieces = [(c, slice(0, nodes)) for c in range(NC)]
    pieces += [(c, slice(first, None)) for c in range(NC)]
    copies = [
        pltpu.make_async_copy(w_hbm.at[piece], w_ref.at[piece], sem.at[i])
        for i, piece in enumerate(pieces)
    ]
    for copy in copies:
        copy.start()
    for c in range(NC):
        copies[c].wait()
        for n in range(nodes):
            left = jnp.concatenate([x_ref[2 * c, n], x_ref[2 * c + 1, n]], axis=1)
            value = dot_t(left, w_ref[c, n])
            if c:
                value = value + s_ref[n]
            s_ref[n] = value
    joined = [
        jnp.concatenate([s_ref[n].astype(BF16), s_ref[n + 1].astype(BF16)], axis=1)
        for n in range(0, nodes, 2)
    ]
    for c in range(NC):
        copies[NC + c].wait()
        update(c, joined)


def solve_two(residual, weights):
    def kernel(x_ref, w_hbm, s_ref, o_ref, keep_ref, w_ref, sem):
        def update(c, joined):
            for half in range(2):
                r = 2 * c + half
                o_ref[r, 0] = dot_t(joined[0], w_ref[c, 4 + half]).astype(BF16)
                o_ref[r, 1] = dot_t(joined[1], w_ref[c, 6 + half]).astype(BF16)
                keep_ref[r] = dot_t(joined[0], w_ref[c, 8 + half]) + dot_t(
                    joined[1], w_ref[c, 10 + half]
                )

        solve_pairs(x_ref, w_hbm, s_ref, w_ref, sem, 4, 4, update)

    return pl.pallas_call(
        kernel,
        in_specs=[VMEM, HBM],
        out_specs=[VMEM, VMEM, VMEM],
        out_shape=[
            jax.ShapeDtypeStruct((4, 32, 128), F32),
            jax.ShapeDtypeStruct((NR, 2, 32, 128), BF16),
            jax.ShapeDtypeStruct((NR, 32, 128), F32),
        ],
        scratch_shapes=[
            pltpu.VMEM(weights.shape, BF16),
            pltpu.SemaphoreType.DMA((2 * NC,)),
        ],
        compiler_params=params(0, STREAM_LIMIT),
        name="solve_two",
    )(residual, weights)


def solve_one(residual, weights, keep):
    def kernel(x_ref, w_hbm, keep_ref, s_ref, o_ref, w_ref, sem):
        def update(c, joined):
            for half in range(2):
                r = 2 * c + half
                part = keep_ref[r] + dot_t(joined[0], w_ref[c, 3 + half])
                o_ref[r, 0] = part.astype(BF16)

        solve_pairs(x_ref, w_hbm, s_ref, w_ref, sem, 2, 3, update)

    return pl.pallas_call(
        kernel,
        in_specs=[VMEM, HBM, VMEM],
        out_specs=[VMEM, VMEM],
        out_shape=[
            jax.ShapeDtypeStruct((2, 32, 128), F32),
            jax.ShapeDtypeStruct((NR, 1, 32, 128), BF16),
        ],
        scratch_shapes=[
            pltpu.VMEM(weights.shape, BF16),
            pltpu.SemaphoreType.DMA((2 * NC,)),
        ],
        compiler_params=params(0, STREAM_LIMIT),
        name="solve_one",
    )(residual, weights, keep)


def solve_root(residual, weights):
    def kernel(x_ref, d_ref, s_ref):
        s_ref[0] = solve_node(x_ref, d_ref, 0, 2)

    return pl.pallas_call(
        kernel,
        in_specs=[VMEM, VMEM],
        out_specs=VMEM,
        out_shape=jax.ShapeDtypeStruct((1, 32, 128), F32),
        compiler_params=params(0),
        name="solve_root",
    )(residual, weights)


def next_residual(parts, rest):
    nodes = rest.shape[0]

    def kernel(p_ref, rest_ref, o_ref):
        residual = rest_ref[...].astype(F32) - jnp.sum(p_ref[...].astype(F32), axis=0)
        half = residual.astype(BF16)
        for r in range(NR):
            o_ref[r] = half

    return pl.pallas_call(
        kernel,
        in_specs=[VMEM, VMEM],
        out_specs=VMEM,
        out_shape=jax.ShapeDtypeStruct((NR, nodes, 32, 128), BF16),
        compiler_params=params(0),
        name="next_residual",
    )(parts, rest)


def exchange(values, axes):
    shape = values.shape
    flat = values.reshape(shape[0], -1, shape[-1])
    return lax.all_to_all(flat, axes, 0, 0, tiled=True).reshape(shape)


def spread_over(values, axes, size):
    return exchange(jnp.broadcast_to(values[None], (size,) + values.shape), axes)


def to_owner(values):
    pairs = [
        (r * NC + c, (2 * c + r % 2) * NC + r // 2) for r in range(NR) for c in range(NC)
    ]
    return lax.ppermute(values, ALL, pairs)


def per_device(right_sides, diag_inverse, panels, block_map):
    row = lax.axis_index(ROW)
    col = lax.axis_index(COL)
    core = lax.axis_index("core")
    leaf_right, diag_inverse = lax.optimization_barrier(
        (right_sides[:8].astype(BF16), diag_inverse)
    )
    moved = to_owner(leaf_right)
    leaf_inverse = lax.all_gather(diag_inverse[:8], COL, axis=0)

    zero = jnp.zeros((), jnp.int32)
    meta = jnp.concatenate(
        [jnp.stack([col, core, row, zero]).astype(jnp.int32), block_map.reshape(-1)]
    )
    stack_two, stack_one = stack_weights(meta, diag_inverse, panels)
    spread = spread_over(moved, ROW, NR)
    spread, stack_two, stack_one = lax.optimization_barrier((spread, stack_two, stack_one))

    leaves, copies = solve_leaves(spread, leaf_inverse)
    own = exchange(copies, "z")
    other = lax.ppermute(own, "core", [(0, 1), (1, 0)])
    stack_two, stack_one, own = lax.optimization_barrier((stack_two, stack_one, own))
    weights_two = lax.all_gather(stack_two, COL, axis=0)
    weights_one = lax.all_gather(stack_one, COL, axis=0)
    parts = update_from_leaves(meta, own, other, panels, right_sides)
    parts = exchange(parts.reshape(NR, 7, 32, 128), ROW)
    residual = to_owner(first_residual(parts))

    spread = spread_over(residual[:4], ROW, NR)
    two, parts, keep = solve_two(spread, weights_two)
    spread = exchange(next_residual(exchange(parts, ROW), residual[4:6]), ROW)
    one, parts = solve_one(spread, weights_one, keep)
    spread = exchange(next_residual(exchange(parts, ROW), residual[6:]), ROW)
    root = solve_root(spread, weights_one)
    return jnp.concatenate([leaves, two, one, root], axis=0)


def solution(mesh):
    split = Mesh(mesh.devices.reshape(4, 8, 8, 2), ALL)
    return jax.shard_map(
        per_device,
        mesh=split,
        in_specs=(P(None, ROW, COL), P(None, ROW, COL), P(None, None, COL, ROW), P()),
        out_specs=P(None, COL, ROW),
        check_vma=False,
    )
```

```python
import jax
import jax.numpy as jnp
from jax import lax
from jax.experimental import pallas as pl
from jax.experimental.pallas import tpu as pltpu
from jax.sharding import Mesh
from jax.sharding import PartitionSpec as P

ROW = ("x", "y")
COL = ("z", "core")
ALL = ("x", "y", "z", "core")
NR = 32
NC = 16
VMEM_LIMIT = 24 * 1024 * 1024
STREAM_LIMIT = 56 * 1024 * 1024
F32 = jnp.float32
BF16 = jnp.bfloat16
VMEM = pl.BlockSpec(memory_space=pltpu.VMEM)
SMEM = pl.BlockSpec(memory_space=pltpu.SMEM)
HBM = pl.BlockSpec(memory_space=pltpu.HBM)


def params(n=1, limit=VMEM_LIMIT):
    return pltpu.CompilerParams(
        vmem_limit_bytes=limit, dimension_semantics=("arbitrary",) * n
    )


def dot_t(a, b):
    return lax.dot_general(a, b, (((1,), (1,)), ((), ())), preferred_element_type=F32)


def slot_of(meta, source, target):
    base = 4 + (source * NC + meta[0]) * 3
    second = jnp.where(meta[base + 1] == target, 1, 0)
    slot = jnp.where(meta[base + 2] == target, 2, second)
    return slot, meta[base + slot] == target


def selected(meta_ref, p_ref, source, target):
    slot, found = slot_of(meta_ref, source, target)
    block = p_ref[source, slot]
    return jnp.where(found, block, jnp.zeros_like(block))


def stack_weights(meta, inverse, panels):
    def kernel(meta_ref, d_ref, p_ref, two_ref, one_ref):
        def join(out_ref, place, source, target):
            for side in range(2):
                columns = slice(128 * side, 128 * side + 128)
                block = selected(meta_ref, p_ref, source + side, target)
                for half in range(2):
                    out_ref[place + half, :, columns] = block[128 * half : 128 * half + 128]

        two_ref[:4] = d_ref[8:12]
        one_ref[:3] = d_ref[12:]
        join(two_ref, 4, 8, 12)
        join(two_ref, 6, 10, 13)
        join(two_ref, 8, 8, 14)
        join(two_ref, 10, 10, 14)
        join(one_ref, 3, 12, 14)

    return pl.pallas_call(
        kernel,
        in_specs=[SMEM, VMEM, VMEM],
        out_specs=[VMEM, VMEM],
        out_shape=[
            jax.ShapeDtypeStruct((12, 128, 256), BF16),
            jax.ShapeDtypeStruct((5, 128, 256), BF16),
        ],
        compiler_params=params(0),
        name="stack_weights",
    )(meta, inverse, panels)


def solve_leaves(spread, inverse):
    def kernel(b_ref, d_hbm, x_ref, h_ref, d_ref, sem):
        copies = []
        for g in range(4):
            part = pl.ds(4 * g, 4)
            copies.append(pltpu.make_async_copy(d_hbm.at[part], d_ref.at[part], sem.at[g]))
            copies[g].start()
        for c in range(NC):
            if c % 4 == 0:
                copies[c // 4].wait()
            for n in range(8):
                left = b_ref[2 * c : 2 * c + 2, n].reshape(32, 256)
                value = dot_t(left, d_ref[c, n])
                if c:
                    value = value + x_ref[n]
                x_ref[n] = value
        for n in range(8):
            half = x_ref[n].astype(BF16)
            for z in range(8):
                h_ref[z, n] = half

    return pl.pallas_call(
        kernel,
        in_specs=[VMEM, HBM],
        out_specs=[VMEM, VMEM],
        out_shape=[
            jax.ShapeDtypeStruct((8, 32, 128), F32),
            jax.ShapeDtypeStruct((8, 8, 32, 128), BF16),
        ],
        scratch_shapes=[
            pltpu.VMEM((NC, 8, 128, 256), BF16),
            pltpu.SemaphoreType.DMA((4,)),
        ],
        compiler_params=params(0, STREAM_LIMIT),
        name="solve_leaves",
    )(spread, inverse)


LEAF_PAIRS = [[0], [2], [4], [6], [0, 2], [4, 6], [0, 2, 4, 6]]


def select_leaves(meta, panels):
    def kernel(meta_ref, p_ref, o_ref):
        place = 0
        for t, firsts in enumerate(LEAF_PAIRS):
            for s in firsts:
                o_ref[place, :, :128] = selected(meta_ref, p_ref, s, 8 + t)
                o_ref[place, :, 128:] = selected(meta_ref, p_ref, s + 1, 8 + t)
                place += 1

    return pl.pallas_call(
        kernel,
        grid=(1,),
        in_specs=[SMEM, pl.BlockSpec((8, 3, 256, 128), lambda i: (0, 0, 0, 0))],
        out_specs=VMEM,
        out_shape=jax.ShapeDtypeStruct((12, 256, 256), BF16),
        compiler_params=params(),
        name="select_leaves",
    )(meta, panels)


def update_from_leaves(meta, solved, blocks, blocks_got, right, right_got):
    def kernel(meta_ref, x_ref, a_ref, b_ref, r_ref, rg_ref, o_ref):
        core, row = meta_ref[1], meta_ref[2]
        joined = {}
        for s in range(0, 8, 2):
            joined[s] = jnp.concatenate(
                [x_ref[:, s].reshape(256, 128), x_ref[:, s + 1].reshape(256, 128)], axis=1
            )
        place = 0
        for t, firsts in enumerate(LEAF_PAIRS):
            for column, block_ref in ((core, a_ref), (1 - core, b_ref)):
                acc = jnp.zeros((256, 256), F32)
                for i, s in enumerate(firsts):
                    acc = acc + dot_t(joined[s], block_ref[place + i])
                for half in range(2):
                    value = acc[:, 128 * half : 128 * half + 128].astype(BF16)
                    o_ref[:, pl.ds(column, 1), half, t] = value.reshape(8, 1, 32, 128)
            place += len(firsts)
        z = row // 4
        start = pl.multiple_of(16 * (row % 2), 16)

        @pl.when(core == (row // 2) % 2)
        def _():
            for t in range(7):
                for half in range(2):
                    columns = slice(128 * half, 128 * half + 128)
                    for column, held in (
                        (core, r_ref[8 + t, :, columns]),
                        (1 - core, rg_ref[t, :, columns]),
                    ):
                        part = o_ref[z, column, half, t, pl.ds(start, 16), :].astype(F32)
                        o_ref[z, column, half, t, pl.ds(start, 16), :] = (part - held).astype(
                            BF16
                        )

    return pl.pallas_call(
        kernel,
        in_specs=[SMEM, VMEM, VMEM, VMEM, VMEM, VMEM],
        out_specs=VMEM,
        out_shape=jax.ShapeDtypeStruct((8, 2, 2, 7, 32, 128), BF16),
        compiler_params=params(0),
        name="update_from_leaves",
    )(meta, solved, blocks, blocks_got, right, right_got)


def first_residual(parts):
    def kernel(p_ref, o_ref):
        o_ref[...] = (-jnp.sum(p_ref[...].astype(F32), axis=0)).astype(BF16)

    return pl.pallas_call(
        kernel,
        in_specs=[VMEM],
        out_specs=VMEM,
        out_shape=jax.ShapeDtypeStruct((7, 32, 128), BF16),
        compiler_params=params(0),
        name="first_residual",
    )(parts)


def solve_node(x_ref, d_ref, n, place):
    acc = jnp.zeros((32, 128), F32)
    for c in range(NC):
        left = jnp.concatenate([x_ref[2 * c, n], x_ref[2 * c + 1, n]], axis=1)
        acc = acc + dot_t(left, d_ref[c, place])
    return acc


def solve_pairs(x_ref, w_hbm, s_ref, w_ref, sem, nodes, first, groups, update):
    size = NC // groups
    parts = [pl.ds(g * size, size) for g in range(groups)]
    pieces = [(part, slice(0, nodes)) for part in parts]
    pieces += [(part, slice(first, None)) for part in parts]
    copies = [
        pltpu.make_async_copy(w_hbm.at[piece], w_ref.at[piece], sem.at[i])
        for i, piece in enumerate(pieces)
    ]
    for copy in copies:
        copy.start()
    for c in range(NC):
        if c % size == 0:
            copies[c // size].wait()
        for n in range(nodes):
            left = jnp.concatenate([x_ref[2 * c, n], x_ref[2 * c + 1, n]], axis=1)
            value = dot_t(left, w_ref[c, n])
            if c:
                value = value + s_ref[n]
            s_ref[n] = value
    joined = [
        jnp.concatenate([s_ref[n].astype(BF16), s_ref[n + 1].astype(BF16)], axis=1)
        for n in range(0, nodes, 2)
    ]
    for c in range(NC):
        if c % size == 0:
            copies[groups + c // size].wait()
        update(c, joined)


def solve_two(residual, weights):
    def kernel(x_ref, w_hbm, s_ref, o_ref, keep_ref, w_ref, sem):
        def update(c, joined):
            for half in range(2):
                r = 2 * c + half
                o_ref[r, 0] = dot_t(joined[0], w_ref[c, 4 + half]).astype(BF16)
                o_ref[r, 1] = dot_t(joined[1], w_ref[c, 6 + half]).astype(BF16)
                keep_ref[r] = dot_t(joined[0], w_ref[c, 8 + half]) + dot_t(
                    joined[1], w_ref[c, 10 + half]
                )

        solve_pairs(x_ref, w_hbm, s_ref, w_ref, sem, 4, 4, 4, update)

    return pl.pallas_call(
        kernel,
        in_specs=[VMEM, HBM],
        out_specs=[VMEM, VMEM, VMEM],
        out_shape=[
            jax.ShapeDtypeStruct((4, 32, 128), F32),
            jax.ShapeDtypeStruct((NR, 2, 32, 128), BF16),
            jax.ShapeDtypeStruct((NR, 32, 128), F32),
        ],
        scratch_shapes=[
            pltpu.VMEM(weights.shape, BF16),
            pltpu.SemaphoreType.DMA((8,)),
        ],
        compiler_params=params(0, STREAM_LIMIT),
        name="solve_two",
    )(residual, weights)


def solve_one(residual, weights, keep):
    def kernel(x_ref, w_hbm, keep_ref, s_ref, o_ref, w_ref, sem):
        def update(c, joined):
            for half in range(2):
                r = 2 * c + half
                part = keep_ref[r] + dot_t(joined[0], w_ref[c, 3 + half])
                o_ref[r, 0] = part.astype(BF16)

        solve_pairs(x_ref, w_hbm, s_ref, w_ref, sem, 2, 3, 2, update)

    return pl.pallas_call(
        kernel,
        in_specs=[VMEM, HBM, VMEM],
        out_specs=[VMEM, VMEM],
        out_shape=[
            jax.ShapeDtypeStruct((2, 32, 128), F32),
            jax.ShapeDtypeStruct((NR, 1, 32, 128), BF16),
        ],
        scratch_shapes=[
            pltpu.VMEM(weights.shape, BF16),
            pltpu.SemaphoreType.DMA((4,)),
        ],
        compiler_params=params(0, STREAM_LIMIT),
        name="solve_one",
    )(residual, weights, keep)


def solve_root(residual, weights):
    def kernel(x_ref, d_ref, s_ref):
        s_ref[0] = solve_node(x_ref, d_ref, 0, 0)

    return pl.pallas_call(
        kernel,
        grid=(1,),
        in_specs=[VMEM, pl.BlockSpec((NC, 1, 128, 256), lambda i: (0, 2, 0, 0))],
        out_specs=VMEM,
        out_shape=jax.ShapeDtypeStruct((1, 32, 128), F32),
        compiler_params=params(1, STREAM_LIMIT),
        name="solve_root",
    )(residual, weights)


def next_residual(parts, rest):
    nodes = rest.shape[0]

    def kernel(p_ref, rest_ref, o_ref):
        residual = rest_ref[...].astype(F32) - jnp.sum(p_ref[...].astype(F32), axis=0)
        half = residual.astype(BF16)
        for r in range(NR):
            o_ref[r] = half

    return pl.pallas_call(
        kernel,
        in_specs=[VMEM, VMEM],
        out_specs=VMEM,
        out_shape=jax.ShapeDtypeStruct((NR, nodes, 32, 128), BF16),
        compiler_params=params(0),
        name="next_residual",
    )(parts, rest)


def exchange(values, axes):
    shape = values.shape
    flat = values.reshape(shape[0], -1, shape[-1])
    return lax.all_to_all(flat, axes, 0, 0, tiled=True).reshape(shape)


def spread_over(values, axes, size):
    return exchange(jnp.broadcast_to(values[None], (size,) + values.shape), axes)


def to_owner(values):
    pairs = [
        (r * NC + c, (2 * c + r % 2) * NC + r // 2) for r in range(NR) for c in range(NC)
    ]
    return lax.ppermute(values, ALL, pairs)


def to_solver(values):
    pairs = [
        (r * NC + c, (4 * (c // 2) + r % 4) * NC + 2 * (r // 4) + c % 2)
        for r in range(NR)
        for c in range(NC)
    ]
    return lax.ppermute(values, ALL, pairs)


def to_other_core(values):
    return lax.ppermute(values, "core", [(0, 1), (1, 0)])


def per_device(right_sides, diag_inverse, panels, block_map):
    row = lax.axis_index(ROW)
    col = lax.axis_index(COL)
    core = lax.axis_index("core")
    leaf_right, diag_inverse = lax.optimization_barrier(
        (right_sides[:8].astype(BF16), diag_inverse)
    )
    moved = to_owner(leaf_right)
    leaf_inverse = lax.all_gather(diag_inverse[:8], COL, axis=0)

    zero = jnp.zeros((), jnp.int32)
    meta = jnp.concatenate(
        [jnp.stack([col, core, row, zero]).astype(jnp.int32), block_map.reshape(-1)]
    )
    stack_two, stack_one = stack_weights(meta, diag_inverse, panels)
    spread = spread_over(moved, ROW, NR)
    blocks = select_leaves(meta, panels)
    blocks_got, right_got = to_other_core(blocks), to_other_core(right_sides[8:])
    spread, stack_two, stack_one, blocks, blocks_got, right_got = lax.optimization_barrier(
        (spread, stack_two, stack_one, blocks, blocks_got, right_got)
    )

    leaves, copies = solve_leaves(spread, leaf_inverse)
    own = exchange(copies, "z")
    stack_two, stack_one, own = lax.optimization_barrier((stack_two, stack_one, own))
    weights_two = lax.all_gather(stack_two, COL, axis=0)
    weights_one = lax.all_gather(stack_one, COL, axis=0)
    parts = update_from_leaves(meta, own, blocks, blocks_got, right_sides, right_got)
    parts = exchange(parts.reshape(NR, 7, 32, 128), ROW)
    residual = to_solver(first_residual(parts))

    spread = spread_over(residual[:4], ROW, NR)
    two, parts, keep = solve_two(spread, weights_two)
    spread = exchange(next_residual(exchange(parts, ROW), residual[4:6]), ROW)
    one, parts = solve_one(spread, weights_one, keep)
    spread = exchange(next_residual(exchange(parts, ROW), residual[6:]), ROW)
    root = solve_root(spread, weights_one)
    return jnp.concatenate([leaves, two, one, root], axis=0)


def solution(mesh):
    split = Mesh(mesh.devices.reshape(4, 8, 8, 2), ALL)
    return jax.shard_map(
        per_device,
        mesh=split,
        in_specs=(P(None, ROW, COL), P(None, ROW, COL), P(None, None, COL, ROW), P()),
        out_specs=P(None, COL, ROW),
        check_vma=False,
    )
```

```python
import jax
import jax.numpy as jnp
from jax import lax
from jax.experimental import pallas as pl
from jax.experimental.pallas import tpu as pltpu
from jax.sharding import Mesh
from jax.sharding import PartitionSpec as P

ROW = ("x", "y")
COL = ("z", "core")
ALL = ("x", "y", "z", "core")
NR = 32
NC = 16
VMEM_LIMIT = 24 * 1024 * 1024
STREAM_LIMIT = 56 * 1024 * 1024
F32 = jnp.float32
BF16 = jnp.bfloat16
VMEM = pl.BlockSpec(memory_space=pltpu.VMEM)
SMEM = pl.BlockSpec(memory_space=pltpu.SMEM)
HBM = pl.BlockSpec(memory_space=pltpu.HBM)


def params(n=1, limit=VMEM_LIMIT):
    return pltpu.CompilerParams(
        vmem_limit_bytes=limit, dimension_semantics=("arbitrary",) * n
    )


def dot_t(a, b):
    return lax.dot_general(a, b, (((1,), (1,)), ((), ())), preferred_element_type=F32)


def slot_of(meta, source, target):
    base = 4 + (source * NC + meta[0]) * 3
    second = jnp.where(meta[base + 1] == target, 1, 0)
    slot = jnp.where(meta[base + 2] == target, 2, second)
    return slot, meta[base + slot] == target


def selected(meta_ref, p_ref, source, target):
    slot, found = slot_of(meta_ref, source, target)
    block = p_ref[source, slot]
    return jnp.where(found, block, jnp.zeros_like(block))


def stack_weights(meta, inverse, panels):
    def kernel(meta_ref, d_ref, p_ref, two_ref, one_ref):
        def join(out_ref, place, source, target):
            for side in range(2):
                columns = slice(128 * side, 128 * side + 128)
                block = selected(meta_ref, p_ref, source + side, target)
                for half in range(2):
                    out_ref[place + half, :, columns] = block[128 * half : 128 * half + 128]

        two_ref[:4] = d_ref[8:12]
        one_ref[:3] = d_ref[12:]
        join(two_ref, 4, 8, 12)
        join(two_ref, 6, 10, 13)
        join(two_ref, 8, 8, 14)
        join(two_ref, 10, 10, 14)
        join(one_ref, 3, 12, 14)

    return pl.pallas_call(
        kernel,
        in_specs=[SMEM, VMEM, VMEM],
        out_specs=[VMEM, VMEM],
        out_shape=[
            jax.ShapeDtypeStruct((12, 128, 256), BF16),
            jax.ShapeDtypeStruct((5, 128, 256), BF16),
        ],
        compiler_params=params(0),
        name="stack_weights",
    )(meta, inverse, panels)


def solve_leaves(spread, inverse):
    def kernel(b_hbm, d_hbm, x_ref, h_ref, b_ref, d_ref, sem):
        copies = []
        for g in range(4):
            part = pl.ds(8 * g, 8)
            copies.append(pltpu.make_async_copy(b_hbm.at[part], b_ref.at[part], sem.at[g]))
        for c in range(NC):
            copies.append(pltpu.make_async_copy(d_hbm.at[c], d_ref.at[c], sem.at[4 + c]))
        for g in range(4):
            for i in (g, *range(4 + 4 * g, 8 + 4 * g)):
                copies[i].start()
        for c in range(NC):
            if c % 4 == 0:
                copies[c // 4].wait()
            copies[4 + c].wait()
            for n in range(8):
                left = b_ref[2 * c : 2 * c + 2, n].reshape(32, 256)
                value = dot_t(left, d_ref[c, n])
                if c:
                    value = value + x_ref[n]
                x_ref[n] = value
        for n in range(8):
            half = x_ref[n].astype(BF16)
            for z in range(8):
                h_ref[z, n] = half

    return pl.pallas_call(
        kernel,
        in_specs=[HBM, HBM],
        out_specs=[VMEM, VMEM],
        out_shape=[
            jax.ShapeDtypeStruct((8, 32, 128), F32),
            jax.ShapeDtypeStruct((8, 8, 32, 128), BF16),
        ],
        scratch_shapes=[
            pltpu.VMEM((32, 8, 16, 256), BF16),
            pltpu.VMEM((NC, 8, 128, 256), BF16),
            pltpu.SemaphoreType.DMA((4 + NC,)),
        ],
        compiler_params=params(0, STREAM_LIMIT),
        name="solve_leaves",
    )(spread, inverse)


LEAF_PAIRS = [[0], [2], [4], [6], [0, 2], [4, 6], [0, 2, 4, 6]]


def select_leaves(meta, panels):
    def kernel(meta_ref, p_ref, o_ref):
        place = 0
        for t, firsts in enumerate(LEAF_PAIRS):
            for s in firsts:
                o_ref[place, :, :128] = selected(meta_ref, p_ref, s, 8 + t)
                o_ref[place, :, 128:] = selected(meta_ref, p_ref, s + 1, 8 + t)
                place += 1

    return pl.pallas_call(
        kernel,
        grid=(1,),
        in_specs=[SMEM, pl.BlockSpec((8, 3, 256, 128), lambda i: (0, 0, 0, 0))],
        out_specs=VMEM,
        out_shape=jax.ShapeDtypeStruct((12, 256, 256), BF16),
        compiler_params=params(),
        name="select_leaves",
    )(meta, panels)


def update_from_leaves(meta, solved, blocks, blocks_got, right, right_got):
    def kernel(meta_ref, x_ref, a_ref, b_hbm, r_ref, rg_ref, o_ref, b_ref, sem):
        core, row = meta_ref[1], meta_ref[2]
        copy = pltpu.make_async_copy(b_hbm, b_ref, sem.at[0])
        copy.start()
        joined = {}
        for s in range(0, 8, 2):
            joined[s] = jnp.concatenate(
                [x_ref[:, s].reshape(256, 128), x_ref[:, s + 1].reshape(256, 128)], axis=1
            )
        for column, block_ref in ((core, a_ref), (1 - core, b_ref)):
            if block_ref is b_ref:
                copy.wait()
            place = 0
            for t, firsts in enumerate(LEAF_PAIRS):
                acc = jnp.zeros((256, 256), F32)
                for s in firsts:
                    acc = acc + dot_t(joined[s], block_ref[place])
                    place += 1
                for half in range(2):
                    value = acc[:, 128 * half : 128 * half + 128].astype(BF16)
                    o_ref[:, pl.ds(column, 1), half, t] = value.reshape(8, 1, 32, 128)
        z = row // 4
        start = pl.multiple_of(16 * (row % 2), 16)

        @pl.when(core == (row // 2) % 2)
        def _():
            for t in range(7):
                for half in range(2):
                    columns = slice(128 * half, 128 * half + 128)
                    for column, held in (
                        (core, r_ref[8 + t, :, columns]),
                        (1 - core, rg_ref[t, :, columns]),
                    ):
                        part = o_ref[z, column, half, t, pl.ds(start, 16), :].astype(F32)
                        o_ref[z, column, half, t, pl.ds(start, 16), :] = (part - held).astype(
                            BF16
                        )

    return pl.pallas_call(
        kernel,
        in_specs=[SMEM, VMEM, VMEM, HBM, VMEM, VMEM],
        out_specs=VMEM,
        out_shape=jax.ShapeDtypeStruct((8, 2, 2, 7, 32, 128), BF16),
        scratch_shapes=[
            pltpu.VMEM((12, 256, 256), BF16),
            pltpu.SemaphoreType.DMA((1,)),
        ],
        compiler_params=params(0, STREAM_LIMIT),
        name="update_from_leaves",
    )(meta, solved, blocks, blocks_got, right, right_got)


def first_residual(parts):
    def kernel(p_ref, o_ref):
        o_ref[...] = (-jnp.sum(p_ref[...].astype(F32), axis=0)).astype(BF16)

    return pl.pallas_call(
        kernel,
        in_specs=[VMEM],
        out_specs=VMEM,
        out_shape=jax.ShapeDtypeStruct((7, 32, 128), BF16),
        compiler_params=params(0),
        name="first_residual",
    )(parts)


def solve_node(x_ref, d_ref, n, place):
    acc = jnp.zeros((32, 128), F32)
    for c in range(NC):
        left = jnp.concatenate([x_ref[2 * c, n], x_ref[2 * c + 1, n]], axis=1)
        acc = acc + dot_t(left, d_ref[c, place])
    return acc


def solve_pairs(x_ref, w_hbm, s_ref, w_ref, sem, nodes, first, last, groups, update):
    size = NC // groups
    parts = [pl.ds(g * size, size) for g in range(groups)]
    pieces = [(part, slice(0, nodes)) for part in parts]
    pieces += [(part, slice(first, last)) for part in parts]
    copies = [
        pltpu.make_async_copy(w_hbm.at[piece], w_ref.at[piece], sem.at[i])
        for i, piece in enumerate(pieces)
    ]
    for copy in copies:
        copy.start()
    for c in range(NC):
        if c % size == 0:
            copies[c // size].wait()
        for n in range(nodes):
            left = jnp.concatenate([x_ref[2 * c, n], x_ref[2 * c + 1, n]], axis=1)
            value = dot_t(left, w_ref[c, n])
            if c:
                value = value + s_ref[n]
            s_ref[n] = value
    joined = [
        jnp.concatenate([s_ref[n].astype(BF16), s_ref[n + 1].astype(BF16)], axis=1)
        for n in range(0, nodes, 2)
    ]
    for c in range(NC):
        if c % size == 0:
            copies[groups + c // size].wait()
        update(c, joined)


def solve_two(residual, weights):
    def kernel(x_ref, w_hbm, s_ref, o_ref, w_ref, sem):
        def update(c, joined):
            for half in range(2):
                r = 2 * c + half
                o_ref[r, 0] = dot_t(joined[0], w_ref[c, 4 + half]).astype(BF16)
                o_ref[r, 1] = dot_t(joined[1], w_ref[c, 6 + half]).astype(BF16)

        solve_pairs(x_ref, w_hbm, s_ref, w_ref, sem, 4, 4, 8, 4, update)

    return pl.pallas_call(
        kernel,
        in_specs=[VMEM, HBM],
        out_specs=[VMEM, VMEM],
        out_shape=[
            jax.ShapeDtypeStruct((4, 32, 128), F32),
            jax.ShapeDtypeStruct((NR, 2, 32, 128), BF16),
        ],
        scratch_shapes=[
            pltpu.VMEM((NC, 8, 128, 256), BF16),
            pltpu.SemaphoreType.DMA((8,)),
        ],
        compiler_params=params(0, STREAM_LIMIT),
        name="solve_two",
    )(residual, weights)


def root_parts(solved, weights):
    def kernel(s_ref, w_hbm, o_ref, w_ref, sem):
        copies = []
        for g in range(4):
            part = pl.ds(4 * g, 4)
            copies.append(
                pltpu.make_async_copy(w_hbm.at[part, slice(8, 12)], w_ref.at[part], sem.at[g])
            )
            copies[g].start()
        joined = [
            jnp.concatenate([s_ref[n].astype(BF16), s_ref[n + 1].astype(BF16)], axis=1)
            for n in (0, 2)
        ]
        for c in range(NC):
            if c % 4 == 0:
                copies[c // 4].wait()
            for half in range(2):
                o_ref[2 * c + half] = dot_t(joined[0], w_ref[c, half]) + dot_t(
                    joined[1], w_ref[c, 2 + half]
                )

    return pl.pallas_call(
        kernel,
        in_specs=[VMEM, HBM],
        out_specs=VMEM,
        out_shape=jax.ShapeDtypeStruct((NR, 32, 128), F32),
        scratch_shapes=[
            pltpu.VMEM((NC, 4, 128, 256), BF16),
            pltpu.SemaphoreType.DMA((4,)),
        ],
        compiler_params=params(0, STREAM_LIMIT),
        name="root_parts",
    )(solved, weights)


def solve_one(residual, weights, keep):
    def kernel(x_ref, w_hbm, keep_ref, s_ref, o_ref, w_ref, sem):
        def update(c, joined):
            for half in range(2):
                r = 2 * c + half
                part = keep_ref[r] + dot_t(joined[0], w_ref[c, 3 + half])
                o_ref[r, 0] = part.astype(BF16)

        solve_pairs(x_ref, w_hbm, s_ref, w_ref, sem, 2, 3, 5, 2, update)

    return pl.pallas_call(
        kernel,
        in_specs=[VMEM, HBM, VMEM],
        out_specs=[VMEM, VMEM],
        out_shape=[
            jax.ShapeDtypeStruct((2, 32, 128), F32),
            jax.ShapeDtypeStruct((NR, 1, 32, 128), BF16),
        ],
        scratch_shapes=[
            pltpu.VMEM(weights.shape, BF16),
            pltpu.SemaphoreType.DMA((4,)),
        ],
        compiler_params=params(0, STREAM_LIMIT),
        name="solve_one",
    )(residual, weights, keep)


def solve_root(residual, weights):
    def kernel(x_ref, d_ref, s_ref):
        s_ref[0] = solve_node(x_ref, d_ref, 0, 0)

    return pl.pallas_call(
        kernel,
        grid=(1,),
        in_specs=[VMEM, pl.BlockSpec((NC, 1, 128, 256), lambda i: (0, 2, 0, 0))],
        out_specs=VMEM,
        out_shape=jax.ShapeDtypeStruct((1, 32, 128), F32),
        compiler_params=params(1, STREAM_LIMIT),
        name="solve_root",
    )(residual, weights)


def next_residual(parts, rest):
    nodes = rest.shape[0]

    def kernel(p_ref, rest_ref, o_ref):
        residual = rest_ref[...].astype(F32) - jnp.sum(p_ref[...].astype(F32), axis=0)
        half = residual.astype(BF16)
        for r in range(NR):
            o_ref[r] = half

    return pl.pallas_call(
        kernel,
        in_specs=[VMEM, VMEM],
        out_specs=VMEM,
        out_shape=jax.ShapeDtypeStruct((NR, nodes, 32, 128), BF16),
        compiler_params=params(0),
        name="next_residual",
    )(parts, rest)


def exchange(values, axes):
    shape = values.shape
    flat = values.reshape(shape[0], -1, shape[-1])
    return lax.all_to_all(flat, axes, 0, 0, tiled=True).reshape(shape)


def spread_over(values, axes, size):
    return exchange(jnp.broadcast_to(values[None], (size,) + values.shape), axes)


def to_owner(values):
    pairs = [
        (r * NC + c, (2 * c + r % 2) * NC + r // 2) for r in range(NR) for c in range(NC)
    ]
    return lax.ppermute(values, ALL, pairs)


def to_solver(values):
    pairs = [
        (r * NC + c, (4 * (c // 2) + r % 4) * NC + 2 * (r // 4) + c % 2)
        for r in range(NR)
        for c in range(NC)
    ]
    return lax.ppermute(values, ALL, pairs)


def to_other_core(values):
    return lax.ppermute(values, "core", [(0, 1), (1, 0)])


def per_device(right_sides, diag_inverse, panels, block_map):
    row = lax.axis_index(ROW)
    col = lax.axis_index(COL)
    core = lax.axis_index("core")
    leaf_right, diag_inverse = lax.optimization_barrier(
        (right_sides[:8].astype(BF16), diag_inverse)
    )
    moved = to_owner(leaf_right)
    leaf_inverse = lax.all_gather(diag_inverse[:8], COL, axis=0)

    zero = jnp.zeros((), jnp.int32)
    meta = jnp.concatenate(
        [jnp.stack([col, core, row, zero]).astype(jnp.int32), block_map.reshape(-1)]
    )
    stack_two, stack_one = stack_weights(meta, diag_inverse, panels)
    spread = spread_over(moved, ROW, NR)
    blocks = select_leaves(meta, panels)
    blocks_got, right_got = to_other_core(blocks), to_other_core(right_sides[8:])
    spread, stack_two, stack_one, blocks, blocks_got, right_got = lax.optimization_barrier(
        (spread, stack_two, stack_one, blocks, blocks_got, right_got)
    )

    leaves, copies = solve_leaves(spread, leaf_inverse)
    own = exchange(copies, "z")
    stack_two, stack_one, own = lax.optimization_barrier((stack_two, stack_one, own))
    weights_two = lax.all_gather(stack_two, COL, axis=0)
    weights_one = lax.all_gather(stack_one, COL, axis=0)
    parts = update_from_leaves(meta, own, blocks, blocks_got, right_sides, right_got)
    parts = exchange(parts.reshape(NR, 7, 32, 128), ROW)
    residual = to_solver(first_residual(parts))

    spread = spread_over(residual[:4], ROW, NR)
    two, parts = solve_two(spread, weights_two)
    parts, keep = lax.optimization_barrier((exchange(parts, ROW), root_parts(two, weights_two)))
    spread = exchange(next_residual(parts, residual[4:6]), ROW)
    one, parts = solve_one(spread, weights_one, keep)
    spread = exchange(next_residual(exchange(parts, ROW), residual[6:]), ROW)
    root = solve_root(spread, weights_one)
    return jnp.concatenate([leaves, two, one, root], axis=0)


def solution(mesh):
    split = Mesh(mesh.devices.reshape(4, 8, 8, 2), ALL)
    return jax.shard_map(
        per_device,
        mesh=split,
        in_specs=(P(None, ROW, COL), P(None, ROW, COL), P(None, None, COL, ROW), P()),
        out_specs=P(None, COL, ROW),
        check_vma=False,
    )
```

```python
import jax
import jax.numpy as jnp
from jax import lax
from jax.experimental import pallas as pl
from jax.experimental.pallas import tpu as pltpu
from jax.sharding import Mesh
from jax.sharding import PartitionSpec as P

ROW = ("x", "y")
COL = ("z", "core")
ALL = ("x", "y", "z", "core")
NR = 32
NC = 16
VMEM_LIMIT = 24 * 1024 * 1024
STREAM_LIMIT = 56 * 1024 * 1024
F32 = jnp.float32
BF16 = jnp.bfloat16
VMEM = pl.BlockSpec(memory_space=pltpu.VMEM)
SMEM = pl.BlockSpec(memory_space=pltpu.SMEM)
HBM = pl.BlockSpec(memory_space=pltpu.HBM)


def params(n=1, limit=VMEM_LIMIT):
    return pltpu.CompilerParams(
        vmem_limit_bytes=limit, dimension_semantics=("arbitrary",) * n
    )


def dot_t(a, b):
    return lax.dot_general(a, b, (((1,), (1,)), ((), ())), preferred_element_type=F32)


def slot_of(meta, source, target):
    base = 4 + (source * NC + meta[0]) * 3
    second = jnp.where(meta[base + 1] == target, 1, 0)
    slot = jnp.where(meta[base + 2] == target, 2, second)
    return slot, meta[base + slot] == target


def selected(meta_ref, p_ref, source, target):
    slot, found = slot_of(meta_ref, source, target)
    block = p_ref[source, slot]
    return jnp.where(found, block, jnp.zeros_like(block))


def stack_weights(meta, inverse, panels):
    def kernel(meta_ref, d_ref, p_ref, two_ref, one_ref):
        def join(out_ref, place, source, target):
            for side in range(2):
                columns = slice(128 * side, 128 * side + 128)
                block = selected(meta_ref, p_ref, source + side, target)
                for half in range(2):
                    out_ref[place + half, :, columns] = block[128 * half : 128 * half + 128]

        two_ref[:4] = d_ref[8:12]
        one_ref[:3] = d_ref[12:]
        join(two_ref, 4, 8, 12)
        join(two_ref, 6, 10, 13)
        join(two_ref, 8, 8, 14)
        join(two_ref, 10, 10, 14)
        join(one_ref, 3, 12, 14)

    return pl.pallas_call(
        kernel,
        in_specs=[SMEM, VMEM, VMEM],
        out_specs=[VMEM, VMEM],
        out_shape=[
            jax.ShapeDtypeStruct((12, 128, 256), BF16),
            jax.ShapeDtypeStruct((5, 128, 256), BF16),
        ],
        compiler_params=params(0),
        name="stack_weights",
    )(meta, inverse, panels)


def solve_leaves(spread, inverse):
    def kernel(b_hbm, d_hbm, x_ref, h_ref, b_ref, d_ref, sem):
        copies = []
        for g in range(4):
            part = pl.ds(8 * g, 8)
            copies.append(pltpu.make_async_copy(b_hbm.at[part], b_ref.at[part], sem.at[g]))
        for c in range(NC):
            copies.append(pltpu.make_async_copy(d_hbm.at[c], d_ref.at[c], sem.at[4 + c]))
        for g in range(4):
            for i in (g, *range(4 + 4 * g, 8 + 4 * g)):
                copies[i].start()
        for c in range(NC):
            if c % 4 == 0:
                copies[c // 4].wait()
            copies[4 + c].wait()
            for n in range(8):
                left = b_ref[2 * c : 2 * c + 2, n].reshape(32, 256)
                value = dot_t(left, d_ref[c, n])
                if c:
                    value = value + x_ref[n]
                x_ref[n] = value
        for n in range(8):
            half = x_ref[n].astype(BF16)
            for z in range(8):
                h_ref[z, n] = half

    return pl.pallas_call(
        kernel,
        in_specs=[HBM, HBM],
        out_specs=[VMEM, VMEM],
        out_shape=[
            jax.ShapeDtypeStruct((8, 32, 128), F32),
            jax.ShapeDtypeStruct((8, 8, 32, 128), BF16),
        ],
        scratch_shapes=[
            pltpu.VMEM((32, 8, 16, 256), BF16),
            pltpu.VMEM((NC, 8, 128, 256), BF16),
            pltpu.SemaphoreType.DMA((4 + NC,)),
        ],
        compiler_params=params(0, STREAM_LIMIT),
        name="solve_leaves",
    )(spread, inverse)


LEAF_PAIRS = [[0], [2], [4], [6], [0, 2], [4, 6], [0, 2, 4, 6]]


def select_leaves(meta, panels):
    def kernel(meta_ref, p_ref, o_ref):
        place = 0
        for t, firsts in enumerate(LEAF_PAIRS):
            for s in firsts:
                o_ref[place, :, :128] = selected(meta_ref, p_ref, s, 8 + t)
                o_ref[place, :, 128:] = selected(meta_ref, p_ref, s + 1, 8 + t)
                place += 1

    return pl.pallas_call(
        kernel,
        grid=(1,),
        in_specs=[SMEM, pl.BlockSpec((8, 3, 256, 128), lambda i: (0, 0, 0, 0))],
        out_specs=VMEM,
        out_shape=jax.ShapeDtypeStruct((12, 256, 256), BF16),
        compiler_params=params(),
        name="select_leaves",
    )(meta, panels)


def update_from_leaves(meta, solved, blocks, blocks_got, right, right_got):
    def kernel(meta_ref, x_ref, a_ref, b_ref, r_ref, rg_ref, o_ref):
        core, row = meta_ref[1], meta_ref[2]
        joined = {}
        for s in range(0, 8, 2):
            joined[s] = jnp.concatenate(
                [x_ref[:, s].reshape(256, 128), x_ref[:, s + 1].reshape(256, 128)], axis=1
            )
        place = 0
        for t, firsts in enumerate(LEAF_PAIRS):
            for column, block_ref in ((core, a_ref), (1 - core, b_ref)):
                acc = jnp.zeros((256, 256), F32)
                for i, s in enumerate(firsts):
                    acc = acc + dot_t(joined[s], block_ref[place + i])
                for half in range(2):
                    value = acc[:, 128 * half : 128 * half + 128].astype(BF16)
                    o_ref[:, pl.ds(column, 1), half, t] = value.reshape(8, 1, 32, 128)
            place += len(firsts)
        z = row // 4
        start = pl.multiple_of(16 * (row % 2), 16)

        @pl.when(core == (row // 2) % 2)
        def _():
            for t in range(7):
                for half in range(2):
                    columns = slice(128 * half, 128 * half + 128)
                    for column, held in (
                        (core, r_ref[8 + t, :, columns]),
                        (1 - core, rg_ref[t, :, columns]),
                    ):
                        part = o_ref[z, column, half, t, pl.ds(start, 16), :].astype(F32)
                        o_ref[z, column, half, t, pl.ds(start, 16), :] = (part - held).astype(
                            BF16
                        )

    return pl.pallas_call(
        kernel,
        in_specs=[SMEM, VMEM, VMEM, VMEM, VMEM, VMEM],
        out_specs=VMEM,
        out_shape=jax.ShapeDtypeStruct((8, 2, 2, 7, 32, 128), BF16),
        compiler_params=params(0),
        name="update_from_leaves",
    )(meta, solved, blocks, blocks_got, right, right_got)


def first_residual(parts):
    def kernel(p_ref, o_ref):
        o_ref[...] = (-jnp.sum(p_ref[...].astype(F32), axis=0)).astype(BF16)

    return pl.pallas_call(
        kernel,
        in_specs=[VMEM],
        out_specs=VMEM,
        out_shape=jax.ShapeDtypeStruct((7, 32, 128), BF16),
        compiler_params=params(0),
        name="first_residual",
    )(parts)


def solve_node(x_ref, d_ref, n, place):
    acc = jnp.zeros((32, 128), F32)
    for c in range(NC):
        left = jnp.concatenate([x_ref[2 * c, n], x_ref[2 * c + 1, n]], axis=1)
        acc = acc + dot_t(left, d_ref[c, place])
    return acc


def solve_pairs(x_ref, w_hbm, s_ref, w_ref, sem, nodes, first, last, groups, update):
    size = NC // groups
    parts = [pl.ds(g * size, size) for g in range(groups)]
    pieces = [(part, slice(0, nodes)) for part in parts]
    pieces += [(part, slice(first, last)) for part in parts]
    copies = [
        pltpu.make_async_copy(w_hbm.at[piece], w_ref.at[piece], sem.at[i])
        for i, piece in enumerate(pieces)
    ]
    for copy in copies:
        copy.start()
    for c in range(NC):
        if c % size == 0:
            copies[c // size].wait()
        for n in range(nodes):
            left = jnp.concatenate([x_ref[2 * c, n], x_ref[2 * c + 1, n]], axis=1)
            value = dot_t(left, w_ref[c, n])
            if c:
                value = value + s_ref[n]
            s_ref[n] = value
    joined = [
        jnp.concatenate([s_ref[n].astype(BF16), s_ref[n + 1].astype(BF16)], axis=1)
        for n in range(0, nodes, 2)
    ]
    for c in range(NC):
        if c % size == 0:
            copies[groups + c // size].wait()
        update(c, joined)


def solve_two(residual, weights):
    def kernel(x_ref, w_hbm, s_ref, o_ref, w_ref, sem):
        def update(c, joined):
            for half in range(2):
                r = 2 * c + half
                o_ref[r, 0] = dot_t(joined[0], w_ref[c, 4 + half]).astype(BF16)
                o_ref[r, 1] = dot_t(joined[1], w_ref[c, 6 + half]).astype(BF16)

        solve_pairs(x_ref, w_hbm, s_ref, w_ref, sem, 4, 4, 8, 4, update)

    return pl.pallas_call(
        kernel,
        in_specs=[VMEM, HBM],
        out_specs=[VMEM, VMEM],
        out_shape=[
            jax.ShapeDtypeStruct((4, 32, 128), F32),
            jax.ShapeDtypeStruct((NR, 2, 32, 128), BF16),
        ],
        scratch_shapes=[
            pltpu.VMEM((NC, 8, 128, 256), BF16),
            pltpu.SemaphoreType.DMA((8,)),
        ],
        compiler_params=params(0, STREAM_LIMIT),
        name="solve_two",
    )(residual, weights)


def root_parts(solved, weights):
    def kernel(s_ref, w_hbm, o_ref, w_ref, sem):
        copies = []
        for g in range(4):
            part = pl.ds(4 * g, 4)
            copies.append(
                pltpu.make_async_copy(w_hbm.at[part, slice(8, 12)], w_ref.at[part], sem.at[g])
            )
            copies[g].start()
        joined = [
            jnp.concatenate([s_ref[n].astype(BF16), s_ref[n + 1].astype(BF16)], axis=1)
            for n in (0, 2)
        ]
        for c in range(NC):
            if c % 4 == 0:
                copies[c // 4].wait()
            for half in range(2):
                o_ref[2 * c + half] = dot_t(joined[0], w_ref[c, half]) + dot_t(
                    joined[1], w_ref[c, 2 + half]
                )

    return pl.pallas_call(
        kernel,
        in_specs=[VMEM, HBM],
        out_specs=VMEM,
        out_shape=jax.ShapeDtypeStruct((NR, 32, 128), F32),
        scratch_shapes=[
            pltpu.VMEM((NC, 4, 128, 256), BF16),
            pltpu.SemaphoreType.DMA((4,)),
        ],
        compiler_params=params(0, STREAM_LIMIT),
        name="root_parts",
    )(solved, weights)


def solve_one(residual, weights, keep):
    def kernel(x_ref, w_hbm, keep_ref, s_ref, o_ref, w_ref, sem):
        def update(c, joined):
            for half in range(2):
                r = 2 * c + half
                part = keep_ref[r] + dot_t(joined[0], w_ref[c, 3 + half])
                o_ref[r, 0] = part.astype(BF16)

        solve_pairs(x_ref, w_hbm, s_ref, w_ref, sem, 2, 3, 5, 2, update)

    return pl.pallas_call(
        kernel,
        in_specs=[VMEM, HBM, VMEM],
        out_specs=[VMEM, VMEM],
        out_shape=[
            jax.ShapeDtypeStruct((2, 32, 128), F32),
            jax.ShapeDtypeStruct((NR, 1, 32, 128), BF16),
        ],
        scratch_shapes=[
            pltpu.VMEM(weights.shape, BF16),
            pltpu.SemaphoreType.DMA((4,)),
        ],
        compiler_params=params(0, STREAM_LIMIT),
        name="solve_one",
    )(residual, weights, keep)


def solve_root(residual, weights):
    def kernel(x_ref, d_ref, s_ref):
        s_ref[0] = solve_node(x_ref, d_ref, 0, 0)

    return pl.pallas_call(
        kernel,
        grid=(1,),
        in_specs=[VMEM, pl.BlockSpec((NC, 1, 128, 256), lambda i: (0, 2, 0, 0))],
        out_specs=VMEM,
        out_shape=jax.ShapeDtypeStruct((1, 32, 128), F32),
        compiler_params=params(1, STREAM_LIMIT),
        name="solve_root",
    )(residual, weights)


def next_residual(parts, rest):
    nodes = rest.shape[0]

    def kernel(p_ref, rest_ref, o_ref):
        residual = rest_ref[...].astype(F32) - jnp.sum(p_ref[...].astype(F32), axis=0)
        half = residual.astype(BF16)
        for r in range(NR):
            o_ref[r] = half

    return pl.pallas_call(
        kernel,
        in_specs=[VMEM, VMEM],
        out_specs=VMEM,
        out_shape=jax.ShapeDtypeStruct((NR, nodes, 32, 128), BF16),
        compiler_params=params(0),
        name="next_residual",
    )(parts, rest)


def exchange(values, axes):
    shape = values.shape
    flat = values.reshape(shape[0], -1, shape[-1])
    return lax.all_to_all(flat, axes, 0, 0, tiled=True).reshape(shape)


def spread_over(values, axes, size):
    return exchange(jnp.broadcast_to(values[None], (size,) + values.shape), axes)


def to_owner(values):
    pairs = [
        (r * NC + c, (2 * c + r % 2) * NC + r // 2) for r in range(NR) for c in range(NC)
    ]
    return lax.ppermute(values, ALL, pairs)


def to_solver(values):
    pairs = [
        (r * NC + c, (4 * (c // 2) + r % 4) * NC + 2 * (r // 4) + c % 2)
        for r in range(NR)
        for c in range(NC)
    ]
    return lax.ppermute(values, ALL, pairs)


def to_other_core(values):
    return lax.ppermute(values, "core", [(0, 1), (1, 0)])


def per_device(right_sides, diag_inverse, panels, block_map):
    row = lax.axis_index(ROW)
    col = lax.axis_index(COL)
    core = lax.axis_index("core")
    leaf_right, diag_inverse = lax.optimization_barrier(
        (right_sides[:8].astype(BF16), diag_inverse)
    )
    moved = to_owner(leaf_right)
    leaf_inverse = lax.all_gather(diag_inverse[:8], COL, axis=0)

    zero = jnp.zeros((), jnp.int32)
    meta = jnp.concatenate(
        [jnp.stack([col, core, row, zero]).astype(jnp.int32), block_map.reshape(-1)]
    )
    stack_two, stack_one = stack_weights(meta, diag_inverse, panels)
    spread = spread_over(moved, ROW, NR)
    blocks = select_leaves(meta, panels)
    blocks_got, right_got = to_other_core(blocks), to_other_core(right_sides[8:])
    spread, stack_two, stack_one, blocks, blocks_got, right_got = lax.optimization_barrier(
        (spread, stack_two, stack_one, blocks, blocks_got, right_got)
    )

    leaves, copies = solve_leaves(spread, leaf_inverse)
    own = exchange(copies, "z")
    stack_two, stack_one, own = lax.optimization_barrier((stack_two, stack_one, own))
    weights_two = lax.all_gather(stack_two, COL, axis=0)
    weights_one = lax.all_gather(stack_one, COL, axis=0)
    parts = update_from_leaves(meta, own, blocks, blocks_got, right_sides, right_got)
    parts = exchange(parts.reshape(NR, 7, 32, 128), ROW)
    residual = to_solver(first_residual(parts))

    spread = spread_over(residual[:4], ROW, NR)
    two, parts = solve_two(spread, weights_two)
    parts, keep = lax.optimization_barrier((exchange(parts, ROW), root_parts(two, weights_two)))
    spread = exchange(next_residual(parts, residual[4:6]), ROW)
    one, parts = solve_one(spread, weights_one, keep)
    spread = exchange(next_residual(exchange(parts, ROW), residual[6:]), ROW)
    root = solve_root(spread, weights_one)
    return jnp.concatenate([leaves, two, one, root], axis=0)


def solution(mesh):
    split = Mesh(mesh.devices.reshape(4, 8, 8, 2), ALL)
    return jax.shard_map(
        per_device,
        mesh=split,
        in_specs=(P(None, ROW, COL), P(None, ROW, COL), P(None, None, COL, ROW), P()),
        out_specs=P(None, COL, ROW),
        check_vma=False,
    )
```

```python
import jax
import jax.numpy as jnp
from jax import lax
from jax.experimental import pallas as pl
from jax.experimental.pallas import tpu as pltpu
from jax.sharding import Mesh
from jax.sharding import PartitionSpec as P

ROW = ("x", "y")
COL = ("z", "core")
ALL = ("x", "y", "z", "core")
NR = 32
NC = 16
VMEM_LIMIT = 24 * 1024 * 1024
STREAM_LIMIT = 56 * 1024 * 1024
F32 = jnp.float32
BF16 = jnp.bfloat16
VMEM = pl.BlockSpec(memory_space=pltpu.VMEM)
SMEM = pl.BlockSpec(memory_space=pltpu.SMEM)
HBM = pl.BlockSpec(memory_space=pltpu.HBM)


def params(n=1, limit=VMEM_LIMIT):
    return pltpu.CompilerParams(
        vmem_limit_bytes=limit, dimension_semantics=("arbitrary",) * n
    )


def dot_t(a, b):
    return lax.dot_general(a, b, (((1,), (1,)), ((), ())), preferred_element_type=F32)


def slot_of(meta, source, target):
    base = 4 + (source * NC + meta[0]) * 3
    second = jnp.where(meta[base + 1] == target, 1, 0)
    slot = jnp.where(meta[base + 2] == target, 2, second)
    return slot, meta[base + slot] == target


def selected(meta_ref, p_ref, source, target):
    slot, found = slot_of(meta_ref, source, target)
    block = p_ref[source, slot]
    return jnp.where(found, block, jnp.zeros_like(block))


def stack_weights(meta, inverse, panels):
    def kernel(meta_ref, d_ref, p_ref, two_ref, one_ref):
        def join(out_ref, place, source, target):
            for side in range(2):
                columns = slice(128 * side, 128 * side + 128)
                block = selected(meta_ref, p_ref, source + side, target)
                for half in range(2):
                    out_ref[place + half, :, columns] = block[128 * half : 128 * half + 128]

        two_ref[:4] = d_ref[8:12]
        one_ref[:3] = d_ref[12:]
        join(two_ref, 4, 8, 12)
        join(two_ref, 6, 10, 13)
        join(two_ref, 8, 8, 14)
        join(two_ref, 10, 10, 14)
        join(one_ref, 3, 12, 14)

    return pl.pallas_call(
        kernel,
        in_specs=[SMEM, VMEM, VMEM],
        out_specs=[VMEM, VMEM],
        out_shape=[
            jax.ShapeDtypeStruct((12, 128, 256), BF16),
            jax.ShapeDtypeStruct((5, 128, 256), BF16),
        ],
        compiler_params=params(0),
        name="stack_weights",
    )(meta, inverse, panels)


def solve_leaves(spread, inverse):
    def kernel(b_hbm, d_hbm, x_ref, h_ref, b_ref, d_ref, sem):
        copies = []
        for g in range(4):
            part = pl.ds(8 * g, 8)
            copies.append(pltpu.make_async_copy(b_hbm.at[part], b_ref.at[part], sem.at[g]))
        for c in range(NC):
            copies.append(pltpu.make_async_copy(d_hbm.at[c], d_ref.at[c], sem.at[4 + c]))
        for g in range(4):
            for i in (g, *range(4 + 4 * g, 8 + 4 * g)):
                copies[i].start()
        for c in range(NC):
            if c % 4 == 0:
                copies[c // 4].wait()
            copies[4 + c].wait()
            for n in range(8):
                left = b_ref[2 * c : 2 * c + 2, n].reshape(32, 256)
                value = dot_t(left, d_ref[c, n])
                if c:
                    value = value + x_ref[n]
                x_ref[n] = value
        for n in range(8):
            half = x_ref[n].astype(BF16)
            for z in range(8):
                h_ref[z, n] = half

    return pl.pallas_call(
        kernel,
        in_specs=[HBM, HBM],
        out_specs=[VMEM, VMEM],
        out_shape=[
            jax.ShapeDtypeStruct((8, 32, 128), F32),
            jax.ShapeDtypeStruct((8, 8, 32, 128), BF16),
        ],
        scratch_shapes=[
            pltpu.VMEM((32, 8, 16, 256), BF16),
            pltpu.VMEM((NC, 8, 128, 256), BF16),
            pltpu.SemaphoreType.DMA((4 + NC,)),
        ],
        compiler_params=params(0, STREAM_LIMIT),
        name="solve_leaves",
    )(spread, inverse)


LEAF_PAIRS = [[0], [2], [4], [6], [0, 2], [4, 6], [0, 2, 4, 6]]


def select_leaves(meta, panels):
    def kernel(meta_ref, p_ref, o_ref):
        place = 0
        for t, firsts in enumerate(LEAF_PAIRS):
            for s in firsts:
                o_ref[place, :, :128] = selected(meta_ref, p_ref, s, 8 + t)
                o_ref[place, :, 128:] = selected(meta_ref, p_ref, s + 1, 8 + t)
                place += 1

    return pl.pallas_call(
        kernel,
        grid=(1,),
        in_specs=[SMEM, pl.BlockSpec((8, 3, 256, 128), lambda i: (0, 0, 0, 0))],
        out_specs=VMEM,
        out_shape=jax.ShapeDtypeStruct((12, 256, 256), BF16),
        compiler_params=params(),
        name="select_leaves",
    )(meta, panels)


def update_from_leaves(meta, solved, blocks, blocks_got, right, right_got):
    def kernel(meta_ref, x_ref, a_ref, b_ref, r_ref, rg_ref, o_ref):
        core, row = meta_ref[1], meta_ref[2]
        joined = {}
        for s in range(0, 8, 2):
            joined[s] = jnp.concatenate(
                [x_ref[:, s].reshape(256, 128), x_ref[:, s + 1].reshape(256, 128)], axis=1
            )
        place = 0
        for t, firsts in enumerate(LEAF_PAIRS):
            for column, block_ref in ((core, a_ref), (1 - core, b_ref)):
                acc = jnp.zeros((256, 256), F32)
                for i, s in enumerate(firsts):
                    acc = acc + dot_t(joined[s], block_ref[place + i])
                for half in range(2):
                    value = acc[:, 128 * half : 128 * half + 128].astype(BF16)
                    o_ref[:, pl.ds(column, 1), half, t] = value.reshape(8, 1, 32, 128)
            place += len(firsts)
        z = row // 4
        start = pl.multiple_of(16 * (row % 2), 16)

        @pl.when(core == (row // 2) % 2)
        def _():
            for t in range(7):
                for half in range(2):
                    columns = slice(128 * half, 128 * half + 128)
                    for column, held in (
                        (core, r_ref[8 + t, :, columns]),
                        (1 - core, rg_ref[t, :, columns]),
                    ):
                        part = o_ref[z, column, half, t, pl.ds(start, 16), :].astype(F32)
                        o_ref[z, column, half, t, pl.ds(start, 16), :] = (part - held).astype(
                            BF16
                        )

    return pl.pallas_call(
        kernel,
        in_specs=[SMEM, VMEM, VMEM, VMEM, VMEM, VMEM],
        out_specs=VMEM,
        out_shape=jax.ShapeDtypeStruct((8, 2, 2, 7, 32, 128), BF16),
        compiler_params=params(0),
        name="update_from_leaves",
    )(meta, solved, blocks, blocks_got, right, right_got)


def first_residual(parts):
    def kernel(p_ref, o_ref):
        o_ref[...] = (-jnp.sum(p_ref[...].astype(F32), axis=0)).astype(BF16)

    return pl.pallas_call(
        kernel,
        in_specs=[VMEM],
        out_specs=VMEM,
        out_shape=jax.ShapeDtypeStruct((7, 32, 128), BF16),
        compiler_params=params(0),
        name="first_residual",
    )(parts)


def solve_node(x_ref, d_ref, n, place):
    acc = jnp.zeros((32, 128), F32)
    for c in range(NC):
        left = jnp.concatenate([x_ref[2 * c, n], x_ref[2 * c + 1, n]], axis=1)
        acc = acc + dot_t(left, d_ref[c, place])
    return acc


def solve_pairs(x_ref, w_hbm, s_ref, w_ref, sem, nodes, first, last, groups, update):
    size = NC // groups
    parts = [pl.ds(g * size, size) for g in range(groups)]
    pieces = [(part, slice(0, nodes)) for part in parts]
    pieces += [(part, slice(first, last)) for part in parts]
    copies = [
        pltpu.make_async_copy(w_hbm.at[piece], w_ref.at[piece], sem.at[i])
        for i, piece in enumerate(pieces)
    ]
    for copy in copies:
        copy.start()
    for c in range(NC):
        if c % size == 0:
            copies[c // size].wait()
        for n in range(nodes):
            left = jnp.concatenate([x_ref[2 * c, n], x_ref[2 * c + 1, n]], axis=1)
            value = dot_t(left, w_ref[c, n])
            if c:
                value = value + s_ref[n]
            s_ref[n] = value
    joined = [
        jnp.concatenate([s_ref[n].astype(BF16), s_ref[n + 1].astype(BF16)], axis=1)
        for n in range(0, nodes, 2)
    ]
    for c in range(NC):
        if c % size == 0:
            copies[groups + c // size].wait()
        update(c, joined)


def solve_two(residual, weights):
    def kernel(x_ref, w_hbm, s_ref, o_ref, w_ref, sem):
        def update(c, joined):
            for half in range(2):
                r = 2 * c + half
                o_ref[r, 0] = dot_t(joined[0], w_ref[c, 4 + half]).astype(BF16)
                o_ref[r, 1] = dot_t(joined[1], w_ref[c, 6 + half]).astype(BF16)

        solve_pairs(x_ref, w_hbm, s_ref, w_ref, sem, 4, 4, 8, 4, update)

    return pl.pallas_call(
        kernel,
        in_specs=[VMEM, HBM],
        out_specs=[VMEM, VMEM],
        out_shape=[
            jax.ShapeDtypeStruct((4, 32, 128), F32),
            jax.ShapeDtypeStruct((NR, 2, 32, 128), BF16),
        ],
        scratch_shapes=[
            pltpu.VMEM((NC, 8, 128, 256), BF16),
            pltpu.SemaphoreType.DMA((8,)),
        ],
        compiler_params=params(0, STREAM_LIMIT),
        name="solve_two",
    )(residual, weights)


def root_parts(solved, weights):
    def kernel(s_ref, w_hbm, o_ref, w_ref, sem):
        copies = []
        for g in range(4):
            part = pl.ds(4 * g, 4)
            copies.append(
                pltpu.make_async_copy(w_hbm.at[part, slice(8, 12)], w_ref.at[part], sem.at[g])
            )
            copies[g].start()
        joined = [
            jnp.concatenate([s_ref[n].astype(BF16), s_ref[n + 1].astype(BF16)], axis=1)
            for n in (0, 2)
        ]
        for c in range(NC):
            if c % 4 == 0:
                copies[c // 4].wait()
            for half in range(2):
                o_ref[2 * c + half] = dot_t(joined[0], w_ref[c, half]) + dot_t(
                    joined[1], w_ref[c, 2 + half]
                )

    return pl.pallas_call(
        kernel,
        in_specs=[VMEM, HBM],
        out_specs=VMEM,
        out_shape=jax.ShapeDtypeStruct((NR, 32, 128), F32),
        scratch_shapes=[
            pltpu.VMEM((NC, 4, 128, 256), BF16),
            pltpu.SemaphoreType.DMA((4,)),
        ],
        compiler_params=params(0, STREAM_LIMIT),
        name="root_parts",
    )(solved, weights)


def solve_one(residual, weights, keep):
    def kernel(x_ref, w_hbm, keep_ref, s_ref, o_ref, w_ref, sem):
        def update(c, joined):
            for half in range(2):
                r = 2 * c + half
                part = keep_ref[r] + dot_t(joined[0], w_ref[c, 3 + half])
                o_ref[r, 0] = part.astype(BF16)

        solve_pairs(x_ref, w_hbm, s_ref, w_ref, sem, 2, 3, 5, 2, update)

    return pl.pallas_call(
        kernel,
        in_specs=[VMEM, HBM, VMEM],
        out_specs=[VMEM, VMEM],
        out_shape=[
            jax.ShapeDtypeStruct((2, 32, 128), F32),
            jax.ShapeDtypeStruct((NR, 1, 32, 128), BF16),
        ],
        scratch_shapes=[
            pltpu.VMEM(weights.shape, BF16),
            pltpu.SemaphoreType.DMA((4,)),
        ],
        compiler_params=params(0, STREAM_LIMIT),
        name="solve_one",
    )(residual, weights, keep)


def solve_root(residual, weights, leaves, two, one):
    def kernel(x_ref, d_ref, leaves_ref, two_ref, one_ref, s_ref):
        s_ref[:8] = leaves_ref[...]
        s_ref[8:12] = two_ref[...]
        s_ref[12:14] = one_ref[...]
        s_ref[14] = solve_node(x_ref, d_ref, 0, 0)

    return pl.pallas_call(
        kernel,
        grid=(1,),
        in_specs=[
            VMEM,
            pl.BlockSpec((NC, 1, 128, 256), lambda i: (0, 2, 0, 0)),
            VMEM,
            VMEM,
            VMEM,
        ],
        out_specs=VMEM,
        out_shape=jax.ShapeDtypeStruct((15, 32, 128), F32),
        compiler_params=params(1, STREAM_LIMIT),
        name="solve_root",
    )(residual, weights, leaves, two, one)


def next_residual(parts, rest):
    nodes = rest.shape[0]

    def kernel(p_ref, rest_ref, o_ref):
        residual = rest_ref[...].astype(F32) - jnp.sum(p_ref[...].astype(F32), axis=0)
        half = residual.astype(BF16)
        for r in range(NR):
            o_ref[r] = half

    return pl.pallas_call(
        kernel,
        in_specs=[VMEM, VMEM],
        out_specs=VMEM,
        out_shape=jax.ShapeDtypeStruct((NR, nodes, 32, 128), BF16),
        compiler_params=params(0),
        name="next_residual",
    )(parts, rest)


def exchange(values, axes):
    shape = values.shape
    flat = values.reshape(shape[0], -1, shape[-1])
    return lax.all_to_all(flat, axes, 0, 0, tiled=True).reshape(shape)


def spread_over(values, axes, size):
    return exchange(jnp.broadcast_to(values[None], (size,) + values.shape), axes)


def to_owner(values):
    pairs = [
        (r * NC + c, (2 * c + r % 2) * NC + r // 2) for r in range(NR) for c in range(NC)
    ]
    return lax.ppermute(values, ALL, pairs)


def to_solver(values):
    pairs = [
        (r * NC + c, (4 * (c // 2) + r % 4) * NC + 2 * (r // 4) + c % 2)
        for r in range(NR)
        for c in range(NC)
    ]
    return lax.ppermute(values, ALL, pairs)


def to_other_core(values):
    return lax.ppermute(values, "core", [(0, 1), (1, 0)])


def per_device(right_sides, diag_inverse, panels, block_map):
    row = lax.axis_index(ROW)
    col = lax.axis_index(COL)
    core = lax.axis_index("core")
    leaf_right, diag_inverse = lax.optimization_barrier(
        (right_sides[:8].astype(BF16), diag_inverse)
    )
    moved = to_owner(leaf_right)
    leaf_inverse = lax.all_gather(diag_inverse[:8], COL, axis=0)

    zero = jnp.zeros((), jnp.int32)
    meta = jnp.concatenate(
        [jnp.stack([col, core, row, zero]).astype(jnp.int32), block_map.reshape(-1)]
    )
    stack_two, stack_one = stack_weights(meta, diag_inverse, panels)
    spread = spread_over(moved, ROW, NR)
    blocks = select_leaves(meta, panels)
    blocks_got, right_got = to_other_core(blocks), to_other_core(right_sides[8:])
    spread, stack_two, stack_one, blocks, blocks_got, right_got = lax.optimization_barrier(
        (spread, stack_two, stack_one, blocks, blocks_got, right_got)
    )

    leaves, copies = solve_leaves(spread, leaf_inverse)
    own = exchange(copies, "z")
    stack_two, stack_one, own = lax.optimization_barrier((stack_two, stack_one, own))
    weights_two = lax.all_gather(stack_two, COL, axis=0)
    weights_one = lax.all_gather(stack_one, COL, axis=0)
    parts = update_from_leaves(meta, own, blocks, blocks_got, right_sides, right_got)
    parts = exchange(parts.reshape(NR, 7, 32, 128), ROW)
    residual = to_solver(first_residual(parts))

    spread = spread_over(residual[:4], ROW, NR)
    two, parts = solve_two(spread, weights_two)
    parts, keep = lax.optimization_barrier((exchange(parts, ROW), root_parts(two, weights_two)))
    spread = exchange(next_residual(parts, residual[4:6]), ROW)
    one, parts = solve_one(spread, weights_one, keep)
    spread = exchange(next_residual(exchange(parts, ROW), residual[6:]), ROW)
    return solve_root(spread, weights_one, leaves, two, one)


def solution(mesh):
    split = Mesh(mesh.devices.reshape(4, 8, 8, 2), ALL)
    return jax.shard_map(
        per_device,
        mesh=split,
        in_specs=(P(None, ROW, COL), P(None, ROW, COL), P(None, None, COL, ROW), P()),
        out_specs=P(None, COL, ROW),
        check_vma=False,
    )
```

```python
import jax
import jax.numpy as jnp
from jax import lax
from jax.experimental import pallas as pl
from jax.experimental.pallas import tpu as pltpu
from jax.sharding import Mesh
from jax.sharding import PartitionSpec as P

ROW = ("x", "y")
COL = ("z", "core")
ALL = ("x", "y", "z", "core")
NR = 32
NC = 16
VMEM_LIMIT = 24 * 1024 * 1024
STREAM_LIMIT = 56 * 1024 * 1024
F32 = jnp.float32
BF16 = jnp.bfloat16
VMEM = pl.BlockSpec(memory_space=pltpu.VMEM)
SMEM = pl.BlockSpec(memory_space=pltpu.SMEM)
HBM = pl.BlockSpec(memory_space=pltpu.HBM)


def params(n=1, limit=VMEM_LIMIT):
    return pltpu.CompilerParams(
        vmem_limit_bytes=limit, dimension_semantics=("arbitrary",) * n
    )


def dot_t(a, b):
    return lax.dot_general(a, b, (((1,), (1,)), ((), ())), preferred_element_type=F32)


def slot_of(meta, source, target):
    base = 4 + (source * NC + meta[0]) * 3
    second = jnp.where(meta[base + 1] == target, 1, 0)
    slot = jnp.where(meta[base + 2] == target, 2, second)
    return slot, meta[base + slot] == target


def selected(meta_ref, p_ref, source, target):
    slot, found = slot_of(meta_ref, source, target)
    block = p_ref[source, slot]
    return jnp.where(found, block, jnp.zeros_like(block))


def stack_weights(meta, inverse, panels):
    def kernel(meta_ref, d_ref, p_ref, two_ref, one_ref):
        def join(out_ref, place, source, target):
            for side in range(2):
                columns = slice(128 * side, 128 * side + 128)
                block = selected(meta_ref, p_ref, source + side, target)
                for half in range(2):
                    out_ref[place + half, :, columns] = block[128 * half : 128 * half + 128]

        two_ref[:4] = d_ref[8:12]
        one_ref[:3] = d_ref[12:]
        join(two_ref, 4, 8, 12)
        join(two_ref, 6, 10, 13)
        join(two_ref, 8, 8, 14)
        join(two_ref, 10, 10, 14)
        join(one_ref, 3, 12, 14)

    return pl.pallas_call(
        kernel,
        in_specs=[SMEM, VMEM, VMEM],
        out_specs=[VMEM, VMEM],
        out_shape=[
            jax.ShapeDtypeStruct((12, 128, 256), BF16),
            jax.ShapeDtypeStruct((5, 128, 256), BF16),
        ],
        compiler_params=params(0),
        name="stack_weights",
    )(meta, inverse, panels)


def solve_leaves(spread, inverse):
    def kernel(b_hbm, d_hbm, x_ref, h_ref, b_ref, d_ref, sem):
        copies = []
        for g in range(4):
            part = pl.ds(8 * g, 8)
            copies.append(pltpu.make_async_copy(b_hbm.at[part], b_ref.at[part], sem.at[g]))
        for c in range(NC):
            copies.append(pltpu.make_async_copy(d_hbm.at[c], d_ref.at[c], sem.at[4 + c]))
        for g in range(4):
            for i in (g, *range(4 + 4 * g, 8 + 4 * g)):
                copies[i].start()
        for c in range(NC):
            if c % 4 == 0:
                copies[c // 4].wait()
            copies[4 + c].wait()
            for n in range(8):
                left = b_ref[2 * c : 2 * c + 2, n].reshape(32, 256)
                value = dot_t(left, d_ref[c, n])
                if c:
                    value = value + x_ref[n]
                x_ref[n] = value
        for n in range(8):
            half = x_ref[n].astype(BF16)
            for z in range(8):
                h_ref[z, n] = half

    return pl.pallas_call(
        kernel,
        in_specs=[HBM, HBM],
        out_specs=[VMEM, VMEM],
        out_shape=[
            jax.ShapeDtypeStruct((8, 32, 128), F32),
            jax.ShapeDtypeStruct((8, 8, 32, 128), BF16),
        ],
        scratch_shapes=[
            pltpu.VMEM((32, 8, 16, 256), BF16),
            pltpu.VMEM((NC, 8, 128, 256), BF16),
            pltpu.SemaphoreType.DMA((4 + NC,)),
        ],
        compiler_params=params(0, STREAM_LIMIT),
        name="solve_leaves",
    )(spread, inverse)


LEAF_PAIRS = [[0], [2], [4], [6], [0, 2], [4, 6], [0, 2, 4, 6]]


def select_leaves(meta, panels):
    def kernel(meta_ref, p_ref, o_ref):
        place = 0
        for t, firsts in enumerate(LEAF_PAIRS):
            for s in firsts:
                o_ref[place, :, :128] = selected(meta_ref, p_ref, s, 8 + t)
                o_ref[place, :, 128:] = selected(meta_ref, p_ref, s + 1, 8 + t)
                place += 1

    return pl.pallas_call(
        kernel,
        grid=(1,),
        in_specs=[SMEM, pl.BlockSpec((8, 3, 256, 128), lambda i: (0, 0, 0, 0))],
        out_specs=VMEM,
        out_shape=jax.ShapeDtypeStruct((12, 256, 256), BF16),
        compiler_params=params(),
        name="select_leaves",
    )(meta, panels)


def update_from_leaves(meta, solved, blocks, blocks_got, right, right_got):
    def kernel(meta_ref, x_ref, a_ref, b_ref, r_ref, rg_ref, o_ref):
        core, row = meta_ref[1], meta_ref[2]
        joined = {}
        for s in range(0, 8, 2):
            joined[s] = jnp.concatenate(
                [x_ref[:, s].reshape(256, 128), x_ref[:, s + 1].reshape(256, 128)], axis=1
            )
        place = 0
        for t, firsts in enumerate(LEAF_PAIRS):
            for column, block_ref in ((core, a_ref), (1 - core, b_ref)):
                acc = jnp.zeros((256, 256), F32)
                for i, s in enumerate(firsts):
                    acc = acc + dot_t(joined[s], block_ref[place + i])
                for half in range(2):
                    value = acc[:, 128 * half : 128 * half + 128].astype(BF16)
                    o_ref[:, pl.ds(column, 1), half, t] = value.reshape(8, 1, 32, 128)
            place += len(firsts)
        z = row // 4
        start = pl.multiple_of(16 * (row % 2), 16)

        @pl.when(core == (row // 2) % 2)
        def _():
            for t in range(7):
                for half in range(2):
                    columns = slice(128 * half, 128 * half + 128)
                    for column, held in (
                        (core, r_ref[8 + t, :, columns]),
                        (1 - core, rg_ref[t, :, columns]),
                    ):
                        part = o_ref[z, column, half, t, pl.ds(start, 16), :].astype(F32)
                        o_ref[z, column, half, t, pl.ds(start, 16), :] = (part - held).astype(
                            BF16
                        )

    return pl.pallas_call(
        kernel,
        in_specs=[SMEM, VMEM, VMEM, VMEM, VMEM, VMEM],
        out_specs=VMEM,
        out_shape=jax.ShapeDtypeStruct((8, 2, 2, 7, 32, 128), BF16),
        compiler_params=params(0),
        name="update_from_leaves",
    )(meta, solved, blocks, blocks_got, right, right_got)


def first_residual(parts):
    def kernel(p_ref, o_ref):
        o_ref[...] = (-jnp.sum(p_ref[...].astype(F32), axis=0)).astype(BF16)

    return pl.pallas_call(
        kernel,
        in_specs=[VMEM],
        out_specs=VMEM,
        out_shape=jax.ShapeDtypeStruct((7, 32, 128), BF16),
        compiler_params=params(0),
        name="first_residual",
    )(parts)


def solve_node(x_ref, d_ref, n, place):
    acc = jnp.zeros((32, 128), F32)
    for c in range(NC):
        left = jnp.concatenate([x_ref[2 * c, n], x_ref[2 * c + 1, n]], axis=1)
        acc = acc + dot_t(left, d_ref[c, place])
    return acc


def solve_pairs(x_ref, w_hbm, s_ref, w_ref, sem, nodes, first, last, groups, update):
    size = NC // groups
    parts = [pl.ds(g * size, size) for g in range(groups)]
    pieces = [(part, slice(0, nodes)) for part in parts]
    pieces += [(part, slice(first, last)) for part in parts]
    copies = [
        pltpu.make_async_copy(w_hbm.at[piece], w_ref.at[piece], sem.at[i])
        for i, piece in enumerate(pieces)
    ]
    for copy in copies:
        copy.start()
    for c in range(NC):
        if c % size == 0:
            copies[c // size].wait()
        for n in range(nodes):
            left = jnp.concatenate([x_ref[2 * c, n], x_ref[2 * c + 1, n]], axis=1)
            value = dot_t(left, w_ref[c, n])
            if c:
                value = value + s_ref[n]
            s_ref[n] = value
    joined = [
        jnp.concatenate([s_ref[n].astype(BF16), s_ref[n + 1].astype(BF16)], axis=1)
        for n in range(0, nodes, 2)
    ]
    for c in range(NC):
        if c % size == 0:
            copies[groups + c // size].wait()
        update(c, joined)


def solve_two(residual, weights):
    def kernel(x_ref, w_hbm, s_ref, o_ref, w_ref, sem):
        def update(c, joined):
            for half in range(2):
                r = 2 * c + half
                o_ref[r, 0] = dot_t(joined[0], w_ref[c, 4 + half]).astype(BF16)
                o_ref[r, 1] = dot_t(joined[1], w_ref[c, 6 + half]).astype(BF16)

        solve_pairs(x_ref, w_hbm, s_ref, w_ref, sem, 4, 4, 8, 4, update)

    return pl.pallas_call(
        kernel,
        in_specs=[VMEM, HBM],
        out_specs=[VMEM, VMEM],
        out_shape=[
            jax.ShapeDtypeStruct((4, 32, 128), F32),
            jax.ShapeDtypeStruct((NR, 2, 32, 128), BF16),
        ],
        scratch_shapes=[
            pltpu.VMEM((NC, 8, 128, 256), BF16),
            pltpu.SemaphoreType.DMA((8,)),
        ],
        compiler_params=params(0, STREAM_LIMIT),
        name="solve_two",
    )(residual, weights)


def root_parts(solved, weights):
    def kernel(s_ref, w_hbm, o_ref, w_ref, sem):
        copies = []
        for g in range(4):
            part = pl.ds(4 * g, 4)
            copies.append(
                pltpu.make_async_copy(w_hbm.at[part, slice(8, 12)], w_ref.at[part], sem.at[g])
            )
            copies[g].start()
        joined = [
            jnp.concatenate([s_ref[n].astype(BF16), s_ref[n + 1].astype(BF16)], axis=1)
            for n in (0, 2)
        ]
        for c in range(NC):
            if c % 4 == 0:
                copies[c // 4].wait()
            for half in range(2):
                o_ref[2 * c + half] = dot_t(joined[0], w_ref[c, half]) + dot_t(
                    joined[1], w_ref[c, 2 + half]
                )

    return pl.pallas_call(
        kernel,
        in_specs=[VMEM, HBM],
        out_specs=VMEM,
        out_shape=jax.ShapeDtypeStruct((NR, 32, 128), F32),
        scratch_shapes=[
            pltpu.VMEM((NC, 4, 128, 256), BF16),
            pltpu.SemaphoreType.DMA((4,)),
        ],
        compiler_params=params(0, STREAM_LIMIT),
        name="root_parts",
    )(solved, weights)


def solve_one(residual, weights, keep):
    def kernel(x_ref, w_hbm, keep_ref, s_ref, o_ref, w_ref, sem):
        def update(c, joined):
            for half in range(2):
                r = 2 * c + half
                part = keep_ref[r] + dot_t(joined[0], w_ref[c, 3 + half])
                o_ref[r, 0] = part.astype(BF16)

        solve_pairs(x_ref, w_hbm, s_ref, w_ref, sem, 2, 3, 5, 2, update)

    return pl.pallas_call(
        kernel,
        in_specs=[VMEM, HBM, VMEM],
        out_specs=[VMEM, VMEM],
        out_shape=[
            jax.ShapeDtypeStruct((2, 32, 128), F32),
            jax.ShapeDtypeStruct((NR, 1, 32, 128), BF16),
        ],
        scratch_shapes=[
            pltpu.VMEM(weights.shape, BF16),
            pltpu.SemaphoreType.DMA((4,)),
        ],
        compiler_params=params(0, STREAM_LIMIT),
        name="solve_one",
    )(residual, weights, keep)


def solve_root(residual, weights, leaves, two, one):
    def kernel(x_ref, d_ref, leaves_ref, two_ref, one_ref, s_ref):
        s_ref[:8] = leaves_ref[...]
        s_ref[8:12] = two_ref[...]
        s_ref[12:14] = one_ref[...]
        s_ref[14] = solve_node(x_ref, d_ref, 0, 0)

    return pl.pallas_call(
        kernel,
        grid=(1,),
        in_specs=[
            VMEM,
            pl.BlockSpec((NC, 1, 128, 256), lambda i: (0, 2, 0, 0)),
            VMEM,
            VMEM,
            VMEM,
        ],
        out_specs=VMEM,
        out_shape=jax.ShapeDtypeStruct((15, 32, 128), F32),
        compiler_params=params(1, STREAM_LIMIT),
        name="solve_root",
    )(residual, weights, leaves, two, one)


def next_residual(parts, rest):
    nodes = rest.shape[0]

    def kernel(p_ref, rest_ref, o_ref):
        residual = rest_ref[...].astype(F32) - jnp.sum(p_ref[...].astype(F32), axis=0)
        half = residual.astype(BF16)
        for r in range(NR):
            o_ref[r] = half

    return pl.pallas_call(
        kernel,
        in_specs=[VMEM, VMEM],
        out_specs=VMEM,
        out_shape=jax.ShapeDtypeStruct((NR, nodes, 32, 128), BF16),
        compiler_params=params(0),
        name="next_residual",
    )(parts, rest)


def exchange(values, axes):
    shape = values.shape
    flat = values.reshape(shape[0], -1, shape[-1])
    return lax.all_to_all(flat, axes, 0, 0, tiled=True).reshape(shape)


def spread_over(values, axes, size):
    return exchange(jnp.broadcast_to(values[None], (size,) + values.shape), axes)


def to_owner(values):
    pairs = [
        (r * NC + c, (2 * c + r % 2) * NC + r // 2) for r in range(NR) for c in range(NC)
    ]
    return lax.ppermute(values, ALL, pairs)


def to_solver(values):
    pairs = [
        (r * NC + c, (4 * (c // 2) + r % 4) * NC + 2 * (r // 4) + c % 2)
        for r in range(NR)
        for c in range(NC)
    ]
    return lax.ppermute(values, ALL, pairs)


def to_other_core(values):
    return lax.ppermute(values, "core", [(0, 1), (1, 0)])


def per_device(right_sides, diag_inverse, panels, block_map):
    row = lax.axis_index(ROW)
    col = lax.axis_index(COL)
    core = lax.axis_index("core")
    leaf_right, diag_inverse = lax.optimization_barrier(
        (right_sides[:8].astype(BF16), diag_inverse)
    )
    moved = to_owner(leaf_right)
    moved, diag_inverse = lax.optimization_barrier((moved, diag_inverse))
    leaf_inverse = lax.all_gather(diag_inverse[:8], COL, axis=0)

    zero = jnp.zeros((), jnp.int32)
    meta = jnp.concatenate(
        [jnp.stack([col, core, row, zero]).astype(jnp.int32), block_map.reshape(-1)]
    )
    stack_two, stack_one = stack_weights(meta, diag_inverse, panels)
    spread = spread_over(moved, ROW, NR)
    blocks = select_leaves(meta, panels)
    blocks_got, right_got = to_other_core(blocks), to_other_core(right_sides[8:])
    spread, stack_two, stack_one, blocks, blocks_got, right_got = lax.optimization_barrier(
        (spread, stack_two, stack_one, blocks, blocks_got, right_got)
    )

    leaves, copies = solve_leaves(spread, leaf_inverse)
    own = exchange(copies, "z")
    stack_two, stack_one, own = lax.optimization_barrier((stack_two, stack_one, own))
    weights_two = lax.all_gather(stack_two, COL, axis=0)
    weights_one = lax.all_gather(stack_one, COL, axis=0)
    parts = update_from_leaves(meta, own, blocks, blocks_got, right_sides, right_got)
    parts = exchange(parts.reshape(NR, 7, 32, 128), ROW)
    residual = to_solver(first_residual(parts))

    spread = spread_over(residual[:4], ROW, NR)
    two, parts = solve_two(spread, weights_two)
    parts, keep = lax.optimization_barrier((exchange(parts, ROW), root_parts(two, weights_two)))
    spread = exchange(next_residual(parts, residual[4:6]), ROW)
    one, parts = solve_one(spread, weights_one, keep)
    spread = exchange(next_residual(exchange(parts, ROW), residual[6:]), ROW)
    return solve_root(spread, weights_one, leaves, two, one)


def solution(mesh):
    split = Mesh(mesh.devices.reshape(4, 8, 8, 2), ALL)
    return jax.shard_map(
        per_device,
        mesh=split,
        in_specs=(P(None, ROW, COL), P(None, ROW, COL), P(None, None, COL, ROW), P()),
        out_specs=P(None, COL, ROW),
        check_vma=False,
    )
```
